32 devices in a mesh: ctx: 16 (over z, x, core), fsdp: 2 (over y).
Axes of the slice: x: 2, y: 2, z: 4, core: 2. Of those that a mesh axis runs over, the one named last changes fastest.
Arguments:
- block_input: bfloat16 [2, 2048, 2048], P('fsdp', 'ctx'), may hold values from -36 to 36
- query_weight: bfloat16 [2048, 2048], P(('ctx', 'fsdp')), may hold values from -0.125 to 0.125
- key_weight: bfloat16 [2048, 1024], P(('ctx', 'fsdp')), may hold values from -0.125 to 0.125
- value_weight: bfloat16 [2048, 1024], P(('ctx', 'fsdp')), may hold values from -0.125 to 0.125
- output_weight: bfloat16 [2048, 2048], P(('ctx', 'fsdp')), may hold values from -0.375 to 0.375
- gate_weight: bfloat16 [2048, 6144], P(('ctx', 'fsdp')), may hold values from -0.125 to 0.125
- up_weight: bfloat16 [2048, 6144], P(('ctx', 'fsdp')), may hold values from -0.125 to 0.125
- down_weight: bfloat16 [2048, 6144], P(('ctx', 'fsdp')), may hold values from -0.078125 to 0.078125
- attn_gain: float32 [2048], replicated, may hold values from 0.5 to 1.5
- mlp_gain: float32 [2048], replicated, may hold values from 0.5 to 1.5
- query_gain: float32 [128], replicated, may hold values from 0.7 to 2.2
- key_gain: float32 [128], replicated, may hold values from 0.7 to 2.2
- block_order: int32 [32], replicated, may hold values from 0 to 31, each once
- cotangent: bfloat16 [2, 2048, 2048], P('fsdp', 'ctx'), may hold values from -18 to 18
Outputs:
- block_output: bfloat16 [2, 2048, 2048], P('fsdp', 'ctx')
- input_grad: float32 [2, 2048, 2048], P('fsdp', 'ctx')
- query_weight_grad: float32 [2048, 2048], P(('ctx', 'fsdp'))
- key_weight_grad: float32 [2048, 1024], P(('ctx', 'fsdp'))
- value_weight_grad: float32 [2048, 1024], P(('ctx', 'fsdp'))
- output_weight_grad: float32 [2048, 2048], P(('ctx', 'fsdp'))
- gate_weight_grad: float32 [2048, 6144], P(('ctx', 'fsdp'))
- up_weight_grad: float32 [2048, 6144], P(('ctx', 'fsdp'))
- down_weight_grad: float32 [2048, 6144], P(('ctx', 'fsdp'))
- attn_gain_grad: float32 [2048], replicated
- mlp_gain_grad: float32 [2048], replicated
- query_gain_grad: float32 [128], replicated
- key_gain_grad: float32 [128], replicated
The draws below stay inside these ranges and needn't reach their ends.
Inputs may be any that keep to these rules, and one draw needn't show every extreme that they name: `block_order`: each value appears exactly once.
All inputs are finite; a program needn't handle non-finite values.
Results may differ from the reference program's by a relative error of at most 0.025.
Values may be sent and summed in bfloat16 or wider, within the bound.
No kernel may reach another device: no remote copies, remote signals or barrier semaphores. Data moves between devices by JAX's collectives and lax.ppermute only.
A program may use at most 512 MiB of HBM per device.

```python
import math
import jax
import jax.numpy as jnp
from jax import lax

D = 2048
HEADS = 16
KV_HEADS = 8
HEAD = 128
FF = 6144
SEQS = 2
LEN = 2048
BLOCKS = 32


def draw_block_input(key, part):
    key = jax.random.fold_in(key, 11)
    key_base, key_rows, key_cols = jax.random.split(key, 3)
    base = jnp.clip(jax.random.normal(key_base, (SEQS, LEN, D), jnp.float32), -6.0, 6.0)
    row_scale = 0.3 * jnp.exp(jax.random.uniform(key_rows, (SEQS, LEN, 1), jnp.float32) * math.log(10.0))
    col_scale = 0.5 * jnp.exp(jax.random.uniform(key_cols, (1, 1, D), jnp.float32) * math.log(4.0))
    return (base * row_scale * col_scale).astype(jnp.bfloat16)


def draw_cotangent(key, part):
    key = jax.random.fold_in(key, 23)
    key_base = jax.random.fold_in(key, 0)
    ramp = 1.0 + 2.0 * jnp.arange(LEN, dtype=jnp.float32) / LEN
    base = jnp.clip(jax.random.normal(key_base, (SEQS, LEN, D), jnp.float32), -6.0, 6.0)
    return (base * ramp[None, :, None]).astype(jnp.bfloat16)


def block_scale(key, extent, pieces, least, top_value):
    factor_of = 1.0
    for position, parts in pieces:
        draws = jax.random.uniform(jax.random.fold_in(jax.random.fold_in(key, 6), position), (parts,), jnp.float32, least / len(pieces), top_value / len(pieces))
        factor_of = factor_of * jnp.repeat(jnp.exp(draws), extent[position] // parts).reshape((-1,) + (1,) * (len(extent) - 1 - position))
    return factor_of


def bell_draw(own_key, extent, width, bound, cuts=(), kind=jnp.bfloat16):
    entries = width * jax.random.normal(own_key, extent, jnp.float32)
    if cuts:
        entries = entries * block_scale(own_key, extent, cuts, -0.22, 0.18)
    return jnp.clip(entries, -bound, bound).astype(kind)


def setup_inputs(seed: int = 0) -> dict:
    key_of = jax.random.split(jax.random.key(seed), 15)
    block_input = draw_block_input(jax.random.fold_in(key_of[14], 71), 0)
    query_weight = bell_draw(key_of[1], (D, HEADS * HEAD), D ** -0.5, 0.125, ((0, 32),))
    key_weight = bell_draw(key_of[2], (D, KV_HEADS * HEAD), D ** -0.5, 0.125, ((0, 32),))
    value_weight = bell_draw(key_of[3], (D, KV_HEADS * HEAD), D ** -0.5, 0.125, ((0, 32),))
    output_weight = bell_draw(key_of[4], (D, HEADS * HEAD), (HEADS * HEAD // 8) ** -0.5, 0.375, ((0, 32),))
    gate_weight = bell_draw(key_of[5], (D, FF), D ** -0.5, 0.125, ((0, 32),))
    up_weight = bell_draw(key_of[6], (D, FF), D ** -0.5, 0.125, ((0, 32),))
    down_weight = bell_draw(key_of[7], (D, FF), FF ** -0.5, 0.078125, ((0, 32),))
    attn_gain = jnp.clip(1.0 + 0.1 * jax.random.normal(key_of[8], (D,), jnp.float32), 0.5, 1.5)
    mlp_gain = jnp.clip(1.0 + 0.1 * jax.random.normal(key_of[9], (D,), jnp.float32), 0.5, 1.5)
    query_gain = jnp.clip(jnp.exp(jax.random.uniform(key_of[10], (HEAD,), jnp.float32, math.log(0.7), math.log(2.2))), 0.7, 2.2)
    key_gain = jnp.clip(jnp.exp(jax.random.uniform(key_of[11], (HEAD,), jnp.float32, math.log(0.7), math.log(2.2))), 0.7, 2.2)
    block_order = jax.random.permutation(key_of[12], BLOCKS).astype(jnp.int32)
    cotangent = draw_cotangent(jax.random.fold_in(key_of[14], 71), 0)
    return {"block_input": block_input, "query_weight": query_weight, "key_weight": key_weight, "value_weight": value_weight, "output_weight": output_weight, "gate_weight": gate_weight, "up_weight": up_weight, "down_weight": down_weight, "attn_gain": attn_gain, "mlp_gain": mlp_gain, "query_gain": query_gain, "key_gain": key_gain, "block_order": block_order, "cotangent": cotangent}


eps_model = 1e-06
rope_base = 1000000.0

def inv_root(field):
    return lax.rsqrt(lax.optimization_barrier(jnp.mean(field * field, axis=-1, keepdims=True)) + eps_model)

def norm_back(field, factor, gain, grad_in):
    weighted = gain * grad_in
    inner_mean = lax.optimization_barrier(jnp.mean(weighted * field, axis=-1, keepdims=True))
    return factor * weighted - field * (factor * factor * factor) * inner_mean

def rope_tables(positions, head_size):
    half_size = head_size // 2
    exponent = jnp.arange(half_size, dtype=jnp.float32) * jnp.float32(2.0 / head_size)
    inverse = jnp.exp(-exponent * jnp.float32(math.log(rope_base)))
    angles = positions.astype(jnp.float32)[:, None] * inverse[None, :]
    return (jnp.cos(angles)[:, None, :], jnp.sin(angles)[:, None, :])

def rotate(field, cosine, sine):
    first_half, second_half = jnp.split(field, 2, axis=-1)
    return jnp.concatenate([first_half * cosine - second_half * sine, second_half * cosine + first_half * sine], axis=-1)

def rotate_back(grad_in, cosine, sine):
    first_half, second_half = jnp.split(grad_in, 2, axis=-1)
    return jnp.concatenate([first_half * cosine + second_half * sine, second_half * cosine - first_half * sine], axis=-1)

def round_trip(field):
    return lax.optimization_barrier(field.astype(jnp.bfloat16)).astype(jnp.float32)

def layout_positions(block_order, length):
    half_rows = length // block_order.shape[0]
    row_index = jnp.arange(length, dtype=jnp.int32)
    return block_order[row_index // half_rows] * half_rows + row_index % half_rows

def attend(query_rot, key_rot, value_heads, positions, score_scale):
    length = key_rot.shape[0]
    q_block = min(512, length)
    keys_f32 = key_rot.astype(jnp.float32)
    values_f32 = value_heads.astype(jnp.float32)

    def one_block(block_index):
        first_row = block_index * q_block
        queries = lax.dynamic_slice_in_dim(query_rot, first_row, q_block, 0).astype(jnp.float32)
        query_pos = lax.dynamic_slice_in_dim(positions, first_row, q_block, 0)
        scores = jnp.einsum('qgjd,kgd->gjqk', queries, keys_f32) * score_scale
        allowed = positions[None, :] <= query_pos[:, None]
        exp_total = lax.optimization_barrier(jnp.sum(jnp.where(allowed, jnp.exp(scores), 0.0), axis=-1))
        log_total = jnp.log(exp_total)
        probs = round_trip(jnp.where(allowed, jnp.exp(scores - log_total[..., None]), 0.0))
        results = jnp.einsum('gjqk,kgd->qgjd', probs, values_f32)
        return (results, log_total)
    results, log_totals = lax.map(one_block, jnp.arange(length // q_block, dtype=jnp.int32))
    results = results.reshape((length,) + results.shape[2:])
    log_totals = jnp.transpose(log_totals, (1, 2, 0, 3)).reshape(log_totals.shape[1], log_totals.shape[2], length)
    return (results, log_totals)

def attend_back(query_rot, key_rot, value_heads, positions, log_total, grad_heads, delta, score_scale):
    length = key_rot.shape[0]
    q_block = min(512, length)
    keys_f32 = key_rot.astype(jnp.float32)
    values_f32 = value_heads.astype(jnp.float32)

    def one_block(carry, block_index):
        key_grad, value_grad = carry
        first_row = block_index * q_block
        queries = lax.dynamic_slice_in_dim(query_rot, first_row, q_block, 0).astype(jnp.float32)
        grads_block = lax.dynamic_slice_in_dim(grad_heads, first_row, q_block, 0).astype(jnp.float32)
        query_pos = lax.dynamic_slice_in_dim(positions, first_row, q_block, 0)
        lse_block = lax.dynamic_slice_in_dim(log_total, first_row, q_block, 2)
        delta_block = lax.dynamic_slice_in_dim(delta, first_row, q_block, 2)
        scores = jnp.einsum('qgjd,kgd->gjqk', queries, keys_f32) * score_scale
        allowed = positions[None, :] <= query_pos[:, None]
        probs = jnp.where(allowed, jnp.exp(scores - lse_block[..., None]), 0.0)
        value_grad = value_grad + jnp.einsum('gjqk,qgjd->kgd', round_trip(probs), grads_block)
        d_probs = jnp.einsum('qgjd,kgd->gjqk', grads_block, values_f32)
        d_scores = round_trip(probs * (d_probs - delta_block[..., None]))
        query_grad = jnp.einsum('gjqk,kgd->qgjd', d_scores, keys_f32) * score_scale
        key_grad = key_grad + jnp.einsum('gjqk,qgjd->kgd', d_scores, queries) * score_scale
        return ((key_grad, value_grad), query_grad)
    zeros_kv = jnp.zeros(key_rot.shape, jnp.float32)
    (key_grad, value_grad), query_grad = lax.scan(one_block, (zeros_kv, zeros_kv), jnp.arange(length // q_block, dtype=jnp.int32))
    return (query_grad.reshape((length,) + query_grad.shape[2:]), key_grad, value_grad)

def layer_sequence(inputs, grad_out, weights, gains, positions):
    query_weight, key_weight, value_weight, output_weight, gate_weight, up_weight, down_weight = weights
    attn_gain, mlp_gain, query_gain, key_gain = gains
    length = inputs.shape[0]
    head_size = query_gain.shape[0]
    heads = query_weight.shape[1] // head_size
    kv_heads = key_weight.shape[1] // head_size
    group = heads // kv_heads
    score_scale = 1.0 / math.sqrt(head_size)
    f32 = jnp.float32
    bf16 = jnp.bfloat16
    inputs32 = inputs.astype(f32)
    scale_attn = inv_root(inputs32)
    normed_attn = (inputs32 * scale_attn * attn_gain).astype(bf16)
    query_raw = jnp.dot(normed_attn, query_weight, preferred_element_type=f32).reshape(length, heads, head_size)
    key_raw = jnp.dot(normed_attn, key_weight, preferred_element_type=f32).reshape(length, kv_heads, head_size)
    value_bf = jnp.dot(normed_attn, value_weight, preferred_element_type=f32).astype(bf16)
    scale_query = inv_root(query_raw)
    scale_key = inv_root(key_raw)
    cosine, sine = rope_tables(positions, head_size)
    query_rot = rotate(query_raw * scale_query * query_gain, cosine, sine).astype(bf16).reshape(length, kv_heads, group, head_size)
    key_rot = rotate(key_raw * scale_key * key_gain, cosine, sine).astype(bf16)
    value_heads = value_bf.reshape(length, kv_heads, head_size)
    attn_out, log_total = attend(query_rot, key_rot, value_heads, positions, score_scale)
    attn_bf = attn_out.reshape(length, heads * head_size).astype(bf16)
    hidden_one = inputs32 + jnp.dot(attn_bf, output_weight.T, preferred_element_type=f32)
    scale_mlp = inv_root(hidden_one)
    normed_mlp = (hidden_one * scale_mlp * mlp_gain).astype(bf16)
    gate_pre = jnp.dot(normed_mlp, gate_weight, preferred_element_type=f32)
    up_pre = jnp.dot(normed_mlp, up_weight, preferred_element_type=f32)
    activated = (jax.nn.silu(gate_pre) * up_pre).astype(bf16)
    outputs = (hidden_one + jnp.dot(activated, down_weight.T, preferred_element_type=f32)).astype(bf16)
    down_grad = jnp.dot(grad_out.T, activated, preferred_element_type=f32)
    act_grad = jnp.dot(grad_out, down_weight, preferred_element_type=f32)
    sigma = jax.nn.sigmoid(gate_pre)
    gate_grad_in = (act_grad * up_pre * sigma * (1.0 + gate_pre * (1.0 - sigma))).astype(bf16)
    up_grad_in = (act_grad * gate_pre * sigma).astype(bf16)
    gate_grad = jnp.dot(normed_mlp.T, gate_grad_in, preferred_element_type=f32)
    up_grad = jnp.dot(normed_mlp.T, up_grad_in, preferred_element_type=f32)
    normed_mlp_grad = jnp.dot(gate_grad_in, gate_weight.T, preferred_element_type=f32) + jnp.dot(up_grad_in, up_weight.T, preferred_element_type=f32)
    mlp_gain_grad = lax.optimization_barrier(jnp.sum(normed_mlp_grad * hidden_one * scale_mlp, axis=0))
    hidden_grad = grad_out.astype(f32) + norm_back(hidden_one, scale_mlp, mlp_gain, normed_mlp_grad)
    hidden_grad_bf = hidden_grad.astype(bf16)
    output_grad = jnp.dot(hidden_grad_bf.T, attn_bf, preferred_element_type=f32)
    attn_grad = jnp.dot(hidden_grad_bf, output_weight, preferred_element_type=f32).astype(bf16)
    attn_grad_heads = attn_grad.reshape(length, kv_heads, group, head_size)
    delta = lax.optimization_barrier(jnp.sum(attn_grad_heads.astype(f32) * attn_bf.reshape(length, kv_heads, group, head_size).astype(f32), axis=-1))
    delta = jnp.transpose(delta, (1, 2, 0))
    query_rot_grad, key_rot_grad, value_grad = attend_back(query_rot, key_rot, value_heads, positions, log_total, attn_grad_heads, delta, score_scale)
    query_normed_grad = rotate_back(query_rot_grad.reshape(length, heads, head_size), cosine, sine)
    key_normed_grad = rotate_back(key_rot_grad, cosine, sine)
    query_gain_grad = lax.optimization_barrier(jnp.sum(query_normed_grad * query_raw * scale_query, axis=(0, 1)))
    key_gain_grad = lax.optimization_barrier(jnp.sum(key_normed_grad * key_raw * scale_key, axis=(0, 1)))
    query_pre_grad = norm_back(query_raw, scale_query, query_gain, query_normed_grad).reshape(length, heads * head_size).astype(bf16)
    key_pre_grad = norm_back(key_raw, scale_key, key_gain, key_normed_grad).reshape(length, kv_heads * head_size).astype(bf16)
    value_pre_grad = value_grad.reshape(length, kv_heads * head_size).astype(bf16)
    query_w_grad = jnp.dot(normed_attn.T, query_pre_grad, preferred_element_type=f32)
    key_w_grad = jnp.dot(normed_attn.T, key_pre_grad, preferred_element_type=f32)
    value_w_grad = jnp.dot(normed_attn.T, value_pre_grad, preferred_element_type=f32)
    normed_attn_grad = jnp.dot(query_pre_grad, query_weight.T, preferred_element_type=f32) + jnp.dot(key_pre_grad, key_weight.T, preferred_element_type=f32) + jnp.dot(value_pre_grad, value_weight.T, preferred_element_type=f32)
    attn_gain_grad = lax.optimization_barrier(jnp.sum(normed_attn_grad * inputs32 * scale_attn, axis=0))
    input_grad = hidden_grad + norm_back(inputs32, scale_attn, attn_gain, normed_attn_grad)
    weight_grads = (query_w_grad, key_w_grad, value_w_grad, output_grad, gate_grad, up_grad, down_grad)
    gain_grads = (attn_gain_grad, mlp_gain_grad, query_gain_grad, key_gain_grad)
    return (outputs, input_grad, weight_grads, gain_grads)

def reference(block_input, query_weight, key_weight, value_weight, output_weight, gate_weight, up_weight, down_weight, attn_gain, mlp_gain, query_gain, key_gain, block_order, cotangent):
    weights = (query_weight, key_weight, value_weight, output_weight, gate_weight, up_weight, down_weight)
    gains = (attn_gain, mlp_gain, query_gain, key_gain)
    positions = layout_positions(block_order, block_input.shape[1])
    outputs_list = []
    input_list = []
    weight_sums = None
    gain_sums = None
    for sequence in range(block_input.shape[0]):
        outputs, input_grad, weight_grads, gain_grads = layer_sequence(block_input[sequence], cotangent[sequence], weights, gains, positions)
        outputs_list.append(outputs)
        input_list.append(input_grad)
        if weight_sums is None:
            weight_sums = weight_grads
            gain_sums = gain_grads
        else:
            weight_sums = jax.tree.map(lambda left, right: left + right, weight_sums, weight_grads)
            gain_sums = jax.tree.map(lambda left, right: left + right, gain_sums, gain_grads)
    return (jnp.stack(outputs_list), jnp.stack(input_list), weight_sums[0], weight_sums[1], weight_sums[2], weight_sums[3], weight_sums[4], weight_sums[5], weight_sums[6], gain_sums[0], gain_sums[1], gain_sums[2], gain_sums[3])
```

```python
import functools
import math

import jax
import jax.numpy as jnp
from jax import lax
from jax.experimental import pallas as pl
from jax.experimental.pallas import tpu as pltpu
from jax.sharding import PartitionSpec as P

eps_model = 1e-06
rope_base = 1000000.0
f32 = jnp.float32
bf16 = jnp.bfloat16


def inv_root(field):
    return lax.rsqrt(jnp.mean(field * field, axis=-1, keepdims=True) + eps_model)


def norm_back(field, factor, gain, grad_in):
    weighted = gain * grad_in
    inner_mean = jnp.mean(weighted * field, axis=-1, keepdims=True)
    return factor * weighted - field * (factor * factor * factor) * inner_mean


def rope_tables(positions, head_size):
    half_size = head_size // 2
    exponent = jnp.arange(half_size, dtype=f32) * f32(2.0 / head_size)
    inverse = jnp.exp(-exponent * f32(math.log(rope_base)))
    angles = positions.astype(f32)[:, None] * inverse[None, :]
    return jnp.cos(angles), jnp.sin(angles)


def rotate(field, cosine, sine):
    first_half, second_half = jnp.split(field, 2, axis=-1)
    return jnp.concatenate(
        [first_half * cosine - second_half * sine, second_half * cosine + first_half * sine],
        axis=-1,
    )


def rotate_back(grad_in, cosine, sine):
    first_half, second_half = jnp.split(grad_in, 2, axis=-1)
    return jnp.concatenate(
        [first_half * cosine + second_half * sine, second_half * cosine - first_half * sine],
        axis=-1,
    )


def dot_nn(left, right):
    return lax.dot_general(left, right, (((1,), (0,)), ((), ())), preferred_element_type=f32)


def dot_nt(left, right):
    return lax.dot_general(left, right, (((1,), (1,)), ((), ())), preferred_element_type=f32)


def dot_tn(left, right):
    return lax.dot_general(left, right, (((0,), (0,)), ((), ())), preferred_element_type=f32)


def sort_rows(source, target, table, blocks, rows):
    def move(index, carry):
        start = pl.multiple_of(table[index] * rows, rows)
        place = pl.multiple_of(index * rows, rows)
        target[pl.ds(place, rows), :] = source[pl.ds(start, rows), :]
        return carry

    lax.fori_loop(0, blocks, move, 0)


def unsort_rows(source, target, table, blocks, rows):
    def move(index, carry):
        start = pl.multiple_of(table[index] * rows, rows)
        place = pl.multiple_of(index * rows, rows)
        target[pl.ds(start, rows), :] = source[pl.ds(place, rows), :]
        return carry

    lax.fori_loop(0, blocks, move, 0)


def allowed_tile(key_first, query_tile, pos_table, tile_k, tile_q, rows, sorted_all):
    key_pos = key_first + lax.broadcasted_iota(jnp.int32, (tile_k, tile_q), 0)
    lane = lax.broadcasted_iota(jnp.int32, (1, tile_q), 1)
    if sorted_all:
        query_pos = query_tile * tile_q + lane
    else:
        per_tile = tile_q // rows
        query_pos = jnp.zeros((1, tile_q), jnp.int32)
        for piece in range(per_tile):
            first = pos_table[query_tile * per_tile + piece] * rows
            inside = (lane >= piece * rows) & (lane < (piece + 1) * rows)
            query_pos = jnp.where(inside, first + lane - piece * rows, query_pos)
    return key_pos <= query_pos


def tile_loop(query_tile, key_tiles, sorted_all, work):
    if sorted_all:
        for key_tile in range(query_tile):
            work(key_tile, False)
        work(query_tile, True)
    else:

        @pl.loop(0, key_tiles)
        def _(key_tile):
            work(key_tile, True)


def query_loop(query_tiles, sorted_all, work):
    if sorted_all:
        for query_tile in range(query_tiles):
            work(query_tile)
    else:

        @pl.loop(0, query_tiles)
        def _(query_tile):
            work(query_tile)


def attend_kernel(
    geometry, key_table, query_table, pos_table, q_ref, k_ref, v_ref, out_ref, lse_ref,
    q_sorted, k_sorted, v_sorted, v_turned, acc, total, out_sorted,
):
    rows, tile, sorted_all, scale = geometry
    keys, queries = k_ref.shape[0], q_ref.shape[0]
    key_tiles, query_tiles = keys // tile, queries // tile
    sort_rows(k_ref, k_sorted, key_table, keys // rows, rows)
    sort_rows(v_ref, v_sorted, key_table, keys // rows, rows)
    sort_rows(q_ref, q_sorted, query_table, queries // rows, rows)
    for key_tile in range(key_tiles):
        piece = v_sorted[key_tile * tile : (key_tile + 1) * tile, :]
        v_turned[:, key_tile * tile : (key_tile + 1) * tile] = piece.astype(f32).T.astype(bf16)

    def query_work(query_tile):
        q_start = pl.multiple_of(query_tile * tile, tile)
        q_tile = q_sorted[pl.ds(q_start, tile), :]
        acc[...] = jnp.zeros_like(acc)
        total[...] = jnp.zeros_like(total)

        def work(key_tile, masked):
            k_start = pl.multiple_of(key_tile * tile, tile)
            scores = dot_nt(k_sorted[pl.ds(k_start, tile), :], q_tile)
            probs = jnp.exp(scores * scale)
            if masked:
                keep = allowed_tile(k_start, query_tile, pos_table, tile, tile, rows, sorted_all)
                probs = jnp.where(keep, probs, 0.0)
            total[...] += jnp.sum(probs, axis=0, keepdims=True)
            acc[...] += dot_nn(v_turned[:, pl.ds(k_start, tile)], probs.astype(bf16))

        tile_loop(query_tile, key_tiles, sorted_all, work)
        lse_ref[:, pl.ds(q_start, tile)] = jnp.log(total[...])
        out_sorted[pl.ds(q_start, tile), :] = (acc[...] / total[...]).T.astype(bf16)

    query_loop(query_tiles, sorted_all, query_work)
    unsort_rows(out_sorted, out_ref, query_table, queries // rows, rows)


def attend(tables, query_rot, key_rot, value, rows, sorted_all, scale):
    queries, head = query_rot.shape
    keys = key_rot.shape[0]
    tile = math.gcd(math.gcd(queries, keys), 512)
    whole = lambda shape: pl.BlockSpec(shape, lambda i, *_: (0, 0))
    return pl.pallas_call(
        functools.partial(attend_kernel, (rows, tile, sorted_all, scale)),
        out_shape=(
            jax.ShapeDtypeStruct((queries, head), bf16),
            jax.ShapeDtypeStruct((1, queries), f32),
        ),
        grid_spec=pltpu.PrefetchScalarGridSpec(
            num_scalar_prefetch=3,
            grid=(1,),
            in_specs=[whole((queries, head)), whole((keys, head)), whole((keys, head))],
            out_specs=(whole((queries, head)), whole((1, queries))),
            scratch_shapes=[
                pltpu.VMEM((queries, head), bf16),
                pltpu.VMEM((keys, head), bf16),
                pltpu.VMEM((keys, head), bf16),
                pltpu.VMEM((head, keys), bf16),
                pltpu.VMEM((head, tile), f32),
                pltpu.VMEM((1, tile), f32),
                pltpu.VMEM((queries, head), bf16),
            ],
        ),
        compiler_params=pltpu.CompilerParams(vmem_limit_bytes=48 * 2**20),
        cost_estimate=pl.CostEstimate(
            flops=2 * queries * keys * head, bytes_accessed=8 * keys * head, transcendentals=queries * keys // 2
        ),
        name="attend",
    )(*tables, query_rot, key_rot, value)


def attend_back_kernel(
    geometry, key_table, query_table, pos_table, q_ref, k_ref, v_ref, o_ref, do_ref, lse_ref,
    dq_ref, dk_ref, dv_ref,
    q_sorted, k_sorted, v_sorted, do_sorted, o_sorted, k_turned, delta, dq_turned, dq_sorted, dk_sorted, dv_sorted,
):
    rows, tile, sorted_all, scale = geometry
    keys, queries = k_ref.shape[0], q_ref.shape[0]
    key_tiles, query_tiles = keys // tile, queries // tile
    sort_rows(k_ref, k_sorted, key_table, keys // rows, rows)
    sort_rows(v_ref, v_sorted, key_table, keys // rows, rows)
    sort_rows(q_ref, q_sorted, query_table, queries // rows, rows)
    sort_rows(do_ref, do_sorted, query_table, queries // rows, rows)
    sort_rows(o_ref, o_sorted, query_table, queries // rows, rows)
    for key_tile in range(key_tiles):
        piece = k_sorted[key_tile * tile : (key_tile + 1) * tile, :]
        k_turned[:, key_tile * tile : (key_tile + 1) * tile] = piece.astype(f32).T.astype(bf16)
    dk_sorted[...] = jnp.zeros_like(dk_sorted)
    dv_sorted[...] = jnp.zeros_like(dv_sorted)

    def query_work(query_tile):
        q_start = pl.multiple_of(query_tile * tile, tile)
        q_tile = q_sorted[pl.ds(q_start, tile), :]
        do_tile = do_sorted[pl.ds(q_start, tile), :]
        product = do_tile.astype(f32) * o_sorted[pl.ds(q_start, tile), :].astype(f32)
        delta[...] = jnp.sum(product.T, axis=0, keepdims=True)
        dq_turned[...] = jnp.zeros_like(dq_turned)

        def work(key_tile, masked):
            k_start = pl.multiple_of(key_tile * tile, tile)
            here = pl.ds(k_start, tile)
            scores = dot_nt(k_sorted[here, :], q_tile)
            probs = jnp.exp(scores * scale - lse_ref[:, pl.ds(q_start, tile)])
            if masked:
                keep = allowed_tile(k_start, query_tile, pos_table, tile, tile, rows, sorted_all)
                probs = jnp.where(keep, probs, 0.0)
            dv_sorted[here, :] += dot_nn(probs.astype(bf16), do_tile)
            d_probs = dot_nt(v_sorted[here, :], do_tile)
            d_scores = (probs * (d_probs - delta[...])).astype(bf16)
            dk_sorted[here, :] += dot_nn(d_scores, q_tile)
            dq_turned[...] += dot_nn(k_turned[:, here], d_scores)

        tile_loop(query_tile, key_tiles, sorted_all, work)
        dq_sorted[pl.ds(q_start, tile), :] = dq_turned[...].T * scale

    query_loop(query_tiles, sorted_all, query_work)
    dk_sorted[...] = dk_sorted[...] * scale
    unsort_rows(dq_sorted, dq_ref, query_table, queries // rows, rows)
    unsort_rows(dk_sorted, dk_ref, key_table, keys // rows, rows)
    unsort_rows(dv_sorted, dv_ref, key_table, keys // rows, rows)


def attend_back(tables, query_rot, key_rot, value, out, d_out, lse, rows, sorted_all, scale):
    queries, head = query_rot.shape
    keys = key_rot.shape[0]
    tile = math.gcd(math.gcd(queries, keys), 512)
    whole = lambda shape: pl.BlockSpec(shape, lambda i, *_: (0, 0))
    q_spec, k_spec = whole((queries, head)), whole((keys, head))
    return pl.pallas_call(
        functools.partial(attend_back_kernel, (rows, tile, sorted_all, scale)),
        out_shape=(
            jax.ShapeDtypeStruct((queries, head), f32),
            jax.ShapeDtypeStruct((keys, head), f32),
            jax.ShapeDtypeStruct((keys, head), f32),
        ),
        grid_spec=pltpu.PrefetchScalarGridSpec(
            num_scalar_prefetch=3,
            grid=(1,),
            in_specs=[q_spec, k_spec, k_spec, q_spec, q_spec, whole((1, queries))],
            out_specs=(q_spec, k_spec, k_spec),
            scratch_shapes=[
                pltpu.VMEM((queries, head), bf16),
                pltpu.VMEM((keys, head), bf16),
                pltpu.VMEM((keys, head), bf16),
                pltpu.VMEM((queries, head), bf16),
                pltpu.VMEM((queries, head), bf16),
                pltpu.VMEM((head, keys), bf16),
                pltpu.VMEM((1, tile), f32),
                pltpu.VMEM((head, tile), f32),
                pltpu.VMEM((queries, head), f32),
                pltpu.VMEM((keys, head), f32),
                pltpu.VMEM((keys, head), f32),
            ],
        ),
        compiler_params=pltpu.CompilerParams(vmem_limit_bytes=56 * 2**20),
        cost_estimate=pl.CostEstimate(
            flops=5 * queries * keys * head, bytes_accessed=20 * keys * head, transcendentals=queries * keys // 2
        ),
        name="attend_back",
    )(*tables, query_rot, key_rot, value, out, d_out, lse)


class Ring:
    def __init__(self, size):
        self.chips = size // 2
        self.reach = self.chips // 2
        order = list(range(0, self.chips, 2)) + list(range(self.chips - 1, 0, -2))
        self.order = order
        self.swap_pairs = [(i, i ^ 1) for i in range(size)]
        self.pass_pairs = []
        for place, chip in enumerate(order):
            after = order[(place + 1) % self.chips]
            self.pass_pairs.append((2 * chip, 2 * after))
            self.pass_pairs.append((2 * after + 1, 2 * chip + 1))

    def swap(self, field):
        return lax.ppermute(field, "ctx", self.swap_pairs)

    def hop(self, field):
        return lax.ppermute(field, "ctx", self.pass_pairs)

    def members(self, rank):
        chip, core = rank // 2, rank % 2
        order = jnp.array(self.order, jnp.int32)
        place = jnp.sum(jnp.where(order == chip, jnp.arange(self.chips, dtype=jnp.int32), 0))
        at = lambda shift: jnp.sum(
            jnp.where(
                jnp.arange(self.chips, dtype=jnp.int32) == (place + shift + self.chips) % self.chips,
                order,
                0,
            )
        )
        sign = 2 * core - 1
        chunks = [[rank, rank ^ 1]]
        for step in range(1, self.reach):
            near, far = at(sign * step), at(-sign * step)
            chunks.append([2 * near + core, 2 * near + 1 - core])
            chunks.append([2 * far + 1 - core, 2 * far + core])
        last = at(self.reach)
        chunks.append([2 * last + core])
        chunks.append([2 * last + 1 - core])
        return chunks

    def gather(self, block):
        rows = block.shape[0]
        held = jnp.concatenate([block, self.swap(block)], axis=0)
        chunks = [held]
        for step in range(1, self.reach + 1):
            if step == self.reach:
                held = held[:rows]
            held = self.hop(held)
            chunks += [held, self.swap(held)]
        return chunks

    def scatter_sum(self, term):
        held = None
        for step in range(self.reach, 0, -1):
            index = 2 * step - 1
            mine, other = term(index), term(index + 1)
            given = self.swap(mine)
            total = other.astype(f32) + given.astype(f32)
            if held is not None:
                rows = held.shape[0]
                if rows == total.shape[0]:
                    total = total + held.astype(f32)
                else:
                    total = jnp.concatenate([total[:rows] + held.astype(f32), total[rows:]], axis=0)
            held = self.hop(total.astype(bf16))
        own = term(0).astype(f32)
        rows = own.shape[0] // 2
        arrived = held.astype(f32)
        given = self.swap((arrived[:rows] + own[rows:]).astype(bf16))
        return arrived[rows:] + own[:rows] + given.astype(f32)


def to_columns(rows_block, fsdp_rank):
    received = lax.all_to_all(rows_block, "ctx", split_axis=0, concat_axis=0, tiled=False)
    partner = lax.ppermute(received, "fsdp", [(0, 1), (1, 0)])
    first = jnp.where(fsdp_rank == 0, received, partner)
    second = jnp.where(fsdp_rank == 0, partner, received)
    both = jnp.stack([first, second], axis=1)
    return both.reshape(-1, rows_block.shape[-1])


def to_rows(columns_grad, extra, fsdp_rank, ctx_size):
    width = columns_grad.shape[1]
    split = columns_grad.reshape(ctx_size, 2, -1, width)
    keep = lax.dynamic_index_in_dim(split, fsdp_rank, 1, keepdims=False)
    give = lax.dynamic_index_in_dim(split, 1 - fsdp_rank, 1, keepdims=False)
    rows = keep.shape[1]
    count = extra.shape[0]
    lines = -(-count // width)
    lines = -(-lines // 16) * 16
    extra_block = jnp.pad(extra, (0, lines * width - count)).reshape(lines, width)
    give_all = jnp.concatenate([give.reshape(-1, width).astype(bf16), extra_block.astype(bf16)], axis=0)
    given = lax.ppermute(give_all, "fsdp", [(0, 1), (1, 0)]).astype(f32)
    grads = keep + given[: ctx_size * rows].reshape(ctx_size, rows, width)
    extras = extra_block + given[ctx_size * rows :]
    sent = jnp.concatenate(
        [
            grads.astype(bf16),
            jnp.broadcast_to(extras.astype(bf16)[None], (ctx_size, lines, width)),
        ],
        axis=1,
    )
    received = lax.all_to_all(sent, "ctx", split_axis=0, concat_axis=0, tiled=False).astype(f32)
    extra_sum = jnp.sum(received[:, rows:], axis=0).reshape(-1)[:count]
    return received[:, :rows], extra_sum


def side_by_side(pieces):
    count, rows, width = pieces.shape
    return jnp.transpose(pieces, (1, 0, 2)).reshape(rows, count * width)


def shards(
    block_input,
    query_weight,
    key_weight,
    value_weight,
    output_weight,
    gate_weight,
    up_weight,
    down_weight,
    attn_gain,
    mlp_gain,
    query_gain,
    key_gain,
    block_order,
    cotangent,
):
    ctx_size = lax.axis_size("ctx")
    ctx_rank = lax.axis_index("ctx")
    fsdp_rank = lax.axis_index("fsdp")
    tokens = block_input.shape[1]
    model = block_input.shape[2]
    head_size = query_gain.shape[0]
    heads = query_weight.shape[1] // head_size
    kv_heads = key_weight.shape[1] // head_size
    slots = block_order.shape[0]
    length = tokens * ctx_size
    half_rows = length // slots
    per_block = tokens // half_rows
    weight_rows = query_weight.shape[0]
    hidden_slice = gate_weight.shape[1] // ctx_size
    splits = ctx_size // heads
    group = ctx_size // kv_heads
    split_rank = ctx_rank % splits
    sorted_all = splits == 1
    score_scale = 1.0 / math.sqrt(head_size)
    ring = Ring(ctx_size)
    head_groups = [[h * splits + s for h in range(heads)] for s in range(splits)]

    inputs_all = lax.all_gather(block_input[0], "ctx", axis=0, tiled=True)
    full_output = lax.all_gather(output_weight, ("ctx", "fsdp"), axis=0, tiled=True)
    cot_slots = lax.all_gather(cotangent[0], "ctx", axis=0, tiled=True)

    def by_head(weight, repeats):
        split = weight.reshape(weight_rows, -1, head_size)
        return jnp.repeat(jnp.transpose(split, (1, 0, 2)), repeats, axis=0)

    head_block = jnp.concatenate(
        [by_head(query_weight, splits), by_head(key_weight, group), by_head(value_weight, group)],
        axis=2,
    )
    head_weight = to_columns(head_block, fsdp_rank)

    def by_slice(weight):
        return jnp.transpose(weight.reshape(weight_rows, ctx_size, hidden_slice), (1, 0, 2))

    mlp_block = jnp.concatenate(
        [by_slice(gate_weight), by_slice(up_weight), by_slice(down_weight)], axis=2
    )
    mlp_weight = to_columns(mlp_block, fsdp_rank)
    gate_up = mlp_weight[:, : 2 * hidden_slice]
    down_part = mlp_weight[:, 2 * hidden_slice :]

    slot_index = jnp.arange(slots, dtype=jnp.int32)
    slot_of = jnp.sum(
        jnp.where(block_order[None, :] == slot_index[:, None], slot_index[None, :], 0), axis=1
    )
    positions = (
        block_order[:, None] * half_rows + jnp.arange(half_rows, dtype=jnp.int32)[None, :]
    ).reshape(-1)
    cosine, sine = rope_tables(positions, head_size)
    if sorted_all:
        tables = (slot_of, slot_of, slot_index)
    else:
        compact = jnp.arange(heads * per_block, dtype=jnp.int32)
        owner = (compact // per_block) * splits + split_rank
        own_pos = jnp.take(block_order, owner * per_block + compact % per_block)
        sequence = jnp.argsort(own_pos)
        tables = (slot_of, compact[sequence], own_pos[sequence])

    def own_queries(field):
        if splits == 1:
            return field
        parts = field.reshape((heads, splits, tokens) + field.shape[1:])
        picked = lax.dynamic_index_in_dim(parts, split_rank, 1, keepdims=False)
        return picked.reshape((heads * tokens,) + field.shape[1:])

    def all_queries(field):
        if splits == 1:
            return field
        parts = jnp.zeros((heads, splits, tokens) + field.shape[1:], field.dtype)
        value = field.reshape((heads, 1, tokens) + field.shape[1:])
        placed = lax.dynamic_update_slice_in_dim(parts, value, split_rank, 1)
        return placed.reshape((length,) + field.shape[1:])

    wide = inputs_all.astype(f32)
    normed_attn = (wide * inv_root(wide) * attn_gain).astype(bf16)
    projected = dot_nn(normed_attn, head_weight)
    query_raw = projected[:, :head_size]
    key_raw = projected[:, head_size : 2 * head_size]
    value_bf = projected[:, 2 * head_size :].astype(bf16)
    scale_query = inv_root(query_raw)
    scale_key = inv_root(key_raw)
    query_rot = rotate(query_raw * scale_query * query_gain, cosine, sine).astype(bf16)
    key_rot = rotate(key_raw * scale_key * key_gain, cosine, sine).astype(bf16)
    query_own = own_queries(query_rot)
    attn_own, lse = attend(tables, query_own, key_rot, value_bf, half_rows, sorted_all, score_scale)

    def exchange(pieces):
        return lax.all_to_all(
            pieces, "ctx", split_axis=0, concat_axis=0, axis_index_groups=head_groups, tiled=False
        )

    attn_bf = side_by_side(exchange(attn_own.reshape(heads, tokens, head_size)))
    inputs32 = block_input[0].astype(f32)
    scale_attn = inv_root(inputs32)
    hidden_one = inputs32 + dot_nt(attn_bf, full_output)
    scale_mlp = inv_root(hidden_one)
    normed_mlp = (hidden_one * scale_mlp * mlp_gain).astype(bf16)

    members = ring.members(ctx_rank)

    def pick(field, index):
        blocks = [
            lax.dynamic_slice_in_dim(field, member * tokens, tokens, 0) for member in members[index]
        ]
        return blocks[0] if len(blocks) == 1 else jnp.concatenate(blocks, axis=0)

    act_grad_slots = dot_nn(cot_slots, down_part)
    normed_chunks = ring.gather(normed_mlp)
    activated_chunks, back_chunks = [], []
    for index, chunk in enumerate(normed_chunks):
        pre = dot_nn(chunk, gate_up)
        gate_pre, up_pre = pre[:, :hidden_slice], pre[:, hidden_slice:]
        sigma = jax.nn.sigmoid(gate_pre)
        act_grad = pick(act_grad_slots, index)
        activated_chunks.append((gate_pre * sigma * up_pre).astype(bf16))
        back_chunks.append(
            jnp.concatenate(
                [
                    (act_grad * up_pre * sigma * (1.0 + gate_pre * (1.0 - sigma))).astype(bf16),
                    (act_grad * gate_pre * sigma).astype(bf16),
                ],
                axis=1,
            )
        )

    normed_mlp_grad = ring.scatter_sum(lambda i: dot_nt(back_chunks[i], gate_up).astype(bf16))
    mlp_out = ring.scatter_sum(lambda i: dot_nt(activated_chunks[i], down_part).astype(bf16))
    block_out = (hidden_one + mlp_out).astype(bf16)

    cot_ring = jnp.concatenate([pick(cot_slots, i) for i in range(len(members))], axis=0)
    gate_up_grad = dot_tn(
        jnp.concatenate(normed_chunks, axis=0), jnp.concatenate(back_chunks, axis=0)
    )
    down_grad = dot_tn(cot_ring, jnp.concatenate(activated_chunks, axis=0))
    mlp_gain_part = jnp.sum(gate_up_grad * gate_up.astype(f32), axis=1) / mlp_gain
    mlp_rows, mlp_gain_sum = to_rows(
        jnp.concatenate([gate_up_grad, down_grad], axis=1), mlp_gain_part, fsdp_rank, ctx_size
    )

    grad32 = cotangent[0].astype(f32)
    hidden_grad = grad32 + norm_back(hidden_one, scale_mlp, mlp_gain, normed_mlp_grad)
    hidden_grad_bf = hidden_grad.astype(bf16)
    hidden_grad_all = lax.all_gather(hidden_grad_bf, "ctx", axis=0, tiled=True)
    attn_grad = dot_nn(hidden_grad_bf, full_output).astype(bf16)
    attn_grad_own = exchange(
        jnp.transpose(attn_grad.reshape(tokens, heads, head_size), (1, 0, 2))
    ).reshape(-1, head_size)
    query_grad, key_grad, value_grad = attend_back(
        tables, query_own, key_rot, value_bf, attn_own, attn_grad_own, lse, half_rows, sorted_all, score_scale
    )
    query_normed_grad = rotate_back(all_queries(query_grad), cosine, sine)
    key_normed_grad = rotate_back(key_grad, cosine, sine)
    query_gain_part = jnp.sum(query_normed_grad * query_raw * scale_query, axis=0)
    key_gain_part = jnp.sum(key_normed_grad * key_raw * scale_key, axis=0)
    first_grads = jnp.concatenate(
        [
            norm_back(query_raw, scale_query, query_gain, query_normed_grad).astype(bf16),
            norm_back(key_raw, scale_key, key_gain, key_normed_grad).astype(bf16),
            value_grad.astype(bf16),
        ],
        axis=1,
    )
    normed_attn_grad = ring.scatter_sum(
        lambda i: dot_nt(pick(first_grads, i), head_weight).astype(bf16)
    )
    input_grad = hidden_grad + norm_back(inputs32, scale_attn, attn_gain, normed_attn_grad)
    head_grad = dot_tn(normed_attn, first_grads)
    output_grad = dot_tn(own_queries(hidden_grad_all), attn_own)
    attn_gain_part = jnp.sum(head_grad * head_weight.astype(f32), axis=1) / attn_gain
    attn_rows, attn_extra = to_rows(
        jnp.concatenate([head_grad, output_grad], axis=1),
        jnp.concatenate([attn_gain_part, query_gain_part, key_gain_part]),
        fsdp_rank,
        ctx_size,
    )

    def home(first, count):
        part = attn_rows[:, :, first * head_size : (first + 1) * head_size]
        if count != ctx_size:
            part = jnp.sum(part.reshape(count, ctx_size // count, weight_rows, head_size), axis=1)
        return side_by_side(part)

    def mlp_home(first):
        return side_by_side(mlp_rows[:, :, first * hidden_slice : (first + 1) * hidden_slice])

    return (
        block_out[None],
        input_grad[None],
        home(0, heads),
        home(1, kv_heads),
        home(2, kv_heads),
        home(3, heads),
        mlp_home(0),
        mlp_home(1),
        mlp_home(2),
        attn_extra[:model],
        mlp_gain_sum,
        attn_extra[model : model + head_size],
        attn_extra[model + head_size :],
    )


def solution(mesh):
    in_specs = (
        P("fsdp", "ctx", None),
        P(("ctx", "fsdp"), None),
        P(("ctx", "fsdp"), None),
        P(("ctx", "fsdp"), None),
        P(("ctx", "fsdp"), None),
        P(("ctx", "fsdp"), None),
        P(("ctx", "fsdp"), None),
        P(("ctx", "fsdp"), None),
        P(),
        P(),
        P(),
        P(),
        P(),
        P("fsdp", "ctx", None),
    )
    out_specs = (
        P("fsdp", "ctx", None),
        P("fsdp", "ctx", None),
        P(("ctx", "fsdp"), None),
        P(("ctx", "fsdp"), None),
        P(("ctx", "fsdp"), None),
        P(("ctx", "fsdp"), None),
        P(("ctx", "fsdp"), None),
        P(("ctx", "fsdp"), None),
        P(("ctx", "fsdp"), None),
        P(),
        P(),
        P(),
        P(),
    )
    return jax.shard_map(shards, mesh=mesh, in_specs=in_specs, out_specs=out_specs, check_vma=False)
```

```python
import functools
import math

import jax
import jax.numpy as jnp
import numpy as np
from jax import lax
from jax.experimental import pallas as pl
from jax.experimental.pallas import tpu as pltpu
from jax.sharding import PartitionSpec as P

eps_model = 1e-06
rope_base = 1000000.0
f32 = jnp.float32
bf16 = jnp.bfloat16


def inv_root(field):
    return lax.rsqrt(jnp.mean(field * field, axis=-1, keepdims=True) + eps_model)


def norm_back(field, factor, gain, grad_in):
    weighted = gain * grad_in
    inner_mean = jnp.mean(weighted * field, axis=-1, keepdims=True)
    return factor * weighted - field * (factor * factor * factor) * inner_mean


def rope_tables(positions, head_size):
    half_size = head_size // 2
    exponent = jnp.arange(half_size, dtype=f32) * f32(2.0 / head_size)
    inverse = jnp.exp(-exponent * f32(math.log(rope_base)))
    angles = positions.astype(f32)[:, None] * inverse[None, :]
    cosine, sine = jnp.cos(angles), jnp.sin(angles)
    return jnp.concatenate([cosine, cosine], axis=1), jnp.concatenate([-sine, sine], axis=1)


def dot_nn(left, right):
    return lax.dot_general(left, right, (((1,), (0,)), ((), ())), preferred_element_type=f32)


def dot_nt(left, right):
    return lax.dot_general(left, right, (((1,), (1,)), ((), ())), preferred_element_type=f32)


def dot_tn(left, right):
    return lax.dot_general(left, right, (((0,), (0,)), ((), ())), preferred_element_type=f32)


def allowed_tile(key_first, query_tile, pos_table, tile_k, tile_q, rows, sorted_all):
    key_pos = key_first + lax.broadcasted_iota(jnp.int32, (tile_k, tile_q), 0)
    lane = lax.broadcasted_iota(jnp.int32, (1, tile_q), 1)
    if sorted_all:
        query_pos = query_tile * tile_q + lane
    else:
        per_tile = tile_q // rows
        query_pos = jnp.zeros((1, tile_q), jnp.int32)
        for piece in range(per_tile):
            first = pos_table[query_tile * per_tile + piece] * rows
            inside = (lane >= piece * rows) & (lane < (piece + 1) * rows)
            query_pos = jnp.where(inside, first + lane - piece * rows, query_pos)
    return key_pos <= query_pos


def tile_loop(query_tile, key_tiles, sorted_all, work):
    if sorted_all:
        for key_tile in range(query_tile):
            work(key_tile, False)
        work(query_tile, True)
    else:

        @pl.loop(0, key_tiles)
        def _(key_tile):
            work(key_tile, True)


def query_loop(query_tiles, sorted_all, work):
    if sorted_all:
        for query_tile in range(query_tiles):
            work(query_tile)
    else:

        @pl.loop(0, query_tiles)
        def _(query_tile):
            work(query_tile)


def block_loop(blocks, work):
    def step(index, carry):
        work(index)
        return carry

    lax.fori_loop(0, blocks, step, 0, unroll=4)


def rows_at(index, rows):
    return pl.ds(pl.multiple_of(index * rows, rows), rows)


def each_key(key_pos, blocks, rows, work):
    for part in range(2):
        block_loop(
            blocks // 2,
            lambda index: work(
                part, rows_at(index, rows), rows_at(key_pos[part * (blocks // 2) + index], rows)
            ),
        )


def each_query(key_pos, query_table, pos_table, blocks, count, rows, sorted_all, work):
    if sorted_all:
        each_key(key_pos, blocks, rows, lambda part, here, place: work(part, here, place, place))
        return

    @pl.loop(0, count)
    def _(index):
        local = query_table[index]
        place, at_pos = rows_at(index, rows), rows_at(pos_table[index], rows)
        for part in range(2):
            inner = local - part * (blocks // 2)

            @pl.when((inner >= 0) & (inner < blocks // 2))
            def _():
                work(part, rows_at(inner, rows), place, at_pos)


def turn(field):
    return pltpu.roll(field, field.shape[-1] // 2, 1)


def attend_kernel(
    geometry, key_pos, query_table, pos_table, raw_a, raw_b, cos_ref, sin_ref, q_gain, k_gain,
    out_a, out_b, lse_ref, q_sorted, k_sorted, v_sorted, v_turned, acc, total, out_sorted,
):
    rows, tile, sorted_all, scale = geometry
    head = q_gain.shape[1]
    keys, queries = k_sorted.shape[0], q_sorted.shape[0]
    key_tiles, query_tiles = keys // tile, queries // tile
    raw, out = (raw_a, raw_b), (out_a, out_b)
    walk = (key_pos, query_table, pos_table, keys // rows, queries // rows, rows, sorted_all)

    def rope(field, gain, place):
        normed = field * inv_root(field) * gain[...]
        return (normed * cos_ref[place, :] + turn(normed) * sin_ref[place, :]).astype(bf16)

    def take_keys(part, here, place):
        k_sorted[place, :] = rope(raw[part][here, head : 2 * head], k_gain, place)
        v_sorted[place, :] = raw[part][here, 2 * head : 3 * head].astype(bf16)

    def take_queries(part, here, place, at_pos):
        q_sorted[place, :] = rope(raw[part][here, :head], q_gain, at_pos)

    each_key(key_pos, keys // rows, rows, take_keys)
    each_query(*walk, take_queries)
    for key_tile in range(key_tiles):
        piece = v_sorted[key_tile * tile : (key_tile + 1) * tile, :]
        v_turned[:, key_tile * tile : (key_tile + 1) * tile] = piece.astype(f32).T.astype(bf16)
    if not sorted_all:
        out_a[...] = jnp.zeros_like(out_a)
        out_b[...] = jnp.zeros_like(out_b)

    def query_work(query_tile):
        q_start = pl.multiple_of(query_tile * tile, tile)
        q_tile = q_sorted[pl.ds(q_start, tile), :]
        acc[...] = jnp.zeros_like(acc)
        total[...] = jnp.zeros_like(total)

        def work(key_tile, masked):
            k_start = pl.multiple_of(key_tile * tile, tile)
            scores = dot_nt(k_sorted[pl.ds(k_start, tile), :], q_tile)
            probs = jnp.exp(scores * scale)
            if masked:
                keep = allowed_tile(k_start, query_tile, pos_table, tile, tile, rows, sorted_all)
                probs = jnp.where(keep, probs, 0.0)
            total[...] += jnp.sum(probs, axis=0, keepdims=True)
            acc[...] += dot_nn(v_turned[:, pl.ds(k_start, tile)], probs.astype(bf16))

        tile_loop(query_tile, key_tiles, sorted_all, work)
        lse_ref[:, pl.ds(q_start, tile)] = jnp.log(total[...])
        out_sorted[pl.ds(q_start, tile), :] = (acc[...] / total[...]).T.astype(bf16)

    query_loop(query_tiles, sorted_all, query_work)

    def put(part, here, place, at_pos):
        out[part][here, :] = out_sorted[place, :]

    each_query(*walk, put)


def whole_spec(shape):
    return pl.BlockSpec(shape, lambda i, *_: (0, 0), pipeline_mode=pl.Buffered(1))


def attend(tables, raw, cosine, sine, query_gain, key_gain, rows, sorted_all, scale):
    head = query_gain.shape[1]
    keys = cosine.shape[0]
    queries = tables[1].shape[0] * rows
    tile = math.gcd(math.gcd(queries, keys), 512)
    narrow, row, part = whole_spec((keys, head)), whole_spec((1, head)), whole_spec((keys // 2, head))
    return pl.pallas_call(
        functools.partial(attend_kernel, (rows, tile, sorted_all, scale)),
        out_shape=(
            jax.ShapeDtypeStruct((keys // 2, head), bf16),
            jax.ShapeDtypeStruct((keys // 2, head), bf16),
            jax.ShapeDtypeStruct((1, queries), f32),
            jax.ShapeDtypeStruct((queries, head), bf16),
            jax.ShapeDtypeStruct((keys, head), bf16),
            jax.ShapeDtypeStruct((keys, head), bf16),
        ),
        grid_spec=pltpu.PrefetchScalarGridSpec(
            num_scalar_prefetch=3,
            grid=(1,),
            in_specs=[whole_spec(raw[0].shape), whole_spec(raw[1].shape), narrow, narrow, row, row],
            out_specs=(part, part, whole_spec((1, queries)), whole_spec((queries, head)), narrow, narrow),
            scratch_shapes=[
                pltpu.VMEM((head, keys), bf16),
                pltpu.VMEM((head, tile), f32),
                pltpu.VMEM((1, tile), f32),
                pltpu.VMEM((queries, head), bf16),
            ],
        ),
        compiler_params=pltpu.CompilerParams(vmem_limit_bytes=48 * 2**20),
        cost_estimate=pl.CostEstimate(
            flops=4 * queries * keys * head, bytes_accessed=28 * keys * head, transcendentals=queries * keys
        ),
        name="attend",
    )(*tables, *raw, cosine, sine, query_gain, key_gain)


def attend_back_kernel(
    geometry, key_pos, query_table, pos_table, raw_a, raw_b, cos_ref, sin_ref, q_gain, k_gain,
    q_sorted, k_sorted, v_sorted, o_a, o_b, do_a, do_b, lse_ref,
    grads_a, grads_b, q_part, k_part,
    do_sorted, o_sorted, k_turned, delta, dq_turned, dq_sorted, dk_sorted, dv_sorted,
):
    rows, tile, sorted_all, scale = geometry
    head = q_gain.shape[1]
    keys, queries = k_sorted.shape[0], q_sorted.shape[0]
    key_tiles, query_tiles = keys // tile, queries // tile
    raw, o_ref, do_ref, grads = (raw_a, raw_b), (o_a, o_b), (do_a, do_b), (grads_a, grads_b)
    walk = (key_pos, query_table, pos_table, keys // rows, queries // rows, rows, sorted_all)

    def take(part, here, place, at_pos):
        do_sorted[place, :] = do_ref[part][here, :]
        o_sorted[place, :] = o_ref[part][here, :]

    each_query(*walk, take)
    for key_tile in range(key_tiles):
        piece = k_sorted[key_tile * tile : (key_tile + 1) * tile, :]
        k_turned[:, key_tile * tile : (key_tile + 1) * tile] = piece.astype(f32).T.astype(bf16)
    dk_sorted[...] = jnp.zeros_like(dk_sorted)
    dv_sorted[...] = jnp.zeros_like(dv_sorted)
    if not sorted_all:
        for part in range(2):
            grads[part][:, :head] = jnp.zeros((keys // 2, head), bf16)

    def query_work(query_tile):
        q_start = pl.multiple_of(query_tile * tile, tile)
        q_tile = q_sorted[pl.ds(q_start, tile), :]
        do_tile = do_sorted[pl.ds(q_start, tile), :]
        product = do_tile.astype(f32) * o_sorted[pl.ds(q_start, tile), :].astype(f32)
        delta[...] = jnp.sum(product.T, axis=0, keepdims=True)
        dq_turned[...] = jnp.zeros_like(dq_turned)

        def work(key_tile, masked):
            k_start = pl.multiple_of(key_tile * tile, tile)
            here = pl.ds(k_start, tile)
            scores = dot_nt(k_sorted[here, :], q_tile)
            probs = jnp.exp(scores * scale - lse_ref[:, pl.ds(q_start, tile)])
            if masked:
                keep = allowed_tile(k_start, query_tile, pos_table, tile, tile, rows, sorted_all)
                probs = jnp.where(keep, probs, 0.0)
            dv_sorted[here, :] += dot_nn(probs.astype(bf16), do_tile)
            d_probs = dot_nt(v_sorted[here, :], do_tile)
            d_scores = (probs * (d_probs - delta[...])).astype(bf16)
            dk_sorted[here, :] += dot_nn(d_scores, q_tile)
            dq_turned[...] += dot_nn(k_turned[:, here], d_scores)

        tile_loop(query_tile, key_tiles, sorted_all, work)
        dq_sorted[pl.ds(q_start, tile), :] = dq_turned[...].T

    query_loop(query_tiles, sorted_all, query_work)
    q_part[...] = jnp.zeros_like(q_part)
    k_part[...] = jnp.zeros_like(k_part)

    def through_norm(field, grad, gain, at_pos, gain_part):
        scaled = grad * scale
        normed_grad = scaled * cos_ref[at_pos, :] - turn(scaled) * sin_ref[at_pos, :]
        factor = inv_root(field)
        gain_part[...] += jnp.sum(normed_grad * field * factor, axis=0, keepdims=True)
        return norm_back(field, factor, gain[...], normed_grad).astype(bf16)

    def put_queries(part, here, place, at_pos):
        grads[part][here, :head] = through_norm(
            raw[part][here, :head], dq_sorted[place, :], q_gain, at_pos, q_part
        )

    def put_keys(part, here, place):
        grads[part][here, head : 2 * head] = through_norm(
            raw[part][here, head : 2 * head], dk_sorted[place, :], k_gain, place, k_part
        )
        grads[part][here, 2 * head :] = dv_sorted[place, :].astype(bf16)

    each_query(*walk, put_queries)
    each_key(key_pos, keys // rows, rows, put_keys)


def attend_back(tables, raw, cosine, sine, query_gain, key_gain, saved, out, d_out, lse, rows, sorted_all, scale):
    head = query_gain.shape[1]
    keys = cosine.shape[0]
    queries = tables[1].shape[0] * rows
    tile = math.gcd(math.gcd(queries, keys), 512)
    narrow, row, part = whole_spec((keys, head)), whole_spec((1, head)), whole_spec((keys // 2, head))
    q_spec, wide = whole_spec((queries, head)), whole_spec((keys // 2, 3 * head))
    return pl.pallas_call(
        functools.partial(attend_back_kernel, (rows, tile, sorted_all, scale)),
        out_shape=(
            jax.ShapeDtypeStruct((keys // 2, 3 * head), bf16),
            jax.ShapeDtypeStruct((keys // 2, 3 * head), bf16),
            jax.ShapeDtypeStruct((1, head), f32),
            jax.ShapeDtypeStruct((1, head), f32),
        ),
        grid_spec=pltpu.PrefetchScalarGridSpec(
            num_scalar_prefetch=3,
            grid=(1,),
            in_specs=[
                whole_spec(raw[0].shape), whole_spec(raw[1].shape), narrow, narrow, row, row,
                q_spec, narrow, narrow, part, part, part, part, whole_spec((1, queries)),
            ],
            out_specs=(wide, wide, row, row),
            scratch_shapes=[
                pltpu.VMEM((queries, head), bf16),
                pltpu.VMEM((queries, head), bf16),
                pltpu.VMEM((head, keys), bf16),
                pltpu.VMEM((1, tile), f32),
                pltpu.VMEM((head, tile), f32),
                pltpu.VMEM((queries, head), f32),
                pltpu.VMEM((keys, head), f32),
                pltpu.VMEM((keys, head), f32),
            ],
        ),
        compiler_params=pltpu.CompilerParams(vmem_limit_bytes=60 * 2**20),
        cost_estimate=pl.CostEstimate(
            flops=10 * queries * keys * head, bytes_accessed=40 * keys * head, transcendentals=queries * keys
        ),
        name="attend_back",
    )(*tables, *raw, cosine, sine, query_gain, key_gain, *saved, *out, *d_out, lse)


class Ring:
    def __init__(self, size):
        self.chips = size // 2
        self.reach = self.chips // 2
        self.order = list(range(0, self.chips, 2)) + list(range(self.chips - 1, 0, -2))
        self.swap_pairs = [(i, i ^ 1) for i in range(size)]
        self.out_pairs = []
        for place, chip in enumerate(self.order):
            after_it = self.order[(place + 1) % self.chips]
            self.out_pairs.append((2 * chip, 2 * after_it))
            self.out_pairs.append((2 * after_it + 1, 2 * chip + 1))
        self.home_pairs = [(target, source) for source, target in self.out_pairs]

    def swap(self, field):
        return lax.ppermute(field, "ctx", self.swap_pairs)

    def out(self, field):
        return lax.ppermute(field, "ctx", self.out_pairs)

    def home(self, field):
        return lax.ppermute(field, "ctx", self.home_pairs)

    def members(self, rank):
        chip, core = rank // 2, rank % 2
        place = self.order.index(chip)
        blocks = [rank]
        for step in range(1, self.reach + 1):
            near = self.order[(place + (2 * core - 1) * step) % self.chips]
            blocks.append(2 * near + core)
            if step < self.reach:
                blocks.append(2 * near + 1 - core)
        return blocks

    def gather(self, block):
        first, second = block, self.swap(block)
        blocks = [block]
        for step in range(1, self.reach + 1):
            first = self.out(first)
            blocks.append(first)
            if step < self.reach:
                second = self.out(second)
                blocks.append(second)
        return blocks

    def scatter_sum(self, term, needs=None):
        needs = needs or {}
        first = self.home(term(2 * self.reach - 1))
        second = None
        marks = {self.reach: first}
        for step in range(self.reach - 1, 0, -1):
            if step in needs:
                first = after(first, needs[step])
            first = self.home((term(2 * step - 1).astype(f32) + first.astype(f32)).astype(bf16))
            other = term(2 * step)
            if second is not None:
                other = (other.astype(f32) + second.astype(f32)).astype(bf16)
            second = self.home(other)
            marks[step] = first
        total = first.astype(f32) + term(0).astype(f32) + self.swap(second).astype(f32)
        return total, marks


def after(value, *events):
    return lax.optimization_barrier((value, events))[0]


def spread(rows_block):
    return lax.all_to_all(rows_block, "ctx", split_axis=0, concat_axis=0, tiled=False)


def swap_rows(field):
    return lax.ppermute(field, "fsdp", [(0, 1), (1, 0)])


def to_columns(received, partner, fsdp_rank):
    first = jnp.where(fsdp_rank == 0, received, partner)
    second = jnp.where(fsdp_rank == 0, partner, received)
    both = jnp.stack([first, second], axis=1)
    return both.reshape(-1, received.shape[-1])


def to_rows(grads, extra, fsdp_rank, ctx_size, events=()):
    width = grads.shape[1]
    split = grads.reshape(ctx_size, 2, -1, width)
    rows = split.shape[2]
    keep = jnp.where(fsdp_rank == 0, split[:, 0], split[:, 1])
    give = jnp.where(fsdp_rank == 0, split[:, 1], split[:, 0])
    if extra is None:
        given = after(swap_rows(give), *events)
        return (keep.astype(f32) + given.astype(f32)).astype(bf16)
    count = extra.shape[0]
    lines = -(-count // width)
    lines = -(-lines // 16) * 16
    extra_block = jnp.pad(extra, (0, lines * width - count)).reshape(lines, width).astype(bf16)
    given = swap_rows(jnp.concatenate([give.reshape(-1, width), extra_block], axis=0))
    given = after(given, *events)
    body = given[: ctx_size * rows].reshape(ctx_size, rows, width)
    total = (keep.astype(f32) + body.astype(f32)).astype(bf16)
    extras = (extra_block.astype(f32) + given[ctx_size * rows :].astype(f32)).astype(bf16)
    return jnp.concatenate(
        [total, jnp.broadcast_to(extras[None], (ctx_size, lines, width))], axis=1
    )


def come_home(sent, rows, count):
    received = spread(sent)
    extra_sum = jnp.sum(received[:, rows:].astype(f32), axis=0).reshape(-1)[:count]
    return received[:, :rows], extra_sum


def side_by_side(pieces):
    count, rows, width = pieces.shape
    return jnp.transpose(pieces, (1, 0, 2)).reshape(rows, count * width)


def shards(
    block_input,
    query_weight,
    key_weight,
    value_weight,
    output_weight,
    gate_weight,
    up_weight,
    down_weight,
    attn_gain,
    mlp_gain,
    query_gain,
    key_gain,
    block_order,
    cotangent,
):
    ctx_size = lax.axis_size("ctx")
    ctx_rank = lax.axis_index("ctx")
    fsdp_rank = lax.axis_index("fsdp")
    core = ctx_rank % 2
    tokens = block_input.shape[1]
    model = block_input.shape[2]
    head_size = query_gain.shape[0]
    kv_heads = key_weight.shape[1] // head_size
    slots = block_order.shape[0]
    length = tokens * ctx_size
    half_rows = length // slots
    per_block = tokens // half_rows
    weight_rows = query_weight.shape[0]
    hidden_slice = gate_weight.shape[1] // ctx_size
    splits = ctx_size // 2 // kv_heads
    split_rank = (ctx_rank // 2) % splits
    sorted_all = splits == 1
    score_scale = 1.0 / math.sqrt(head_size)
    ring = Ring(ctx_size)

    def block_rows(field, index):
        return field[index * tokens : (index + 1) * tokens]

    def by_head(weight):
        split = jnp.transpose(weight.reshape(weight_rows, kv_heads, -1, head_size), (1, 2, 0, 3))
        return jnp.broadcast_to(split[:, None], (kv_heads, splits) + split.shape[1:]).reshape(
            -1, weight_rows, head_size
        )

    key_value = jnp.stack(
        [key_weight.reshape(weight_rows, kv_heads, head_size),
         value_weight.reshape(weight_rows, kv_heads, head_size)],
        axis=2,
    ).reshape(weight_rows, -1)
    head_block = jnp.concatenate(
        [by_head(query_weight), by_head(output_weight), by_head(key_value)], axis=2
    )
    head_received = spread(head_block)
    head_mine = to_columns(head_received, swap_rows(head_received), fsdp_rank)
    head_other = ring.swap(head_mine)

    def column(field, index):
        return field[:, index * head_size : (index + 1) * head_size]

    def key_first(mine, other):
        return jnp.where(core == 0, mine, other), jnp.where(core == 0, other, mine)

    key_columns, value_columns = key_first(column(head_mine, 2), column(head_other, 2))
    head_weight = jnp.concatenate(
        [column(head_mine, 0), key_columns, value_columns, column(head_other, 0)], axis=1
    )
    output_part = jnp.concatenate([column(head_mine, 1), column(head_other, 1)], axis=1)

    member_table = np.array(
        [ring.members(rank) + ring.members(rank ^ 1) for rank in range(ctx_size)], np.int32
    )
    ranks = jnp.arange(ctx_size, dtype=jnp.int32)
    listed = jnp.sum(jnp.where(ranks[:, None] == ctx_rank, member_table, 0), axis=0)
    slot_index = jnp.arange(slots, dtype=jnp.int32)
    local_slot = (
        listed[:, None] * per_block + jnp.arange(per_block, dtype=jnp.int32)[None, :]
    ).reshape(-1)
    local_pos = jnp.sum(
        jnp.where(local_slot[:, None] == slot_index[None, :], block_order[None, :], 0), axis=1
    )
    cosine, sine = rope_tables(jnp.arange(length, dtype=jnp.int32), head_size)
    if sorted_all:
        tables = (local_pos, slot_index, slot_index)
    else:
        local_of_pos = jnp.sum(
            jnp.where(local_pos[None, :] == slot_index[:, None], slot_index[None, :], 0), axis=1
        )
        compact = jnp.arange(slots // splits, dtype=jnp.int32)
        owner = (compact // per_block) * splits + split_rank
        own_pos = jnp.sort(jnp.take(block_order, owner * per_block + compact % per_block))
        tables = (local_pos, jnp.take(local_of_pos, own_pos), own_pos)
    query_row, key_row = query_gain[None, :], key_gain[None, :]

    input_blocks = ring.gather(block_input[0])
    input_blocks[3], tables, cosine, sine = lax.optimization_barrier(
        (input_blocks[3], tables, cosine, sine)
    )
    input_blocks[4] = after(input_blocks[4], head_received)

    def by_slice(weight):
        return jnp.transpose(weight.reshape(weight_rows, ctx_size, hidden_slice), (1, 0, 2))

    gate_up_block = jnp.concatenate([by_slice(gate_weight), by_slice(up_weight)], axis=2)
    down_block = by_slice(down_weight)
    input_blocks[5], gate_up_block, down_block = lax.optimization_barrier(
        (input_blocks[5], gate_up_block, down_block)
    )
    normed_list = []
    for block in input_blocks:
        wide = block.astype(f32)
        normed_list.append((wide * inv_root(wide) * attn_gain).astype(bf16))
    normed_attn = lax.optimization_barrier(jnp.concatenate(normed_list, axis=0))
    projected = dot_nn(normed_attn, head_weight)
    projected_given = ring.swap(
        jnp.concatenate(
            [projected[:, 3 * head_size :], projected[:, head_size : 3 * head_size]], axis=1
        )
    )
    raw = (projected, projected_given)
    attn_a, attn_b, lse, *saved = attend(
        tables, raw, cosine, sine, query_row, key_row, half_rows, sorted_all, score_scale
    )
    gate_up_received = spread(after(gate_up_block, input_blocks[-2]))
    gate_up_partner = swap_rows(gate_up_received)
    down_received = spread(after(down_block, gate_up_received))
    down_partner = swap_rows(down_received)
    attn_a, attn_b = after((attn_a, attn_b), gate_up_received)
    attn_pair = jnp.concatenate([attn_a, ring.swap(attn_b)], axis=1)

    inputs32 = block_input[0].astype(f32)
    scale_attn = inv_root(inputs32)
    attn_terms = dot_nt(attn_pair, output_part).astype(bf16)
    attn_out, _ = ring.scatter_sum(
        lambda i: block_rows(attn_terms, i),
        {ring.reach - 1: down_received, ring.reach - 2: gate_up_partner},
    )
    attn_out, gate_up_partner, down_partner = lax.optimization_barrier(
        (attn_out, gate_up_partner, down_partner)
    )
    hidden_one = inputs32 + attn_out
    scale_mlp = inv_root(hidden_one)
    normed_mlp = (hidden_one * scale_mlp * mlp_gain).astype(bf16)
    gate_up_mine = to_columns(gate_up_received, gate_up_partner, fsdp_rank)
    gate_up = jnp.concatenate([gate_up_mine, ring.swap(gate_up_mine)], axis=1)
    down_mine = to_columns(down_received, down_partner, fsdp_rank)
    down_part = jnp.concatenate([down_mine, ring.swap(down_mine)], axis=1)

    normed_blocks = ring.gather(normed_mlp)
    normed_all = jnp.concatenate(normed_blocks, axis=0)
    cot_blocks = ring.gather(after(cotangent[0], normed_blocks[-2]))
    cot_all = jnp.concatenate(cot_blocks, axis=0)
    hidden_all = dot_nn(normed_all, gate_up)
    act_grad_all = dot_nn(cot_all, down_part)
    activated_list, back_list = [], []
    for member in range(2):
        gate_pre = hidden_all[:, 2 * member * hidden_slice : (2 * member + 1) * hidden_slice]
        up_pre = hidden_all[:, (2 * member + 1) * hidden_slice : (2 * member + 2) * hidden_slice]
        act_grad = act_grad_all[:, member * hidden_slice : (member + 1) * hidden_slice]
        sigma = jax.nn.sigmoid(gate_pre)
        activated_list.append((gate_pre * sigma * up_pre).astype(bf16))
        back_list.append(
            (act_grad * up_pre * sigma * (1.0 + gate_pre * (1.0 - sigma))).astype(bf16)
        )
        back_list.append((act_grad * gate_pre * sigma).astype(bf16))
    activated_all = jnp.concatenate(activated_list, axis=1)
    back_all = jnp.concatenate(back_list, axis=1)
    far = (2 * ring.reach - 3) * tokens
    far_terms = dot_nt(back_all[far:], gate_up).astype(bf16)
    near_terms = dot_nt(back_all[:far], gate_up).astype(bf16)
    near_blocks = far // tokens
    normed_mlp_grad, _ = ring.scatter_sum(
        lambda i: block_rows(near_terms, i) if i < near_blocks else block_rows(far_terms, i - near_blocks)
    )
    out_terms = dot_nt(activated_all, down_part).astype(bf16)
    mlp_out, _ = ring.scatter_sum(lambda i: block_rows(out_terms, i))
    block_out = (hidden_one + mlp_out).astype(bf16)
    grad32 = cotangent[0].astype(f32)
    hidden_grad = grad32 + norm_back(hidden_one, scale_mlp, mlp_gain, normed_mlp_grad)
    hidden_grad_bf = hidden_grad.astype(bf16)

    mlp_gain_part = (
        jnp.sum(near_terms.astype(f32) * normed_all[:far].astype(f32), axis=0)
        + jnp.sum(far_terms.astype(f32) * normed_all[far:].astype(f32), axis=0)
    ) / mlp_gain
    pair = 2 * hidden_slice
    add = lambda left, right: (left.astype(f32) + right.astype(f32)).astype(bf16)
    down_give = dot_tn(cot_all, activated_all[:, hidden_slice:]).astype(bf16)
    down_keep = dot_tn(cot_all, activated_all[:, :hidden_slice]).astype(bf16)
    gate_up_give = dot_tn(normed_all, back_all[:, pair:]).astype(bf16)
    gate_up_keep = dot_tn(normed_all, back_all[:, :pair]).astype(bf16)

    grad_blocks = ring.gather(hidden_grad_bf)
    grad_all = jnp.concatenate(grad_blocks, axis=0)
    attn_grad_pair = dot_nn(grad_all, output_part).astype(bf16)
    attn_grad = (attn_grad_pair[:, :head_size], ring.swap(attn_grad_pair[:, head_size:]))
    down_sent = to_rows(
        add(down_keep, ring.swap(down_give)), mlp_gain_part, fsdp_rank, ctx_size, (grad_blocks[1],)
    )
    gate_up_sent = to_rows(
        add(gate_up_keep, ring.swap(gate_up_give)), None, fsdp_rank, ctx_size, (grad_blocks[-1],)
    )
    attn_grad, down_sent, gate_up_sent = lax.optimization_barrier(
        (attn_grad, down_sent, gate_up_sent)
    )
    gate_up_rows = spread(gate_up_sent)
    down_rows, mlp_gain_sum = come_home(down_sent, weight_rows, model)
    first_a, first_b, query_gain_part, key_gain_part = attend_back(
        tables, raw, cosine, sine, query_row, key_row, saved, (attn_a, attn_b), attn_grad, lse,
        half_rows, sorted_all, score_scale,
    )
    given_grads = ring.swap(first_b)
    half_grads = jnp.concatenate(
        [
            first_a[:, :head_size],
            add(first_a[:, head_size:], given_grads[:, head_size:]),
            given_grads[:, :head_size],
        ],
        axis=1,
    )
    input_terms = dot_nt(half_grads, head_weight).astype(bf16)
    normed_attn_grad, marks = ring.scatter_sum(
        lambda i: block_rows(input_terms, i), {ring.reach - 2: gate_up_rows}
    )
    late_grads = after(half_grads, marks[ring.reach])
    input_grad = hidden_grad + norm_back(inputs32, scale_attn, attn_gain, normed_attn_grad)
    head_grad = dot_tn(normed_attn, late_grads).astype(bf16)
    output_grad = dot_tn(grad_all, attn_pair).astype(bf16)
    attn_gain_part = (
        jnp.sum(input_terms.astype(f32) * normed_attn.astype(f32), axis=0) / attn_gain
    )
    kv_keep, kv_give = key_first(column(head_grad, 1), column(head_grad, 2))
    attn_keep = jnp.concatenate([column(head_grad, 0), column(output_grad, 0), kv_keep], axis=1)
    attn_give = jnp.concatenate([column(head_grad, 3), column(output_grad, 1), kv_give], axis=1)
    attn_rows, attn_extra = come_home(
        to_rows(
            add(attn_keep, ring.swap(attn_give)),
            jnp.concatenate([attn_gain_part, query_gain_part[0], key_gain_part[0]]),
            fsdp_rank,
            ctx_size,
        ),
        weight_rows,
        model + 2 * head_size,
    )

    def home(index):
        part = attn_rows[:, :, index * head_size : (index + 1) * head_size].astype(f32)
        return jnp.sum(part.reshape(kv_heads, splits, 2, weight_rows, head_size), axis=1)

    key_value_rows = home(2)
    flat = lambda part: side_by_side(part.reshape(-1, weight_rows, head_size))

    gate_rows, up_rows = gate_up_rows[:, :, :hidden_slice], gate_up_rows[:, :, hidden_slice:]

    return (
        block_out[None],
        input_grad[None],
        flat(home(0)),
        flat(key_value_rows[:, 0]),
        flat(key_value_rows[:, 1]),
        flat(home(1)),
        side_by_side(gate_rows).astype(f32),
        side_by_side(up_rows).astype(f32),
        side_by_side(down_rows).astype(f32),
        attn_extra[:model],
        mlp_gain_sum,
        attn_extra[model : model + head_size],
        attn_extra[model + head_size :],
    )


def solution(mesh):
    in_specs = (
        P("fsdp", "ctx", None),
        P(("ctx", "fsdp"), None),
        P(("ctx", "fsdp"), None),
        P(("ctx", "fsdp"), None),
        P(("ctx", "fsdp"), None),
        P(("ctx", "fsdp"), None),
        P(("ctx", "fsdp"), None),
        P(("ctx", "fsdp"), None),
        P(),
        P(),
        P(),
        P(),
        P(),
        P("fsdp", "ctx", None),
    )
    out_specs = (
        P("fsdp", "ctx", None),
        P("fsdp", "ctx", None),
        P(("ctx", "fsdp"), None),
        P(("ctx", "fsdp"), None),
        P(("ctx", "fsdp"), None),
        P(("ctx", "fsdp"), None),
        P(("ctx", "fsdp"), None),
        P(("ctx", "fsdp"), None),
        P(("ctx", "fsdp"), None),
        P(),
        P(),
        P(),
        P(),
    )
    return jax.shard_map(shards, mesh=mesh, in_specs=in_specs, out_specs=out_specs, check_vma=False)
```

```python
import functools
import math

import jax
import jax.numpy as jnp
import numpy as np
from jax import lax
from jax.experimental import pallas as pl
from jax.experimental.layout import Layout, with_layout_constraint
from jax.experimental.pallas import tpu as pltpu
from jax.sharding import PartitionSpec as P

eps_model = 1e-06
rope_base = 1000000.0
f32 = jnp.float32
bf16 = jnp.bfloat16


def inv_root(field):
    return lax.rsqrt(jnp.mean(field * field, axis=-1, keepdims=True) + eps_model)


def norm_back(field, factor, gain, grad_in):
    weighted = gain * grad_in
    inner_mean = jnp.mean(weighted * field, axis=-1, keepdims=True)
    return factor * weighted - field * (factor * factor * factor) * inner_mean


def rope_tables(positions, head_size):
    half_size = head_size // 2
    exponent = jnp.arange(half_size, dtype=f32) * f32(2.0 / head_size)
    inverse = jnp.exp(-exponent * f32(math.log(rope_base)))
    angles = positions.astype(f32)[:, None] * inverse[None, :]
    cosine, sine = jnp.cos(angles), jnp.sin(angles)
    return jnp.concatenate([cosine, cosine], axis=1), jnp.concatenate([-sine, sine], axis=1)


def dot_nn(left, right):
    return lax.dot_general(left, right, (((1,), (0,)), ((), ())), preferred_element_type=f32)


def dot_nt(left, right):
    return lax.dot_general(left, right, (((1,), (1,)), ((), ())), preferred_element_type=f32)


def dot_tn(left, right):
    return lax.dot_general(left, right, (((0,), (0,)), ((), ())), preferred_element_type=f32)


def allowed_tile(key_first, query_tile, pos_table, tile_k, tile_q, rows, sorted_all):
    key_pos = key_first + lax.broadcasted_iota(jnp.int32, (tile_k, tile_q), 0)
    lane = lax.broadcasted_iota(jnp.int32, (1, tile_q), 1)
    if sorted_all:
        query_pos = query_tile * tile_q + lane
    else:
        per_tile = tile_q // rows
        query_pos = jnp.zeros((1, tile_q), jnp.int32)
        for piece in range(per_tile):
            first = pos_table[query_tile * per_tile + piece] * rows
            inside = (lane >= piece * rows) & (lane < (piece + 1) * rows)
            query_pos = jnp.where(inside, first + lane - piece * rows, query_pos)
    return key_pos <= query_pos


def tile_loop(query_tile, key_tiles, sorted_all, work):
    if sorted_all:
        for key_tile in range(query_tile):
            work(key_tile, False)
        work(query_tile, True)
    else:

        @pl.loop(0, key_tiles)
        def _(key_tile):
            work(key_tile, True)


def query_loop(query_tiles, sorted_all, work):
    if sorted_all:
        for query_tile in range(query_tiles):
            work(query_tile)
    else:

        @pl.loop(0, query_tiles)
        def _(query_tile):
            work(query_tile)


def block_loop(blocks, work):
    def step(index, carry):
        work(index)
        return carry

    lax.fori_loop(0, blocks, step, 0, unroll=4)


def rows_at(index, rows):
    return pl.ds(pl.multiple_of(index * rows, rows), rows)


def each_key(key_pos, blocks, rows, work):
    for part in range(2):
        block_loop(
            blocks // 2,
            lambda index: work(
                part, rows_at(index, rows), rows_at(key_pos[part * (blocks // 2) + index], rows)
            ),
        )


def each_query(key_pos, query_table, pos_table, blocks, count, rows, sorted_all, work):
    if sorted_all:
        each_key(key_pos, blocks, rows, lambda part, here, place: work(part, here, place, place))
        return

    @pl.loop(0, count)
    def _(index):
        local = query_table[index]
        place, at_pos = rows_at(index, rows), rows_at(pos_table[index], rows)
        for part in range(2):
            inner = local - part * (blocks // 2)

            @pl.when((inner >= 0) & (inner < blocks // 2))
            def _():
                work(part, rows_at(inner, rows), place, at_pos)


def turn(field):
    return pltpu.roll(field, field.shape[-1] // 2, 1)


def attend_kernel(
    geometry, key_pos, query_table, pos_table, raw_a, raw_b, cos_ref, sin_ref, q_gain, k_gain,
    out_a, out_b, lse_ref, q_sorted, k_sorted, v_sorted, v_turned, acc, total, out_sorted,
):
    rows, tile, sorted_all, scale = geometry
    head = q_gain.shape[1]
    keys, queries = k_sorted.shape[0], q_sorted.shape[0]
    key_tiles, query_tiles = keys // tile, queries // tile
    raw, out = (raw_a, raw_b), (out_a, out_b)
    walk = (key_pos, query_table, pos_table, keys // rows, queries // rows, rows, sorted_all)

    def rope(field, gain, place):
        normed = field * inv_root(field) * gain[...]
        return (normed * cos_ref[place, :] + turn(normed) * sin_ref[place, :]).astype(bf16)

    def take_keys(part, here, place):
        k_sorted[place, :] = rope(raw[part][here, head : 2 * head], k_gain, place)
        v_sorted[place, :] = raw[part][here, 2 * head : 3 * head].astype(bf16)

    def take_queries(part, here, place, at_pos):
        q_sorted[place, :] = rope(raw[part][here, :head], q_gain, at_pos)

    each_key(key_pos, keys // rows, rows, take_keys)
    each_query(*walk, take_queries)
    for key_tile in range(key_tiles):
        piece = v_sorted[key_tile * tile : (key_tile + 1) * tile, :]
        v_turned[:, key_tile * tile : (key_tile + 1) * tile] = piece.astype(f32).T.astype(bf16)
    if not sorted_all:
        out_a[...] = jnp.zeros_like(out_a)
        out_b[...] = jnp.zeros_like(out_b)

    def query_work(query_tile):
        q_start = pl.multiple_of(query_tile * tile, tile)
        q_tile = q_sorted[pl.ds(q_start, tile), :]
        acc[...] = jnp.zeros_like(acc)
        total[...] = jnp.zeros_like(total)

        def work(key_tile, masked):
            k_start = pl.multiple_of(key_tile * tile, tile)
            scores = dot_nt(k_sorted[pl.ds(k_start, tile), :], q_tile)
            probs = jnp.exp(scores * scale)
            if masked:
                keep = allowed_tile(k_start, query_tile, pos_table, tile, tile, rows, sorted_all)
                probs = jnp.where(keep, probs, 0.0)
            total[...] += jnp.sum(probs, axis=0, keepdims=True)
            acc[...] += dot_nn(v_turned[:, pl.ds(k_start, tile)], probs.astype(bf16))

        tile_loop(query_tile, key_tiles, sorted_all, work)
        lse_ref[:, pl.ds(q_start, tile)] = jnp.log(total[...])
        out_sorted[pl.ds(q_start, tile), :] = (acc[...] / total[...]).T.astype(bf16)

    query_loop(query_tiles, sorted_all, query_work)

    def put(part, here, place, at_pos):
        out[part][here, :] = out_sorted[place, :]

    each_query(*walk, put)


def whole_spec(shape):
    return pl.BlockSpec(memory_space=pltpu.VMEM)


def attend(tables, raw, cosine, sine, query_gain, key_gain, rows, sorted_all, scale):
    head = query_gain.shape[1]
    keys = cosine.shape[0]
    queries = tables[1].shape[0] * rows
    tile = math.gcd(math.gcd(queries, keys), 512)
    narrow, row, part = whole_spec((keys, head)), whole_spec((1, head)), whole_spec((keys // 2, head))
    return pl.pallas_call(
        functools.partial(attend_kernel, (rows, tile, sorted_all, scale)),
        out_shape=(
            jax.ShapeDtypeStruct((keys // 2, head), bf16),
            jax.ShapeDtypeStruct((keys // 2, head), bf16),
            jax.ShapeDtypeStruct((1, queries), f32),
            jax.ShapeDtypeStruct((queries, head), bf16),
            jax.ShapeDtypeStruct((keys, head), bf16),
            jax.ShapeDtypeStruct((keys, head), bf16),
        ),
        grid_spec=pltpu.PrefetchScalarGridSpec(
            num_scalar_prefetch=3,
            grid=(1,),
            in_specs=[whole_spec(raw[0].shape), whole_spec(raw[1].shape), narrow, narrow, row, row],
            out_specs=(part, part, whole_spec((1, queries)), whole_spec((queries, head)), narrow, narrow),
            scratch_shapes=[
                pltpu.VMEM((head, keys), bf16),
                pltpu.VMEM((head, tile), f32),
                pltpu.VMEM((1, tile), f32),
                pltpu.VMEM((queries, head), bf16),
            ],
        ),
        compiler_params=pltpu.CompilerParams(vmem_limit_bytes=48 * 2**20),
        cost_estimate=pl.CostEstimate(
            flops=4 * queries * keys * head, bytes_accessed=28 * keys * head, transcendentals=queries * keys
        ),
        name="attend",
    )(*tables, *raw, cosine, sine, query_gain, key_gain)


def attend_back_kernel(
    geometry, key_pos, query_table, pos_table, raw_a, raw_b, cos_ref, sin_ref, q_gain, k_gain,
    q_sorted, k_sorted, v_sorted, o_a, o_b, do_a, do_b, lse_ref,
    grads_a, grads_b, q_part, k_part,
    do_sorted, o_sorted, k_turned, delta, dq_turned, dq_sorted, dk_sorted, dv_sorted,
):
    rows, tile, sorted_all, scale = geometry
    head = q_gain.shape[1]
    keys, queries = k_sorted.shape[0], q_sorted.shape[0]
    key_tiles, query_tiles = keys // tile, queries // tile
    raw, o_ref, do_ref, grads = (raw_a, raw_b), (o_a, o_b), (do_a, do_b), (grads_a, grads_b)
    walk = (key_pos, query_table, pos_table, keys // rows, queries // rows, rows, sorted_all)

    def take(part, here, place, at_pos):
        do_sorted[place, :] = do_ref[part][here, :]
        o_sorted[place, :] = o_ref[part][here, :]

    each_query(*walk, take)
    for key_tile in range(key_tiles):
        piece = k_sorted[key_tile * tile : (key_tile + 1) * tile, :]
        k_turned[:, key_tile * tile : (key_tile + 1) * tile] = piece.astype(f32).T.astype(bf16)
    dk_sorted[...] = jnp.zeros_like(dk_sorted)
    dv_sorted[...] = jnp.zeros_like(dv_sorted)
    if not sorted_all:
        for part in range(2):
            grads[part][:, :head] = jnp.zeros((keys // 2, head), bf16)

    def query_work(query_tile):
        q_start = pl.multiple_of(query_tile * tile, tile)
        q_tile = q_sorted[pl.ds(q_start, tile), :]
        do_tile = do_sorted[pl.ds(q_start, tile), :]
        product = do_tile.astype(f32) * o_sorted[pl.ds(q_start, tile), :].astype(f32)
        delta[...] = jnp.sum(product.T, axis=0, keepdims=True)
        dq_turned[...] = jnp.zeros_like(dq_turned)

        def work(key_tile, masked):
            k_start = pl.multiple_of(key_tile * tile, tile)
            here = pl.ds(k_start, tile)
            scores = dot_nt(k_sorted[here, :], q_tile)
            probs = jnp.exp(scores * scale - lse_ref[:, pl.ds(q_start, tile)])
            if masked:
                keep = allowed_tile(k_start, query_tile, pos_table, tile, tile, rows, sorted_all)
                probs = jnp.where(keep, probs, 0.0)
            dv_sorted[here, :] += dot_nn(probs.astype(bf16), do_tile)
            d_probs = dot_nt(v_sorted[here, :], do_tile)
            d_scores = (probs * (d_probs - delta[...])).astype(bf16)
            dk_sorted[here, :] += dot_nn(d_scores, q_tile)
            dq_turned[...] += dot_nn(k_turned[:, here], d_scores)

        tile_loop(query_tile, key_tiles, sorted_all, work)
        dq_sorted[pl.ds(q_start, tile), :] = dq_turned[...].T

    query_loop(query_tiles, sorted_all, query_work)
    q_part[...] = jnp.zeros_like(q_part)
    k_part[...] = jnp.zeros_like(k_part)

    def through_norm(field, grad, gain, at_pos, gain_part):
        scaled = grad * scale
        normed_grad = scaled * cos_ref[at_pos, :] - turn(scaled) * sin_ref[at_pos, :]
        factor = inv_root(field)
        gain_part[...] += jnp.sum(normed_grad * field * factor, axis=0, keepdims=True)
        return norm_back(field, factor, gain[...], normed_grad).astype(bf16)

    def put_queries(part, here, place, at_pos):
        grads[part][here, :head] = through_norm(
            raw[part][here, :head], dq_sorted[place, :], q_gain, at_pos, q_part
        )

    def put_keys(part, here, place):
        grads[part][here, head : 2 * head] = through_norm(
            raw[part][here, head : 2 * head], dk_sorted[place, :], k_gain, place, k_part
        )
        grads[part][here, 2 * head :] = dv_sorted[place, :].astype(bf16)

    each_query(*walk, put_queries)
    each_key(key_pos, keys // rows, rows, put_keys)


def attend_back(tables, raw, cosine, sine, query_gain, key_gain, saved, out, d_out, lse, rows, sorted_all, scale):
    head = query_gain.shape[1]
    keys = cosine.shape[0]
    queries = tables[1].shape[0] * rows
    tile = math.gcd(math.gcd(queries, keys), 512)
    narrow, row, part = whole_spec((keys, head)), whole_spec((1, head)), whole_spec((keys // 2, head))
    q_spec, wide = whole_spec((queries, head)), whole_spec((keys // 2, 3 * head))
    return pl.pallas_call(
        functools.partial(attend_back_kernel, (rows, tile, sorted_all, scale)),
        out_shape=(
            jax.ShapeDtypeStruct((keys // 2, 3 * head), bf16),
            jax.ShapeDtypeStruct((keys // 2, 3 * head), bf16),
            jax.ShapeDtypeStruct((1, head), f32),
            jax.ShapeDtypeStruct((1, head), f32),
        ),
        grid_spec=pltpu.PrefetchScalarGridSpec(
            num_scalar_prefetch=3,
            grid=(1,),
            in_specs=[
                whole_spec(raw[0].shape), whole_spec(raw[1].shape), narrow, narrow, row, row,
                q_spec, narrow, narrow, part, part, part, part, whole_spec((1, queries)),
            ],
            out_specs=(wide, wide, row, row),
            scratch_shapes=[
                pltpu.VMEM((queries, head), bf16),
                pltpu.VMEM((queries, head), bf16),
                pltpu.VMEM((head, keys), bf16),
                pltpu.VMEM((1, tile), f32),
                pltpu.VMEM((head, tile), f32),
                pltpu.VMEM((queries, head), f32),
                pltpu.VMEM((keys, head), f32),
                pltpu.VMEM((keys, head), f32),
            ],
        ),
        compiler_params=pltpu.CompilerParams(vmem_limit_bytes=60 * 2**20),
        cost_estimate=pl.CostEstimate(
            flops=10 * queries * keys * head, bytes_accessed=40 * keys * head, transcendentals=queries * keys
        ),
        name="attend_back",
    )(*tables, *raw, cosine, sine, query_gain, key_gain, *saved, *out, *d_out, lse)


def project_kernel(weight_ref, gain_ref, *refs):
    count = len(refs) - 2
    normed_ref, out_ref = refs[count:]
    rows = refs[0].shape[0]
    for index in range(count):
        wide = refs[index][...].astype(f32)
        normed = (wide * inv_root(wide) * gain_ref[...]).astype(bf16)
        place = pl.ds(index * rows, rows)
        normed_ref[place, :] = normed
        out_ref[place, :] = dot_nn(normed, weight_ref[...])


def project(blocks, gain, weight):
    rows, width = blocks[0].shape
    total, columns = rows * len(blocks), weight.shape[1]
    return pl.pallas_call(
        project_kernel,
        out_shape=(
            jax.ShapeDtypeStruct((total, width), bf16),
            jax.ShapeDtypeStruct((total, columns), f32),
        ),
        grid=(1,),
        in_specs=[whole_spec(weight.shape), whole_spec((1, width))]
        + [whole_spec((rows, width))] * len(blocks),
        out_specs=(whole_spec((total, width)), whole_spec((total, columns))),
        compiler_params=pltpu.CompilerParams(vmem_limit_bytes=48 * 2**20),
        cost_estimate=pl.CostEstimate(
            flops=2 * total * width * columns, bytes_accessed=4 * total * width, transcendentals=total
        ),
        name="project",
    )(weight, gain[None, :], *blocks)


class Ring:
    def __init__(self, size):
        self.chips = size // 2
        self.reach = self.chips // 2
        self.order = list(range(0, self.chips, 2)) + list(range(self.chips - 1, 0, -2))
        self.swap_pairs = [(i, i ^ 1) for i in range(size)]
        self.out_pairs = []
        for place, chip in enumerate(self.order):
            after_it = self.order[(place + 1) % self.chips]
            self.out_pairs.append((2 * chip, 2 * after_it))
            self.out_pairs.append((2 * after_it + 1, 2 * chip + 1))
        self.home_pairs = [(target, source) for source, target in self.out_pairs]

    def swap(self, field):
        return lax.ppermute(field, "ctx", self.swap_pairs)

    def out(self, field):
        return lax.ppermute(field, "ctx", self.out_pairs)

    def home(self, field):
        return lax.ppermute(field, "ctx", self.home_pairs)

    def members(self, rank):
        chip, core = rank // 2, rank % 2
        place = self.order.index(chip)
        blocks = [rank]
        for step in range(1, self.reach + 1):
            near = self.order[(place + (2 * core - 1) * step) % self.chips]
            blocks.append(2 * near + core)
            if step < self.reach:
                blocks.append(2 * near + 1 - core)
        return blocks

    def gather(self, block, hooks=None):
        hooks = hooks or {}
        streams = [block, self.swap(block)]
        blocks = [block]
        for hop in range(2 * self.reach - 1):
            held = streams[hop % 2]
            if hop >= 3:
                held = after(held, blocks[hop - 2])
            if hop in hooks:
                held = after(held, hooks[hop](blocks))
            streams[hop % 2] = self.out(held)
            blocks.append(streams[hop % 2])
        return blocks

    def scatter_hops(self, term, streams, hops, needs=None, first_twice=False):
        needs = needs or {}
        order = list(range(2 * self.reach - 1, 0, -1))
        if first_twice:
            for place in range(1, len(order), 2):
                order[place : place + 2] = reversed(order[place : place + 2])
        streams, marks, total = list(streams), [], None
        for hop in hops:
            index = order[hop]
            stream, held = 1 - index % 2, streams[1 - index % 2]
            if held is None:
                total = term(index)
            else:
                held = held if total is None else after(held, total)
                total = (term(index).astype(f32) + held.astype(f32)).astype(bf16)
            if hop in needs:
                total = after(total, needs[hop](marks))
            streams[stream] = self.home(total)
            marks.append(streams[stream])
        return streams, marks

    def scatter_end(self, term, streams):
        first, second = streams
        return first.astype(f32) + term(0).astype(f32) + self.swap(second).astype(f32)

    def scatter_sum(self, term, needs=None, first_twice=False):
        streams, marks = self.scatter_hops(
            term, [None, None], range(2 * self.reach - 1), needs, first_twice
        )
        return self.scatter_end(term, streams), marks


def after(value, *events):
    return lax.optimization_barrier((value, events))[0]


def spread(rows_block):
    return lax.all_to_all(rows_block, "ctx", split_axis=0, concat_axis=0, tiled=False)


def swap_rows(field):
    return lax.ppermute(field, "fsdp", [(0, 1), (1, 0)])


def to_columns(received, partner, fsdp_rank):
    first = jnp.where(fsdp_rank == 0, received, partner)
    second = jnp.where(fsdp_rank == 0, partner, received)
    both = jnp.stack([first, second], axis=1)
    return both.reshape(-1, received.shape[-1])


def halves(grads, extra, fsdp_rank, ctx_size):
    width = grads.shape[1]
    split = grads.reshape(ctx_size, 2, -1, width)
    keep = jnp.where(fsdp_rank == 0, split[:, 0], split[:, 1])
    give = jnp.where(fsdp_rank == 0, split[:, 1], split[:, 0])
    if extra is None:
        return keep, give, None
    count = extra.shape[0]
    lines = -(-count // width)
    lines = -(-lines // 16) * 16
    extra_block = jnp.pad(extra, (0, lines * width - count)).reshape(lines, width).astype(bf16)
    return keep, jnp.concatenate([give.reshape(-1, width), extra_block], axis=0), extra_block


def join(keep, given, extra_block):
    if extra_block is None:
        return (keep.astype(f32) + given.astype(f32)).astype(bf16)
    ctx_size, rows, width = keep.shape
    body = given[: ctx_size * rows].reshape(keep.shape)
    total = (keep.astype(f32) + body.astype(f32)).astype(bf16)
    extras = (extra_block.astype(f32) + given[ctx_size * rows :].astype(f32)).astype(bf16)
    return jnp.concatenate(
        [total, jnp.broadcast_to(extras[None], (ctx_size,) + extras.shape)], axis=1
    )


def apart(received, rows, width, count):
    lines = received[:, rows:, :width].astype(f32)
    return received[:, :rows], jnp.sum(lines, axis=0).reshape(-1)[:count]


def side_by_side(pieces):
    count, rows, width = pieces.shape
    return jnp.transpose(pieces, (1, 0, 2)).reshape(rows, count * width)


def shards(
    block_input,
    query_weight,
    key_weight,
    value_weight,
    output_weight,
    gate_weight,
    up_weight,
    down_weight,
    attn_gain,
    mlp_gain,
    query_gain,
    key_gain,
    block_order,
    cotangent,
):
    ctx_size = lax.axis_size("ctx")
    ctx_rank = lax.axis_index("ctx")
    fsdp_rank = lax.axis_index("fsdp")
    core = ctx_rank % 2
    tokens = block_input.shape[1]
    model = block_input.shape[2]
    head_size = query_gain.shape[0]
    kv_heads = key_weight.shape[1] // head_size
    slots = block_order.shape[0]
    length = tokens * ctx_size
    half_rows = length // slots
    per_block = tokens // half_rows
    weight_rows = query_weight.shape[0]
    hidden_slice = gate_weight.shape[1] // ctx_size
    splits = ctx_size // 2 // kv_heads
    split_rank = (ctx_rank // 2) % splits
    sorted_all = splits == 1
    score_scale = 1.0 / math.sqrt(head_size)
    ring = Ring(ctx_size)
    always = jnp.min(block_order) >= 0

    def fenced(work, *values):
        shapes = jax.eval_shape(work, *values)
        blank = lambda *_: jax.tree.map(lambda leaf: jnp.zeros(leaf.shape, leaf.dtype), shapes)
        return lax.cond(always, work, blank, *values)

    def block_rows(field, index):
        return field[index * tokens : (index + 1) * tokens]

    def by_head(weight):
        split = jnp.transpose(weight.reshape(weight_rows, kv_heads, -1, head_size), (1, 2, 0, 3))
        return jnp.broadcast_to(split[:, None], (kv_heads, splits) + split.shape[1:]).reshape(
            -1, weight_rows, head_size
        )

    key_value = jnp.stack(
        [key_weight.reshape(weight_rows, kv_heads, head_size),
         value_weight.reshape(weight_rows, kv_heads, head_size)],
        axis=2,
    ).reshape(weight_rows, -1)
    head_block = jnp.concatenate(
        [by_head(query_weight), by_head(output_weight), by_head(key_value)], axis=2
    )
    head_received = spread(head_block)
    head_mine = to_columns(head_received, swap_rows(head_received), fsdp_rank)
    head_other = ring.swap(head_mine)

    def column(field, index):
        return field[:, index * head_size : (index + 1) * head_size]

    def key_first(mine, other):
        return jnp.where(core == 0, mine, other), jnp.where(core == 0, other, mine)

    key_columns, value_columns = key_first(column(head_mine, 2), column(head_other, 2))
    head_weight = jnp.concatenate(
        [column(head_mine, 0), key_columns, value_columns, column(head_other, 0)], axis=1
    )
    output_part = jnp.concatenate([column(head_mine, 1), column(head_other, 1)], axis=1)

    last_hop = 2 * ring.reach - 2
    angles = {}

    def make_angles(blocks):
        angles["tables"] = rope_tables(
            after(jnp.arange(length, dtype=jnp.int32), blocks[2]), head_size
        )
        return angles["tables"]

    input_blocks = ring.gather(block_input[0], {last_hop - 1: make_angles})
    member_table = np.array(
        [ring.members(rank) + ring.members(rank ^ 1) for rank in range(ctx_size)], np.int32
    )
    ranks = jnp.arange(ctx_size, dtype=jnp.int32)
    listed = jnp.sum(jnp.where(ranks[:, None] == ctx_rank, member_table, 0), axis=0)
    slot_index = jnp.arange(slots, dtype=jnp.int32)
    local_slot = (
        listed[:, None] * per_block + jnp.arange(per_block, dtype=jnp.int32)[None, :]
    ).reshape(-1)
    local_pos = jnp.sum(
        jnp.where(local_slot[:, None] == slot_index[None, :], block_order[None, :], 0), axis=1
    )
    cosine, sine = angles["tables"]
    if sorted_all:
        tables = (local_pos, slot_index, slot_index)
    else:
        local_of_pos = jnp.sum(
            jnp.where(local_pos[None, :] == slot_index[:, None], slot_index[None, :], 0), axis=1
        )
        compact = jnp.arange(slots // splits, dtype=jnp.int32)
        owner = (compact // per_block) * splits + split_rank
        own_pos = jnp.sort(jnp.take(block_order, owner * per_block + compact % per_block))
        tables = (local_pos, jnp.take(local_of_pos, own_pos), own_pos)
    query_row, key_row = query_gain[None, :], key_gain[None, :]

    input_blocks[4] = after(input_blocks[4], head_received)

    def by_slice(weight):
        return jnp.transpose(weight.reshape(weight_rows, ctx_size, hidden_slice), (1, 0, 2))

    gate, up, down = after((gate_weight, up_weight, down_weight), input_blocks[3])
    mlp_block = jnp.concatenate([by_slice(gate), by_slice(up), by_slice(down)], axis=2)
    normed_attn, projected = project(input_blocks, attn_gain, head_weight)
    projected_given = ring.swap(
        jnp.concatenate(
            [projected[:, 3 * head_size :], projected[:, head_size : 3 * head_size]], axis=1
        )
    )
    raw = (projected, projected_given)
    attn_a, attn_b, lse, *saved = attend(
        tables, raw, cosine, sine, query_row, key_row, half_rows, sorted_all, score_scale
    )
    mlp_received = spread(after(mlp_block, input_blocks[-1], input_blocks[-2]))
    mlp_received = after(mlp_received, attn_a)
    mlp_partner = swap_rows(mlp_received)
    attn_pair = jnp.concatenate([attn_a, ring.swap(attn_b)], axis=1)

    inputs32 = block_input[0].astype(f32)
    attn_terms = dot_nt(attn_pair, output_part).astype(bf16)
    attn_out = fenced(
        lambda terms: ring.scatter_sum(lambda i: block_rows(terms, i))[0], attn_terms
    )
    hidden_one = inputs32 + attn_out
    scale_mlp = inv_root(hidden_one)
    normed_mlp = (hidden_one * scale_mlp * mlp_gain).astype(bf16)
    mlp_mine = to_columns(mlp_received, mlp_partner, fsdp_rank)
    mlp_other = ring.swap(mlp_mine)
    pair = 2 * hidden_slice
    gate_up = jnp.concatenate([mlp_mine[:, :pair], mlp_other[:, :pair]], axis=1)
    down_part = jnp.concatenate([mlp_mine[:, pair:], mlp_other[:, pair:]], axis=1)

    normed_blocks = ring.gather(normed_mlp)
    normed_all = jnp.concatenate(normed_blocks, axis=0)
    gate_up, down_part = lax.optimization_barrier((gate_up, down_part))
    middle = ring.reach * tokens
    hidden_parts = [dot_nn(normed_all[:middle], gate_up), dot_nn(normed_all[middle:], gate_up)]
    cot_blocks = ring.gather(
        after(cotangent[0], normed_blocks[-2]),
        {
            last_hop - 4: lambda _: gate_up,
            last_hop - 3: lambda _: hidden_parts[0],
            last_hop - 1: lambda _: hidden_parts[1],
        },
    )
    hidden_all = jnp.concatenate(hidden_parts, axis=0)
    cot_all = jnp.concatenate(cot_blocks, axis=0)
    act_grad_all = dot_nn(cot_all, down_part)
    activated_list, back_list = [], []
    for member in range(2):
        gate_pre = hidden_all[:, 2 * member * hidden_slice : (2 * member + 1) * hidden_slice]
        up_pre = hidden_all[:, (2 * member + 1) * hidden_slice : (2 * member + 2) * hidden_slice]
        act_grad = act_grad_all[:, member * hidden_slice : (member + 1) * hidden_slice]
        sigma = jax.nn.sigmoid(gate_pre)
        activated_list.append((gate_pre * sigma * up_pre).astype(bf16))
        back_list.append(
            (act_grad * up_pre * sigma * (1.0 + gate_pre * (1.0 - sigma))).astype(bf16)
        )
        back_list.append((act_grad * gate_pre * sigma).astype(bf16))
    activated_all = jnp.concatenate(activated_list, axis=1)
    back_all = jnp.concatenate(back_list, axis=1)
    far = (2 * ring.reach - 3) * tokens
    far_terms = dot_nt(back_all[far:], gate_up).astype(bf16)
    near_blocks = far // tokens
    add = lambda left, right: (left.astype(f32) + right.astype(f32)).astype(bf16)

    def feed_forward_grads(far_terms, back_all, activated_all, normed_all, cot_all, gate_up):
        near_terms = dot_nt(back_all[:far], gate_up).astype(bf16)
        ready = {}

        def piece(left, right, mark):
            grad = dot_tn(left, after(right, mark)).astype(bf16)
            return with_layout_constraint(grad, Layout((0, 1)))

        def down_away(marks):
            ready["down_give"] = piece(cot_all, activated_all[:, hidden_slice:], marks[0])
            return ready["down_give"]

        def gate_up_away(marks):
            ready["gate_up_give"] = piece(normed_all, back_all[:, pair:], marks[1])
            return ready["gate_up_give"]

        def down_here(marks):
            ready["down"] = piece(cot_all, activated_all[:, :hidden_slice], marks[2])
            return ready["down"]

        def gate_up_here(marks):
            ready["gate_up"] = piece(normed_all, back_all[:, :pair], marks[3])
            return ready["gate_up"]

        summed, marks = ring.scatter_sum(
            lambda i: block_rows(near_terms, i)
            if i < near_blocks
            else block_rows(far_terms, i - near_blocks),
            {2: down_away, 3: gate_up_away, 4: down_here, 5: gate_up_here},
            first_twice=True,
        )
        ready["down"] = add(ready["down"], ring.swap(ready["down_give"]))
        ready["gate_up"] = add(ready["gate_up"], ring.swap(ready["gate_up_give"]))
        near_late, far_late = after((near_terms, far_terms), marks[4])
        gain_part = jnp.sum(
            near_late.astype(f32) * normed_all[:far].astype(f32), axis=0
        ) + jnp.sum(far_late.astype(f32) * normed_all[far:].astype(f32), axis=0)
        down_own, down_away, _ = halves(ready["down"], None, fsdp_rank, ctx_size)
        gate_up_own, gate_up_away, _ = halves(ready["gate_up"], None, fsdp_rank, ctx_size)
        return summed, gain_part / mlp_gain, down_own, down_away, gate_up_own, gate_up_away

    normed_mlp_grad, mlp_gain_part, down_own, down_away, gate_up_own, gate_up_away = fenced(
        feed_forward_grads, far_terms, back_all, activated_all, normed_all, cot_all, gate_up
    )
    grad32 = cotangent[0].astype(f32)
    hidden_grad = grad32 + norm_back(hidden_one, scale_mlp, mlp_gain, normed_mlp_grad)
    hidden_grad_bf = hidden_grad.astype(bf16)
    down_other, gate_up_other = swap_rows(down_away), swap_rows(gate_up_away)

    grad_all = fenced(lambda block: jnp.concatenate(ring.gather(block), axis=0), hidden_grad_bf)
    attn_grad_pair = dot_nn(grad_all, output_part).astype(bf16)
    attn_grad = (attn_grad_pair[:, :head_size], ring.swap(attn_grad_pair[:, head_size:]))
    mlp_sent = jnp.concatenate(
        [join(down_own, down_other, None), join(gate_up_own, gate_up_other, None)], axis=2
    )
    attn_grad, mlp_sent = lax.optimization_barrier((attn_grad, mlp_sent))

    mlp_rows = spread(mlp_sent)

    def attention_back(attn_grad, attn_a, attn_b, projected, given):
        first_a, first_b, query_gain_part, key_gain_part = attend_back(
            tables, (projected, given), cosine, sine, query_row, key_row, saved, (attn_a, attn_b),
            attn_grad, lse, half_rows, sorted_all, score_scale,
        )
        given_grads = ring.swap(first_b)
        half_grads = jnp.concatenate(
            [
                first_a[:, :head_size],
                add(first_a[:, head_size:], given_grads[:, head_size:]),
                given_grads[:, :head_size],
            ],
            axis=1,
        )
        input_terms = dot_nt(half_grads, head_weight).astype(bf16)
        return half_grads, input_terms, query_gain_part[0], key_gain_part[0]

    half_grads, input_terms, query_gain_part, key_gain_part = fenced(
        attention_back, attn_grad, attn_a, attn_b, *raw
    )

    def attention_grads(input_terms, half_grads, grad_all, normed_attn, attn_pair):
        ready = {}

        def weight_grads(marks):
            late_grads, late_attn = after((half_grads, attn_pair), marks[0])
            head_grad = dot_tn(normed_attn, late_grads).astype(bf16)
            output_grad = dot_tn(grad_all, late_attn).astype(bf16)
            kv_keep, kv_give = key_first(column(head_grad, 1), column(head_grad, 2))
            keep = jnp.concatenate([column(head_grad, 0), column(output_grad, 0), kv_keep], axis=1)
            give = jnp.concatenate([column(head_grad, 3), column(output_grad, 1), kv_give], axis=1)
            ready["gain"] = (
                jnp.sum(after(input_terms, marks[1]).astype(f32) * normed_attn.astype(f32), axis=0)
                / attn_gain
            )
            ready["grads"] = add(keep, ring.swap(give))
            return ready["grads"], ready["gain"]

        summed, _ = ring.scatter_sum(
            lambda i: block_rows(input_terms, i), {last_hop: weight_grads}
        )
        return summed, ready["grads"], ready["gain"]

    normed_attn_grad, attn_grads, attn_gain_part = fenced(
        attention_grads, input_terms, half_grads, grad_all, normed_attn, attn_pair
    )
    gains = jnp.concatenate([attn_gain_part, query_gain_part, key_gain_part, mlp_gain_part])

    def out_and_home(activated_all, down_part, attn_grads, gains, mlp_rows, summed_grad, hidden_grad, inputs32):
        own, away, lines = halves(attn_grads, gains, fsdp_rank, ctx_size)
        out_terms = dot_nt(activated_all, down_part).astype(bf16)
        ready = {}

        def other_rows(_):
            ready["other"] = swap_rows(away)
            return ready["other"]

        def rows_home(_):
            ready["rows"] = spread(join(own, ready["other"], lines))
            return ready["rows"]

        def unpack(marks):
            rows = after(mlp_rows, marks[1])
            ready["mlp"] = tuple(
                side_by_side(rows[:, :, i * hidden_slice : (i + 1) * hidden_slice]).astype(f32)
                for i in range(3)
            )
            return ready["mlp"]

        def finish(marks):
            ready["input"] = hidden_grad + norm_back(
                inputs32, inv_root(inputs32), attn_gain, after(summed_grad, marks[0])
            )
            return ready["input"]

        summed, _ = ring.scatter_sum(
            lambda i: block_rows(out_terms, i),
            {2: finish, last_hop - 2: other_rows, last_hop - 1: unpack, last_hop: rows_home},
        )
        return summed, ready["rows"], ready["input"], ready["mlp"]

    attn_grads, mlp_rows = lax.optimization_barrier((attn_grads, mlp_rows))
    mlp_out, attn_home, input_grad, mlp_grads = fenced(
        out_and_home, activated_all, down_part, attn_grads, gains, mlp_rows, normed_attn_grad,
        hidden_grad, inputs32,
    )
    block_out = (hidden_one + mlp_out).astype(bf16)
    attn_rows, attn_extra = apart(
        attn_home,
        weight_rows,
        3 * head_size,
        2 * model + 2 * head_size,
    )

    def home(index):
        part = attn_rows[:, :, index * head_size : (index + 1) * head_size].astype(f32)
        return jnp.sum(part.reshape(kv_heads, splits, 2, weight_rows, head_size), axis=1)

    key_value_rows = home(2)
    flat = lambda part: side_by_side(part.reshape(-1, weight_rows, head_size))

    down_rows, gate_rows, up_rows = mlp_grads

    return (
        block_out[None],
        input_grad[None],
        flat(home(0)),
        flat(key_value_rows[:, 0]),
        flat(key_value_rows[:, 1]),
        flat(home(1)),
        gate_rows,
        up_rows,
        down_rows,
        attn_extra[:model],
        attn_extra[model + 2 * head_size :],
        attn_extra[model : model + head_size],
        attn_extra[model + head_size : model + 2 * head_size],
    )


def solution(mesh):
    in_specs = (
        P("fsdp", "ctx", None),
        P(("ctx", "fsdp"), None),
        P(("ctx", "fsdp"), None),
        P(("ctx", "fsdp"), None),
        P(("ctx", "fsdp"), None),
        P(("ctx", "fsdp"), None),
        P(("ctx", "fsdp"), None),
        P(("ctx", "fsdp"), None),
        P(),
        P(),
        P(),
        P(),
        P(),
        P("fsdp", "ctx", None),
    )
    out_specs = (
        P("fsdp", "ctx", None),
        P("fsdp", "ctx", None),
        P(("ctx", "fsdp"), None),
        P(("ctx", "fsdp"), None),
        P(("ctx", "fsdp"), None),
        P(("ctx", "fsdp"), None),
        P(("ctx", "fsdp"), None),
        P(("ctx", "fsdp"), None),
        P(("ctx", "fsdp"), None),
        P(),
        P(),
        P(),
        P(),
    )
    return jax.shard_map(shards, mesh=mesh, in_specs=in_specs, out_specs=out_specs, check_vma=False)
```

```python
import functools
import math

import jax
import jax.numpy as jnp
import numpy as np
from jax import lax
from jax.experimental import pallas as pl
from jax.experimental.layout import Layout, with_layout_constraint
from jax.experimental.pallas import tpu as pltpu
from jax.sharding import PartitionSpec as P

eps_model = 1e-06
rope_base = 1000000.0
f32 = jnp.float32
bf16 = jnp.bfloat16


def inv_root(field):
    return lax.rsqrt(jnp.mean(field * field, axis=-1, keepdims=True) + eps_model)


def norm_back(field, factor, gain, grad_in):
    weighted = gain * grad_in
    inner_mean = jnp.mean(weighted * field, axis=-1, keepdims=True)
    return factor * weighted - field * (factor * factor * factor) * inner_mean


def rope_tables(positions, head_size):
    half_size = head_size // 2
    exponent = jnp.arange(half_size, dtype=f32) * f32(2.0 / head_size)
    inverse = jnp.exp(-exponent * f32(math.log(rope_base)))
    angles = positions.astype(f32)[:, None] * inverse[None, :]
    cosine, sine = jnp.cos(angles), jnp.sin(angles)
    return jnp.concatenate([cosine, cosine], axis=1), jnp.concatenate([-sine, sine], axis=1)


def dot_nn(left, right):
    return lax.dot_general(left, right, (((1,), (0,)), ((), ())), preferred_element_type=f32)


def dot_nt(left, right):
    return lax.dot_general(left, right, (((1,), (1,)), ((), ())), preferred_element_type=f32)


def dot_tn(left, right):
    return lax.dot_general(left, right, (((0,), (0,)), ((), ())), preferred_element_type=f32)


def allowed_tile(key_first, query_tile, pos_table, tile_k, tile_q, rows, sorted_all):
    key_pos = key_first + lax.broadcasted_iota(jnp.int32, (tile_k, tile_q), 0)
    lane = lax.broadcasted_iota(jnp.int32, (1, tile_q), 1)
    if sorted_all:
        query_pos = query_tile * tile_q + lane
    else:
        per_tile = tile_q // rows
        query_pos = jnp.zeros((1, tile_q), jnp.int32)
        for piece in range(per_tile):
            first = pos_table[query_tile * per_tile + piece] * rows
            inside = (lane >= piece * rows) & (lane < (piece + 1) * rows)
            query_pos = jnp.where(inside, first + lane - piece * rows, query_pos)
    return key_pos <= query_pos


def tile_loop(query_tile, key_tiles, sorted_all, work):
    if sorted_all:
        for key_tile in range(query_tile):
            work(key_tile, False)
        work(query_tile, True)
    else:

        @pl.loop(0, key_tiles)
        def _(key_tile):
            work(key_tile, True)


def query_loop(query_tiles, sorted_all, work):
    if sorted_all:
        for query_tile in range(query_tiles):
            work(query_tile)
    else:

        @pl.loop(0, query_tiles)
        def _(query_tile):
            work(query_tile)


def block_loop(blocks, work):
    def step(index, carry):
        work(index)
        return carry

    lax.fori_loop(0, blocks, step, 0, unroll=4)


def rows_at(index, rows):
    return pl.ds(pl.multiple_of(index * rows, rows), rows)


def each_key(key_pos, blocks, rows, work):
    for part in range(2):
        block_loop(
            blocks // 2,
            lambda index: work(
                part, rows_at(index, rows), rows_at(key_pos[part * (blocks // 2) + index], rows)
            ),
        )


def each_query(key_pos, query_table, pos_table, blocks, count, rows, sorted_all, work):
    if sorted_all:
        each_key(key_pos, blocks, rows, lambda part, here, place: work(part, here, place, place))
        return

    @pl.loop(0, count)
    def _(index):
        local = query_table[index]
        place, at_pos = rows_at(index, rows), rows_at(pos_table[index], rows)
        for part in range(2):
            inner = local - part * (blocks // 2)

            @pl.when((inner >= 0) & (inner < blocks // 2))
            def _():
                work(part, rows_at(inner, rows), place, at_pos)


def turn(field):
    return pltpu.roll(field, field.shape[-1] // 2, 1)


def attend_kernel(
    geometry, key_pos, query_table, pos_table, raw_a, raw_b, cos_ref, sin_ref, q_gain, k_gain,
    out_a, out_b, lse_ref, q_sorted, k_sorted, v_sorted, v_turned, acc, total, out_sorted,
):
    rows, tile, sorted_all, scale = geometry
    head = q_gain.shape[1]
    keys, queries = k_sorted.shape[0], q_sorted.shape[0]
    key_tiles, query_tiles = keys // tile, queries // tile
    raw, out = (raw_a, raw_b), (out_a, out_b)
    walk = (key_pos, query_table, pos_table, keys // rows, queries // rows, rows, sorted_all)

    def rope(field, gain, place):
        normed = field * inv_root(field) * gain[...]
        return (normed * cos_ref[place, :] + turn(normed) * sin_ref[place, :]).astype(bf16)

    def take_keys(part, here, place):
        k_sorted[place, :] = rope(raw[part][here, head : 2 * head], k_gain, place)
        v_sorted[place, :] = raw[part][here, 2 * head : 3 * head].astype(bf16)

    def take_queries(part, here, place, at_pos):
        q_sorted[place, :] = rope(raw[part][here, :head], q_gain, at_pos)

    each_key(key_pos, keys // rows, rows, take_keys)
    each_query(*walk, take_queries)
    for key_tile in range(key_tiles):
        piece = v_sorted[key_tile * tile : (key_tile + 1) * tile, :]
        v_turned[:, key_tile * tile : (key_tile + 1) * tile] = piece.astype(f32).T.astype(bf16)
    if not sorted_all:
        out_a[...] = jnp.zeros_like(out_a)
        out_b[...] = jnp.zeros_like(out_b)

    def query_work(query_tile):
        q_start = pl.multiple_of(query_tile * tile, tile)
        q_tile = q_sorted[pl.ds(q_start, tile), :]
        acc[...] = jnp.zeros_like(acc)
        total[...] = jnp.zeros_like(total)

        def work(key_tile, masked):
            k_start = pl.multiple_of(key_tile * tile, tile)
            scores = dot_nt(k_sorted[pl.ds(k_start, tile), :], q_tile)
            probs = jnp.exp(scores * scale)
            if masked:
                keep = allowed_tile(k_start, query_tile, pos_table, tile, tile, rows, sorted_all)
                probs = jnp.where(keep, probs, 0.0)
            total[...] += jnp.sum(probs, axis=0, keepdims=True)
            acc[...] += dot_nn(v_turned[:, pl.ds(k_start, tile)], probs.astype(bf16))

        tile_loop(query_tile, key_tiles, sorted_all, work)
        lse_ref[:, pl.ds(q_start, tile)] = jnp.log(total[...])
        out_sorted[pl.ds(q_start, tile), :] = (acc[...] / total[...]).T.astype(bf16)

    query_loop(query_tiles, sorted_all, query_work)

    def put(part, here, place, at_pos):
        out[part][here, :] = out_sorted[place, :]

    each_query(*walk, put)


def whole_spec(shape):
    return pl.BlockSpec(memory_space=pltpu.VMEM)


def attend(tables, raw, cosine, sine, query_gain, key_gain, rows, sorted_all, scale):
    head = query_gain.shape[1]
    keys = cosine.shape[0]
    queries = tables[1].shape[0] * rows
    tile = math.gcd(math.gcd(queries, keys), 512)
    narrow, row, part = whole_spec((keys, head)), whole_spec((1, head)), whole_spec((keys // 2, head))
    return pl.pallas_call(
        functools.partial(attend_kernel, (rows, tile, sorted_all, scale)),
        out_shape=(
            jax.ShapeDtypeStruct((keys // 2, head), bf16),
            jax.ShapeDtypeStruct((keys // 2, head), bf16),
            jax.ShapeDtypeStruct((1, queries), f32),
            jax.ShapeDtypeStruct((queries, head), bf16),
            jax.ShapeDtypeStruct((keys, head), bf16),
            jax.ShapeDtypeStruct((keys, head), bf16),
        ),
        grid_spec=pltpu.PrefetchScalarGridSpec(
            num_scalar_prefetch=3,
            grid=(1,),
            in_specs=[whole_spec(raw[0].shape), whole_spec(raw[1].shape), narrow, narrow, row, row],
            out_specs=(part, part, whole_spec((1, queries)), whole_spec((queries, head)), narrow, narrow),
            scratch_shapes=[
                pltpu.VMEM((head, keys), bf16),
                pltpu.VMEM((head, tile), f32),
                pltpu.VMEM((1, tile), f32),
                pltpu.VMEM((queries, head), bf16),
            ],
        ),
        compiler_params=pltpu.CompilerParams(vmem_limit_bytes=(12 << 20) + 5120 * keys),
        cost_estimate=pl.CostEstimate(
            flops=4 * queries * keys * head, bytes_accessed=28 * keys * head, transcendentals=queries * keys
        ),
        name="attend",
    )(*tables, *raw, cosine, sine, query_gain, key_gain)


def attend_back_kernel(
    geometry, key_pos, query_table, pos_table, raw_a, raw_b, cos_ref, sin_ref, q_gain, k_gain,
    q_sorted, k_sorted, v_sorted, o_a, o_b, do_a, do_b, lse_ref,
    grads_a, grads_b, q_part, k_part,
    do_sorted, o_sorted, k_turned, delta, dq_turned, dq_sorted, dk_sorted, dv_sorted,
):
    rows, tile, sorted_all, scale = geometry
    head = q_gain.shape[1]
    keys, queries = k_sorted.shape[0], q_sorted.shape[0]
    key_tiles, query_tiles = keys // tile, queries // tile
    raw, o_ref, do_ref, grads = (raw_a, raw_b), (o_a, o_b), (do_a, do_b), (grads_a, grads_b)
    walk = (key_pos, query_table, pos_table, keys // rows, queries // rows, rows, sorted_all)

    def take(part, here, place, at_pos):
        do_sorted[place, :] = do_ref[part][here, :]
        o_sorted[place, :] = o_ref[part][here, :]

    each_query(*walk, take)
    for key_tile in range(key_tiles):
        piece = k_sorted[key_tile * tile : (key_tile + 1) * tile, :]
        k_turned[:, key_tile * tile : (key_tile + 1) * tile] = piece.astype(f32).T.astype(bf16)
    dk_sorted[...] = jnp.zeros_like(dk_sorted)
    dv_sorted[...] = jnp.zeros_like(dv_sorted)
    if not sorted_all:
        for part in range(2):
            grads[part][:, :head] = jnp.zeros((keys // 2, head), bf16)

    def query_work(query_tile):
        q_start = pl.multiple_of(query_tile * tile, tile)
        q_tile = q_sorted[pl.ds(q_start, tile), :]
        do_tile = do_sorted[pl.ds(q_start, tile), :]
        product = do_tile.astype(f32) * o_sorted[pl.ds(q_start, tile), :].astype(f32)
        delta[...] = jnp.sum(product.T, axis=0, keepdims=True)
        dq_turned[...] = jnp.zeros_like(dq_turned)

        def work(key_tile, masked):
            k_start = pl.multiple_of(key_tile * tile, tile)
            here = pl.ds(k_start, tile)
            scores = dot_nt(k_sorted[here, :], q_tile)
            probs = jnp.exp(scores * scale - lse_ref[:, pl.ds(q_start, tile)])
            if masked:
                keep = allowed_tile(k_start, query_tile, pos_table, tile, tile, rows, sorted_all)
                probs = jnp.where(keep, probs, 0.0)
            dv_sorted[here, :] += dot_nn(probs.astype(bf16), do_tile)
            d_probs = dot_nt(v_sorted[here, :], do_tile)
            d_scores = (probs * (d_probs - delta[...])).astype(bf16)
            dk_sorted[here, :] += dot_nn(d_scores, q_tile)
            dq_turned[...] += dot_nn(k_turned[:, here], d_scores)

        tile_loop(query_tile, key_tiles, sorted_all, work)
        dq_sorted[pl.ds(q_start, tile), :] = dq_turned[...].T

    query_loop(query_tiles, sorted_all, query_work)
    q_part[...] = jnp.zeros_like(q_part)
    k_part[...] = jnp.zeros_like(k_part)

    def through_norm(field, grad, gain, at_pos, gain_part):
        scaled = grad * scale
        normed_grad = scaled * cos_ref[at_pos, :] - turn(scaled) * sin_ref[at_pos, :]
        factor = inv_root(field)
        gain_part[...] += jnp.sum(normed_grad * field * factor, axis=0, keepdims=True)
        return norm_back(field, factor, gain[...], normed_grad).astype(bf16)

    def put_queries(part, here, place, at_pos):
        grads[part][here, :head] = through_norm(
            raw[part][here, :head], dq_sorted[place, :], q_gain, at_pos, q_part
        )

    def put_keys(part, here, place):
        grads[part][here, head : 2 * head] = through_norm(
            raw[part][here, head : 2 * head], dk_sorted[place, :], k_gain, place, k_part
        )
        grads[part][here, 2 * head :] = dv_sorted[place, :].astype(bf16)

    each_query(*walk, put_queries)
    each_key(key_pos, keys // rows, rows, put_keys)


def attend_back(tables, raw, cosine, sine, query_gain, key_gain, saved, out, d_out, lse, rows, sorted_all, scale):
    head = query_gain.shape[1]
    keys = cosine.shape[0]
    queries = tables[1].shape[0] * rows
    tile = math.gcd(math.gcd(queries, keys), 512)
    narrow, row, part = whole_spec((keys, head)), whole_spec((1, head)), whole_spec((keys // 2, head))
    q_spec, wide = whole_spec((queries, head)), whole_spec((keys // 2, 3 * head))
    return pl.pallas_call(
        functools.partial(attend_back_kernel, (rows, tile, sorted_all, scale)),
        out_shape=(
            jax.ShapeDtypeStruct((keys // 2, 3 * head), bf16),
            jax.ShapeDtypeStruct((keys // 2, 3 * head), bf16),
            jax.ShapeDtypeStruct((1, head), f32),
            jax.ShapeDtypeStruct((1, head), f32),
        ),
        grid_spec=pltpu.PrefetchScalarGridSpec(
            num_scalar_prefetch=3,
            grid=(1,),
            in_specs=[
                whole_spec(raw[0].shape), whole_spec(raw[1].shape), narrow, narrow, row, row,
                q_spec, narrow, narrow, part, part, part, part, whole_spec((1, queries)),
            ],
            out_specs=(wide, wide, row, row),
            scratch_shapes=[
                pltpu.VMEM((queries, head), bf16),
                pltpu.VMEM((queries, head), bf16),
                pltpu.VMEM((head, keys), bf16),
                pltpu.VMEM((1, tile), f32),
                pltpu.VMEM((head, tile), f32),
                pltpu.VMEM((queries, head), f32),
                pltpu.VMEM((keys, head), f32),
                pltpu.VMEM((keys, head), f32),
            ],
        ),
        compiler_params=pltpu.CompilerParams(
            vmem_limit_bytes=min(60 << 20, (16 << 20) + 7168 * keys)
        ),
        cost_estimate=pl.CostEstimate(
            flops=10 * queries * keys * head, bytes_accessed=40 * keys * head, transcendentals=queries * keys
        ),
        name="attend_back",
    )(*tables, *raw, cosine, sine, query_gain, key_gain, *saved, *out, *d_out, lse)


def project_kernel(weight_ref, gain_ref, *refs):
    count = len(refs) - 2
    normed_ref, out_ref = refs[count:]
    rows = refs[0].shape[0]
    for index in range(count):
        wide = refs[index][...].astype(f32)
        normed = (wide * inv_root(wide) * gain_ref[...]).astype(bf16)
        place = pl.ds(index * rows, rows)
        normed_ref[place, :] = normed
        out_ref[place, :] = dot_nn(normed, weight_ref[...])


def project(blocks, gain, weight):
    rows, width = blocks[0].shape
    total, columns = rows * len(blocks), weight.shape[1]
    return pl.pallas_call(
        project_kernel,
        out_shape=(
            jax.ShapeDtypeStruct((total, width), bf16),
            jax.ShapeDtypeStruct((total, columns), f32),
        ),
        grid=(1,),
        in_specs=[whole_spec(weight.shape), whole_spec((1, width))]
        + [whole_spec((rows, width))] * len(blocks),
        out_specs=(whole_spec((total, width)), whole_spec((total, columns))),
        compiler_params=pltpu.CompilerParams(
            vmem_limit_bytes=(12 << 20) + 12 * total * width
        ),
        cost_estimate=pl.CostEstimate(
            flops=2 * total * width * columns, bytes_accessed=4 * total * width, transcendentals=total
        ),
        name="project",
    )(weight, gain[None, :], *blocks)


class Ring:
    def __init__(self, size):
        self.chips = size // 2
        self.reach = self.chips // 2
        self.order = list(range(0, self.chips, 2)) + list(range(self.chips - 1, 0, -2))
        self.swap_pairs = [(i, i ^ 1) for i in range(size)]
        self.out_pairs = []
        for place, chip in enumerate(self.order):
            after_it = self.order[(place + 1) % self.chips]
            self.out_pairs.append((2 * chip, 2 * after_it))
            self.out_pairs.append((2 * after_it + 1, 2 * chip + 1))
        self.home_pairs = [(target, source) for source, target in self.out_pairs]

    def swap(self, field):
        return lax.ppermute(field, "ctx", self.swap_pairs)

    def out(self, field):
        return lax.ppermute(field, "ctx", self.out_pairs)

    def home(self, field):
        return lax.ppermute(field, "ctx", self.home_pairs)

    def members(self, rank):
        chip, core = rank // 2, rank % 2
        place = self.order.index(chip)
        blocks = [rank]
        for step in range(1, self.reach + 1):
            near = self.order[(place + (2 * core - 1) * step) % self.chips]
            blocks.append(2 * near + core)
            if step < self.reach:
                blocks.append(2 * near + 1 - core)
        return blocks

    def gather(self, block, hooks=None):
        hooks = hooks or {}
        streams = [block, self.swap(block)]
        blocks = [block]
        for hop in range(2 * self.reach - 1):
            held = streams[hop % 2]
            if hop >= 3:
                held = after(held, blocks[hop - 2])
            if hop in hooks:
                held = after(held, hooks[hop](blocks))
            streams[hop % 2] = self.out(held)
            blocks.append(streams[hop % 2])
        return blocks

    def scatter_hops(self, term, streams, hops, needs=None, first_twice=False):
        needs = needs or {}
        order = list(range(2 * self.reach - 1, 0, -1))
        if first_twice:
            for place in range(1, len(order), 2):
                order[place : place + 2] = reversed(order[place : place + 2])
        streams, marks, total = list(streams), [], None
        for hop in hops:
            index = order[hop]
            stream, held = 1 - index % 2, streams[1 - index % 2]
            if held is None:
                total = term(index)
            else:
                held = held if total is None else after(held, total)
                total = (term(index).astype(f32) + held.astype(f32)).astype(bf16)
            if hop in needs:
                total = after(total, needs[hop](marks))
            streams[stream] = self.home(total)
            marks.append(streams[stream])
        return streams, marks

    def scatter_end(self, term, streams):
        first, second = streams
        return first.astype(f32) + term(0).astype(f32) + self.swap(second).astype(f32)

    def scatter_sum(self, term, needs=None, first_twice=False):
        streams, marks = self.scatter_hops(
            term, [None, None], range(2 * self.reach - 1), needs, first_twice
        )
        return self.scatter_end(term, streams), marks


def after(value, *events):
    return lax.optimization_barrier((value, events))[0]


def spread(rows_block):
    return lax.all_to_all(rows_block, "ctx", split_axis=0, concat_axis=0, tiled=False)


def swap_rows(field):
    return lax.ppermute(field, "fsdp", [(0, 1), (1, 0)])


def to_columns(received, partner, fsdp_rank):
    first = jnp.where(fsdp_rank == 0, received, partner)
    second = jnp.where(fsdp_rank == 0, partner, received)
    both = jnp.stack([first, second], axis=1)
    return both.reshape(-1, received.shape[-1])


def halves(grads, extra, fsdp_rank, ctx_size):
    width = grads.shape[1]
    split = grads.reshape(ctx_size, 2, -1, width)
    keep = jnp.where(fsdp_rank == 0, split[:, 0], split[:, 1])
    give = jnp.where(fsdp_rank == 0, split[:, 1], split[:, 0])
    if extra is None:
        return keep, give, None
    count = extra.shape[0]
    lines = -(-count // width)
    lines = -(-lines // 16) * 16
    extra_block = jnp.pad(extra, (0, lines * width - count)).reshape(lines, width).astype(bf16)
    return keep, jnp.concatenate([give.reshape(-1, width), extra_block], axis=0), extra_block


def join(keep, given, extra_block):
    if extra_block is None:
        return (keep.astype(f32) + given.astype(f32)).astype(bf16)
    ctx_size, rows, width = keep.shape
    body = given[: ctx_size * rows].reshape(keep.shape)
    total = (keep.astype(f32) + body.astype(f32)).astype(bf16)
    extras = (extra_block.astype(f32) + given[ctx_size * rows :].astype(f32)).astype(bf16)
    return jnp.concatenate(
        [total, jnp.broadcast_to(extras[None], (ctx_size,) + extras.shape)], axis=1
    )


def apart(received, rows, width, count):
    lines = received[:, rows:, :width].astype(f32)
    return received[:, :rows], jnp.sum(lines, axis=0).reshape(-1)[:count]


def side_by_side(pieces):
    count, rows, width = pieces.shape
    return jnp.transpose(pieces, (1, 0, 2)).reshape(rows, count * width)


def shards(
    block_input,
    query_weight,
    key_weight,
    value_weight,
    output_weight,
    gate_weight,
    up_weight,
    down_weight,
    attn_gain,
    mlp_gain,
    query_gain,
    key_gain,
    block_order,
    cotangent,
):
    ctx_size = lax.axis_size("ctx")
    ctx_rank = lax.axis_index("ctx")
    fsdp_rank = lax.axis_index("fsdp")
    core = ctx_rank % 2
    tokens = block_input.shape[1]
    model = block_input.shape[2]
    head_size = query_gain.shape[0]
    kv_heads = key_weight.shape[1] // head_size
    slots = block_order.shape[0]
    length = tokens * ctx_size
    half_rows = length // slots
    per_block = tokens // half_rows
    weight_rows = query_weight.shape[0]
    hidden_slice = gate_weight.shape[1] // ctx_size
    splits = ctx_size // 2 // kv_heads
    split_rank = (ctx_rank // 2) % splits
    sorted_all = splits == 1
    score_scale = 1.0 / math.sqrt(head_size)
    ring = Ring(ctx_size)
    always = jnp.min(block_order) >= 0

    def fenced(work, *values):
        shapes = jax.eval_shape(work, *values)
        blank = lambda *_: jax.tree.map(lambda leaf: jnp.zeros(leaf.shape, leaf.dtype), shapes)
        return lax.cond(always, work, blank, *values)

    def block_rows(field, index):
        return field[index * tokens : (index + 1) * tokens]

    def by_head(weight):
        split = jnp.transpose(weight.reshape(weight_rows, kv_heads, -1, head_size), (1, 2, 0, 3))
        return jnp.broadcast_to(split[:, None], (kv_heads, splits) + split.shape[1:]).reshape(
            -1, weight_rows, head_size
        )

    key_value = jnp.stack(
        [key_weight.reshape(weight_rows, kv_heads, head_size),
         value_weight.reshape(weight_rows, kv_heads, head_size)],
        axis=2,
    ).reshape(weight_rows, -1)
    head_block = jnp.concatenate(
        [by_head(query_weight), by_head(output_weight), by_head(key_value)], axis=2
    )
    head_received = spread(head_block)
    head_mine = to_columns(head_received, swap_rows(head_received), fsdp_rank)
    head_other = ring.swap(head_mine)

    def column(field, index):
        return field[:, index * head_size : (index + 1) * head_size]

    def key_first(mine, other):
        return jnp.where(core == 0, mine, other), jnp.where(core == 0, other, mine)

    key_columns, value_columns = key_first(column(head_mine, 2), column(head_other, 2))
    head_weight = jnp.concatenate(
        [column(head_mine, 0), key_columns, value_columns, column(head_other, 0)], axis=1
    )
    output_part = jnp.concatenate([column(head_mine, 1), column(head_other, 1)], axis=1)

    last_hop = 2 * ring.reach - 2
    angles = {}

    def make_angles(blocks):
        angles["tables"] = rope_tables(
            after(jnp.arange(length, dtype=jnp.int32), blocks[2]), head_size
        )
        return angles["tables"]

    input_blocks = ring.gather(block_input[0], {last_hop - 1: make_angles})
    member_table = np.array(
        [ring.members(rank) + ring.members(rank ^ 1) for rank in range(ctx_size)], np.int32
    )
    ranks = jnp.arange(ctx_size, dtype=jnp.int32)
    listed = jnp.sum(jnp.where(ranks[:, None] == ctx_rank, member_table, 0), axis=0)
    slot_index = jnp.arange(slots, dtype=jnp.int32)
    local_slot = (
        listed[:, None] * per_block + jnp.arange(per_block, dtype=jnp.int32)[None, :]
    ).reshape(-1)
    local_pos = jnp.sum(
        jnp.where(local_slot[:, None] == slot_index[None, :], block_order[None, :], 0), axis=1
    )
    cosine, sine = angles["tables"]
    if sorted_all:
        tables = (local_pos, slot_index, slot_index)
    else:
        local_of_pos = jnp.sum(
            jnp.where(local_pos[None, :] == slot_index[:, None], slot_index[None, :], 0), axis=1
        )
        compact = jnp.arange(slots // splits, dtype=jnp.int32)
        owner = (compact // per_block) * splits + split_rank
        own_pos = jnp.sort(jnp.take(block_order, owner * per_block + compact % per_block))
        tables = (local_pos, jnp.take(local_of_pos, own_pos), own_pos)
    query_row, key_row = query_gain[None, :], key_gain[None, :]

    input_blocks[4] = after(input_blocks[4], head_received)

    def by_slice(weight):
        return jnp.transpose(weight.reshape(weight_rows, ctx_size, hidden_slice), (1, 0, 2))

    gate, up, down = after((gate_weight, up_weight, down_weight), input_blocks[3])
    mlp_block = jnp.concatenate([by_slice(gate), by_slice(up), by_slice(down)], axis=2)
    normed_attn, projected = project(input_blocks, attn_gain, head_weight)
    projected_given = ring.swap(
        jnp.concatenate(
            [projected[:, 3 * head_size :], projected[:, head_size : 3 * head_size]], axis=1
        )
    )
    raw = (projected, projected_given)
    attn_a, attn_b, lse, *saved = attend(
        tables, raw, cosine, sine, query_row, key_row, half_rows, sorted_all, score_scale
    )
    mlp_received = spread(after(mlp_block, input_blocks[-1], input_blocks[-2]))
    mlp_received = after(mlp_received, attn_a)
    mlp_partner = swap_rows(mlp_received)
    attn_pair = jnp.concatenate([attn_a, ring.swap(attn_b)], axis=1)

    inputs32 = block_input[0].astype(f32)
    attn_terms = dot_nt(attn_pair, output_part).astype(bf16)
    attn_out = fenced(
        lambda terms: ring.scatter_sum(lambda i: block_rows(terms, i))[0], attn_terms
    )
    hidden_one = inputs32 + attn_out
    scale_mlp = inv_root(hidden_one)
    normed_mlp = (hidden_one * scale_mlp * mlp_gain).astype(bf16)
    mlp_mine = to_columns(mlp_received, mlp_partner, fsdp_rank)
    mlp_other = ring.swap(mlp_mine)
    pair = 2 * hidden_slice
    gate_up = jnp.concatenate([mlp_mine[:, :pair], mlp_other[:, :pair]], axis=1)
    down_part = jnp.concatenate([mlp_mine[:, pair:], mlp_other[:, pair:]], axis=1)

    normed_blocks = ring.gather(normed_mlp)
    normed_all = jnp.concatenate(normed_blocks, axis=0)
    gate_up, down_part = lax.optimization_barrier((gate_up, down_part))
    middle = ring.reach * tokens
    hidden_parts = [dot_nn(normed_all[:middle], gate_up), dot_nn(normed_all[middle:], gate_up)]
    cot_blocks = ring.gather(
        after(cotangent[0], normed_blocks[-2]),
        {
            last_hop - 4: lambda _: gate_up,
            last_hop - 3: lambda _: hidden_parts[0],
            last_hop - 1: lambda _: hidden_parts[1],
        },
    )
    hidden_all = jnp.concatenate(hidden_parts, axis=0)
    cot_all = jnp.concatenate(cot_blocks, axis=0)
    act_grad_all = dot_nn(cot_all, down_part)
    activated_list, back_list = [], []
    for member in range(2):
        gate_pre = hidden_all[:, 2 * member * hidden_slice : (2 * member + 1) * hidden_slice]
        up_pre = hidden_all[:, (2 * member + 1) * hidden_slice : (2 * member + 2) * hidden_slice]
        act_grad = act_grad_all[:, member * hidden_slice : (member + 1) * hidden_slice]
        sigma = jax.nn.sigmoid(gate_pre)
        activated_list.append((gate_pre * sigma * up_pre).astype(bf16))
        back_list.append(
            (act_grad * up_pre * sigma * (1.0 + gate_pre * (1.0 - sigma))).astype(bf16)
        )
        back_list.append((act_grad * gate_pre * sigma).astype(bf16))
    activated_all = jnp.concatenate(activated_list, axis=1)
    back_all = jnp.concatenate(back_list, axis=1)
    far = (2 * ring.reach - 3) * tokens
    far_terms = dot_nt(back_all[far:], gate_up).astype(bf16)
    near_blocks = far // tokens
    add = lambda left, right: (left.astype(f32) + right.astype(f32)).astype(bf16)

    def feed_forward_grads(far_terms, back_all, activated_all, normed_all, cot_all, gate_up):
        near_terms = dot_nt(back_all[:far], gate_up).astype(bf16)
        ready = {}

        def piece(left, right, mark):
            grad = dot_tn(left, after(right, mark)).astype(bf16)
            return with_layout_constraint(grad, Layout((0, 1)))

        def down_away(marks):
            ready["down_give"] = piece(cot_all, activated_all[:, hidden_slice:], marks[0])
            return ready["down_give"]

        def gate_up_away(marks):
            ready["gate_up_give"] = piece(normed_all, back_all[:, pair:], marks[1])
            return ready["gate_up_give"]

        def down_here(marks):
            ready["down"] = piece(cot_all, activated_all[:, :hidden_slice], marks[2])
            return ready["down"]

        def gate_up_here(marks):
            ready["gate_up"] = piece(normed_all, back_all[:, :pair], marks[3])
            return ready["gate_up"]

        summed, marks = ring.scatter_sum(
            lambda i: block_rows(near_terms, i)
            if i < near_blocks
            else block_rows(far_terms, i - near_blocks),
            {2: down_away, 3: gate_up_away, 4: down_here, 5: gate_up_here},
            first_twice=True,
        )
        ready["down"] = add(ready["down"], ring.swap(ready["down_give"]))
        ready["gate_up"] = add(ready["gate_up"], ring.swap(ready["gate_up_give"]))
        near_late, far_late = after((near_terms, far_terms), marks[4])
        gain_part = jnp.sum(
            near_late.astype(f32) * normed_all[:far].astype(f32), axis=0
        ) + jnp.sum(far_late.astype(f32) * normed_all[far:].astype(f32), axis=0)
        down_own, down_away, _ = halves(ready["down"], None, fsdp_rank, ctx_size)
        gate_up_own, gate_up_away, _ = halves(ready["gate_up"], None, fsdp_rank, ctx_size)
        return summed, gain_part / mlp_gain, down_own, down_away, gate_up_own, gate_up_away

    normed_mlp_grad, mlp_gain_part, down_own, down_away, gate_up_own, gate_up_away = fenced(
        feed_forward_grads, far_terms, back_all, activated_all, normed_all, cot_all, gate_up
    )
    grad32 = cotangent[0].astype(f32)
    hidden_grad = grad32 + norm_back(hidden_one, scale_mlp, mlp_gain, normed_mlp_grad)
    hidden_grad_bf = hidden_grad.astype(bf16)
    down_own, gate_up_own = lax.optimization_barrier((down_own, gate_up_own))
    down_other, gate_up_other = swap_rows(down_away), swap_rows(gate_up_away)


    def gather_grads(block, activated_all, down_part):
        ready = {}

        def output_terms(blocks):
            ready["out"] = dot_nt(after(activated_all, blocks[2]), down_part).astype(bf16)
            return ready["out"]

        blocks = ring.gather(block, {last_hop - 1: output_terms})
        return jnp.concatenate(blocks, axis=0), ready["out"]

    grad_all, out_terms = fenced(gather_grads, hidden_grad_bf, activated_all, down_part)
    attn_grad_pair = dot_nn(grad_all, output_part).astype(bf16)
    attn_grad = (attn_grad_pair[:, :head_size], ring.swap(attn_grad_pair[:, head_size:]))
    mlp_sent = jnp.concatenate(
        [join(down_own, down_other, None), join(gate_up_own, gate_up_other, None)], axis=2
    )
    attn_grad, mlp_sent = lax.optimization_barrier((attn_grad, mlp_sent))

    mlp_rows = spread(mlp_sent)

    def attention_back(attn_grad, attn_a, attn_b, projected, given):
        first_a, first_b, query_gain_part, key_gain_part = attend_back(
            tables, (projected, given), cosine, sine, query_row, key_row, saved, (attn_a, attn_b),
            attn_grad, lse, half_rows, sorted_all, score_scale,
        )
        given_grads = ring.swap(first_b)
        half_grads = jnp.concatenate(
            [
                first_a[:, :head_size],
                add(first_a[:, head_size:], given_grads[:, head_size:]),
                given_grads[:, :head_size],
            ],
            axis=1,
        )
        input_terms = dot_nt(half_grads, head_weight).astype(bf16)
        return half_grads, input_terms, query_gain_part[0], key_gain_part[0]

    half_grads, input_terms, query_gain_part, key_gain_part = fenced(
        attention_back, attn_grad, attn_a, attn_b, *raw
    )

    def attention_grads(input_terms, half_grads, grad_all, normed_attn, attn_pair):
        ready = {}

        def weight_grads(marks):
            late_grads, late_attn = after((half_grads, attn_pair), marks[0])
            head_grad = dot_tn(normed_attn, late_grads).astype(bf16)
            output_grad = dot_tn(grad_all, late_attn).astype(bf16)
            kv_keep, kv_give = key_first(column(head_grad, 1), column(head_grad, 2))
            keep = jnp.concatenate([column(head_grad, 0), column(output_grad, 0), kv_keep], axis=1)
            give = jnp.concatenate([column(head_grad, 3), column(output_grad, 1), kv_give], axis=1)
            ready["gain"] = (
                jnp.sum(after(input_terms, marks[1]).astype(f32) * normed_attn.astype(f32), axis=0)
                / attn_gain
            )
            ready["grads"] = add(keep, ring.swap(give))
            return ready["grads"], ready["gain"]

        summed, _ = ring.scatter_sum(
            lambda i: block_rows(input_terms, i), {last_hop: weight_grads}
        )
        return summed, ready["grads"], ready["gain"]

    normed_attn_grad, attn_grads, attn_gain_part = fenced(
        attention_grads, input_terms, half_grads, grad_all, normed_attn, attn_pair
    )
    gains = jnp.concatenate([attn_gain_part, query_gain_part, key_gain_part, mlp_gain_part])

    def out_and_home(out_terms, attn_grads, gains, mlp_rows, summed_grad, hidden_grad, inputs32):
        own, away, lines = halves(attn_grads, gains, fsdp_rank, ctx_size)
        ready = {}

        def other_rows(_):
            ready["other"] = swap_rows(away)
            return ready["other"]

        def rows_home(_):
            sent = join(own, ready["other"], lines)
            ready["rows"] = spread(sent)
            return sent

        def unpack(marks):
            rows = after(mlp_rows, marks[4])
            ready["mlp"] = tuple(
                side_by_side(rows[:, :, i * hidden_slice : (i + 1) * hidden_slice]).astype(f32)
                for i in range(3)
            )
            return ready["mlp"]

        def finish(marks):
            ready["input"] = hidden_grad + norm_back(
                inputs32, inv_root(inputs32), attn_gain, after(summed_grad, marks[3])
            )
            return ready["input"]

        summed, marks = ring.scatter_sum(
            lambda i: block_rows(out_terms, i),
            {4: other_rows, 5: rows_home},
        )
        finish(marks)
        unpack(marks)
        return summed, ready["rows"], ready["input"], ready["mlp"]

    attn_grads, mlp_rows = lax.optimization_barrier((attn_grads, mlp_rows))
    mlp_out, attn_home, input_grad, mlp_grads = fenced(
        out_and_home, out_terms, attn_grads, gains, mlp_rows, normed_attn_grad,
        hidden_grad, inputs32,
    )
    block_out = (hidden_one + mlp_out).astype(bf16)
    attn_rows, attn_extra = apart(
        attn_home,
        weight_rows,
        3 * head_size,
        2 * model + 2 * head_size,
    )

    def home(index):
        part = attn_rows[:, :, index * head_size : (index + 1) * head_size].astype(f32)
        return jnp.sum(part.reshape(kv_heads, splits, 2, weight_rows, head_size), axis=1)

    key_value_rows = home(2)
    flat = lambda part: side_by_side(part.reshape(-1, weight_rows, head_size))

    down_rows, gate_rows, up_rows = mlp_grads

    return (
        block_out[None],
        input_grad[None],
        flat(home(0)),
        flat(key_value_rows[:, 0]),
        flat(key_value_rows[:, 1]),
        flat(home(1)),
        gate_rows,
        up_rows,
        down_rows,
        attn_extra[:model],
        attn_extra[model + 2 * head_size :],
        attn_extra[model : model + head_size],
        attn_extra[model + head_size : model + 2 * head_size],
    )


def solution(mesh):
    in_specs = (
        P("fsdp", "ctx", None),
        P(("ctx", "fsdp"), None),
        P(("ctx", "fsdp"), None),
        P(("ctx", "fsdp"), None),
        P(("ctx", "fsdp"), None),
        P(("ctx", "fsdp"), None),
        P(("ctx", "fsdp"), None),
        P(("ctx", "fsdp"), None),
        P(),
        P(),
        P(),
        P(),
        P(),
        P("fsdp", "ctx", None),
    )
    out_specs = (
        P("fsdp", "ctx", None),
        P("fsdp", "ctx", None),
        P(("ctx", "fsdp"), None),
        P(("ctx", "fsdp"), None),
        P(("ctx", "fsdp"), None),
        P(("ctx", "fsdp"), None),
        P(("ctx", "fsdp"), None),
        P(("ctx", "fsdp"), None),
        P(("ctx", "fsdp"), None),
        P(),
        P(),
        P(),
        P(),
    )
    return jax.shard_map(shards, mesh=mesh, in_specs=in_specs, out_specs=out_specs, check_vma=False)
```

```python
import functools
import math

import jax
import jax.numpy as jnp
import numpy as np
from jax import lax
from jax.experimental import pallas as pl
from jax.experimental.layout import Layout, with_layout_constraint
from jax.experimental.pallas import tpu as pltpu
from jax.sharding import PartitionSpec as P

eps_model = 1e-06
rope_base = 1000000.0
f32 = jnp.float32
bf16 = jnp.bfloat16


def inv_root(field):
    return lax.rsqrt(jnp.mean(field * field, axis=-1, keepdims=True) + eps_model)


def norm_back(field, factor, gain, grad_in):
    weighted = gain * grad_in
    inner_mean = jnp.mean(weighted * field, axis=-1, keepdims=True)
    return factor * weighted - field * (factor * factor * factor) * inner_mean


def rope_tables(positions, head_size):
    half_size = head_size // 2
    exponent = jnp.arange(half_size, dtype=f32) * f32(2.0 / head_size)
    inverse = jnp.exp(-exponent * f32(math.log(rope_base)))
    angles = positions.astype(f32)[:, None] * inverse[None, :]
    cosine, sine = jnp.cos(angles), jnp.sin(angles)
    return jnp.concatenate([cosine, cosine], axis=1), jnp.concatenate([-sine, sine], axis=1)


def dot_nn(left, right):
    return lax.dot_general(left, right, (((1,), (0,)), ((), ())), preferred_element_type=f32)


def dot_nt(left, right):
    return lax.dot_general(left, right, (((1,), (1,)), ((), ())), preferred_element_type=f32)


def dot_tn(left, right):
    return lax.dot_general(left, right, (((0,), (0,)), ((), ())), preferred_element_type=f32)


def allowed_tile(key_first, query_tile, pos_table, tile_k, tile_q, rows, sorted_all):
    key_pos = key_first + lax.broadcasted_iota(jnp.int32, (tile_k, tile_q), 0)
    lane = lax.broadcasted_iota(jnp.int32, (1, tile_q), 1)
    if sorted_all:
        query_pos = query_tile * tile_q + lane
    else:
        per_tile = tile_q // rows
        query_pos = jnp.zeros((1, tile_q), jnp.int32)
        for piece in range(per_tile):
            first = pos_table[query_tile * per_tile + piece] * rows
            inside = (lane >= piece * rows) & (lane < (piece + 1) * rows)
            query_pos = jnp.where(inside, first + lane - piece * rows, query_pos)
    return key_pos <= query_pos


def tile_loop(query_tile, key_tiles, sorted_all, work):
    if sorted_all:
        for key_tile in range(query_tile):
            work(key_tile, False)
        work(query_tile, True)
    else:

        @pl.loop(0, key_tiles)
        def _(key_tile):
            work(key_tile, True)


def query_loop(query_tiles, sorted_all, work):
    if sorted_all:
        for query_tile in range(query_tiles):
            work(query_tile)
    else:

        @pl.loop(0, query_tiles)
        def _(query_tile):
            work(query_tile)


def block_loop(blocks, work):
    def step(index, carry):
        work(index)
        return carry

    lax.fori_loop(0, blocks, step, 0, unroll=4)


def rows_at(index, rows):
    return pl.ds(pl.multiple_of(index * rows, rows), rows)


def each_key(key_pos, blocks, rows, work):
    for part in range(2):
        block_loop(
            blocks // 2,
            lambda index: work(
                part, rows_at(index, rows), rows_at(key_pos[part * (blocks // 2) + index], rows)
            ),
        )


def each_query(key_pos, query_table, pos_table, blocks, count, rows, sorted_all, work):
    if sorted_all:
        each_key(key_pos, blocks, rows, lambda part, here, place: work(part, here, place, place))
        return

    @pl.loop(0, count)
    def _(index):
        local = query_table[index]
        place, at_pos = rows_at(index, rows), rows_at(pos_table[index], rows)
        for part in range(2):
            inner = local - part * (blocks // 2)

            @pl.when((inner >= 0) & (inner < blocks // 2))
            def _():
                work(part, rows_at(inner, rows), place, at_pos)


def turn(field):
    return pltpu.roll(field, field.shape[-1] // 2, 1)


def attend_kernel(
    geometry, key_pos, query_table, pos_table, raw_a, raw_b, cos_ref, sin_ref, q_gain, k_gain,
    out_a, out_b, lse_ref, q_sorted, k_sorted, v_sorted, v_turned, acc, total, out_sorted,
):
    rows, tile, sorted_all, scale = geometry
    head = q_gain.shape[1]
    keys, queries = k_sorted.shape[0], q_sorted.shape[0]
    key_tiles, query_tiles = keys // tile, queries // tile
    raw, out = (raw_a, raw_b), (out_a, out_b)
    walk = (key_pos, query_table, pos_table, keys // rows, queries // rows, rows, sorted_all)

    def rope(field, gain, place):
        normed = field * inv_root(field) * gain[...]
        return (normed * cos_ref[place, :] + turn(normed) * sin_ref[place, :]).astype(bf16)

    def take_keys(part, here, place):
        k_sorted[place, :] = rope(raw[part][here, head : 2 * head], k_gain, place)
        v_sorted[place, :] = raw[part][here, 2 * head : 3 * head].astype(bf16)

    def take_queries(part, here, place, at_pos):
        q_sorted[place, :] = rope(raw[part][here, :head], q_gain, at_pos)

    each_key(key_pos, keys // rows, rows, take_keys)
    each_query(*walk, take_queries)
    for key_tile in range(key_tiles):
        piece = v_sorted[key_tile * tile : (key_tile + 1) * tile, :]
        v_turned[:, key_tile * tile : (key_tile + 1) * tile] = piece.astype(f32).T.astype(bf16)
    if not sorted_all:
        out_a[...] = jnp.zeros_like(out_a)
        out_b[...] = jnp.zeros_like(out_b)

    def query_work(query_tile):
        q_start = pl.multiple_of(query_tile * tile, tile)
        q_tile = q_sorted[pl.ds(q_start, tile), :]
        acc[...] = jnp.zeros_like(acc)
        total[...] = jnp.zeros_like(total)

        def work(key_tile, masked):
            k_start = pl.multiple_of(key_tile * tile, tile)
            scores = dot_nt(k_sorted[pl.ds(k_start, tile), :], q_tile)
            probs = jnp.exp(scores * scale)
            if masked:
                keep = allowed_tile(k_start, query_tile, pos_table, tile, tile, rows, sorted_all)
                probs = jnp.where(keep, probs, 0.0)
            total[...] += jnp.sum(probs, axis=0, keepdims=True)
            acc[...] += dot_nn(v_turned[:, pl.ds(k_start, tile)], probs.astype(bf16))

        tile_loop(query_tile, key_tiles, sorted_all, work)
        lse_ref[:, pl.ds(q_start, tile)] = jnp.log(total[...])
        out_sorted[pl.ds(q_start, tile), :] = (acc[...] / total[...]).T.astype(bf16)

    query_loop(query_tiles, sorted_all, query_work)

    def put(part, here, place, at_pos):
        out[part][here, :] = out_sorted[place, :]

    each_query(*walk, put)


def whole_spec(shape):
    return pl.BlockSpec(memory_space=pltpu.VMEM)


def attend(tables, raw, cosine, sine, query_gain, key_gain, rows, sorted_all, scale):
    head = query_gain.shape[1]
    keys = cosine.shape[0]
    queries = tables[1].shape[0] * rows
    tile = math.gcd(math.gcd(queries, keys), 512)
    narrow, row, part = whole_spec((keys, head)), whole_spec((1, head)), whole_spec((keys // 2, head))
    return pl.pallas_call(
        functools.partial(attend_kernel, (rows, tile, sorted_all, scale)),
        out_shape=(
            jax.ShapeDtypeStruct((keys // 2, head), bf16),
            jax.ShapeDtypeStruct((keys // 2, head), bf16),
            jax.ShapeDtypeStruct((1, queries), f32),
            jax.ShapeDtypeStruct((queries, head), bf16),
            jax.ShapeDtypeStruct((keys, head), bf16),
            jax.ShapeDtypeStruct((keys, head), bf16),
        ),
        grid_spec=pltpu.PrefetchScalarGridSpec(
            num_scalar_prefetch=3,
            grid=(1,),
            in_specs=[whole_spec(raw[0].shape), whole_spec(raw[1].shape), narrow, narrow, row, row],
            out_specs=(part, part, whole_spec((1, queries)), whole_spec((queries, head)), narrow, narrow),
            scratch_shapes=[
                pltpu.VMEM((head, keys), bf16),
                pltpu.VMEM((head, tile), f32),
                pltpu.VMEM((1, tile), f32),
                pltpu.VMEM((queries, head), bf16),
            ],
        ),
        compiler_params=pltpu.CompilerParams(vmem_limit_bytes=(12 << 20) + 5120 * keys),
        cost_estimate=pl.CostEstimate(
            flops=4 * queries * keys * head, bytes_accessed=28 * keys * head, transcendentals=queries * keys
        ),
        name="attend",
    )(*tables, *raw, cosine, sine, query_gain, key_gain)


def attend_back_kernel(
    geometry, key_pos, query_table, pos_table, raw_a, raw_b, cos_ref, sin_ref, q_gain, k_gain,
    q_sorted, k_sorted, v_sorted, o_a, o_b, do_a, do_b, lse_ref,
    grads_a, grads_b, q_part, k_part,
    do_sorted, o_sorted, k_turned, delta, dq_turned, dq_sorted, dk_sorted, dv_sorted,
):
    rows, tile, sorted_all, scale = geometry
    head = q_gain.shape[1]
    keys, queries = k_sorted.shape[0], q_sorted.shape[0]
    key_tiles, query_tiles = keys // tile, queries // tile
    raw, o_ref, do_ref, grads = (raw_a, raw_b), (o_a, o_b), (do_a, do_b), (grads_a, grads_b)
    walk = (key_pos, query_table, pos_table, keys // rows, queries // rows, rows, sorted_all)

    def take(part, here, place, at_pos):
        do_sorted[place, :] = do_ref[part][here, :]
        o_sorted[place, :] = o_ref[part][here, :]

    each_query(*walk, take)
    for key_tile in range(key_tiles):
        piece = k_sorted[key_tile * tile : (key_tile + 1) * tile, :]
        k_turned[:, key_tile * tile : (key_tile + 1) * tile] = piece.astype(f32).T.astype(bf16)
    dk_sorted[...] = jnp.zeros_like(dk_sorted)
    dv_sorted[...] = jnp.zeros_like(dv_sorted)
    if not sorted_all:
        for part in range(2):
            grads[part][:, :head] = jnp.zeros((keys // 2, head), bf16)

    def query_work(query_tile):
        q_start = pl.multiple_of(query_tile * tile, tile)
        q_tile = q_sorted[pl.ds(q_start, tile), :]
        do_tile = do_sorted[pl.ds(q_start, tile), :]
        product = do_tile.astype(f32) * o_sorted[pl.ds(q_start, tile), :].astype(f32)
        delta[...] = jnp.sum(product.T, axis=0, keepdims=True)
        dq_turned[...] = jnp.zeros_like(dq_turned)

        def work(key_tile, masked):
            k_start = pl.multiple_of(key_tile * tile, tile)
            here = pl.ds(k_start, tile)
            scores = dot_nt(k_sorted[here, :], q_tile)
            probs = jnp.exp(scores * scale - lse_ref[:, pl.ds(q_start, tile)])
            if masked:
                keep = allowed_tile(k_start, query_tile, pos_table, tile, tile, rows, sorted_all)
                probs = jnp.where(keep, probs, 0.0)
            dv_sorted[here, :] += dot_nn(probs.astype(bf16), do_tile)
            d_probs = dot_nt(v_sorted[here, :], do_tile)
            d_scores = (probs * (d_probs - delta[...])).astype(bf16)
            dk_sorted[here, :] += dot_nn(d_scores, q_tile)
            dq_turned[...] += dot_nn(k_turned[:, here], d_scores)

        tile_loop(query_tile, key_tiles, sorted_all, work)
        dq_sorted[pl.ds(q_start, tile), :] = dq_turned[...].T

    query_loop(query_tiles, sorted_all, query_work)
    q_part[...] = jnp.zeros_like(q_part)
    k_part[...] = jnp.zeros_like(k_part)

    def through_norm(field, grad, gain, at_pos, gain_part):
        scaled = grad * scale
        normed_grad = scaled * cos_ref[at_pos, :] - turn(scaled) * sin_ref[at_pos, :]
        factor = inv_root(field)
        gain_part[...] += jnp.sum(normed_grad * field * factor, axis=0, keepdims=True)
        return norm_back(field, factor, gain[...], normed_grad).astype(bf16)

    def put_queries(part, here, place, at_pos):
        grads[part][here, :head] = through_norm(
            raw[part][here, :head], dq_sorted[place, :], q_gain, at_pos, q_part
        )

    def put_keys(part, here, place):
        grads[part][here, head : 2 * head] = through_norm(
            raw[part][here, head : 2 * head], dk_sorted[place, :], k_gain, place, k_part
        )
        grads[part][here, 2 * head :] = dv_sorted[place, :].astype(bf16)

    each_query(*walk, put_queries)
    each_key(key_pos, keys // rows, rows, put_keys)


def attend_back(tables, raw, cosine, sine, query_gain, key_gain, saved, out, d_out, lse, rows, sorted_all, scale):
    head = query_gain.shape[1]
    keys = cosine.shape[0]
    queries = tables[1].shape[0] * rows
    tile = math.gcd(math.gcd(queries, keys), 512)
    narrow, row, part = whole_spec((keys, head)), whole_spec((1, head)), whole_spec((keys // 2, head))
    q_spec, wide = whole_spec((queries, head)), whole_spec((keys // 2, 3 * head))
    return pl.pallas_call(
        functools.partial(attend_back_kernel, (rows, tile, sorted_all, scale)),
        out_shape=(
            jax.ShapeDtypeStruct((keys // 2, 3 * head), bf16),
            jax.ShapeDtypeStruct((keys // 2, 3 * head), bf16),
            jax.ShapeDtypeStruct((1, head), f32),
            jax.ShapeDtypeStruct((1, head), f32),
        ),
        grid_spec=pltpu.PrefetchScalarGridSpec(
            num_scalar_prefetch=3,
            grid=(1,),
            in_specs=[
                whole_spec(raw[0].shape), whole_spec(raw[1].shape), narrow, narrow, row, row,
                q_spec, narrow, narrow, part, part, part, part, whole_spec((1, queries)),
            ],
            out_specs=(wide, wide, row, row),
            scratch_shapes=[
                pltpu.VMEM((queries, head), bf16),
                pltpu.VMEM((queries, head), bf16),
                pltpu.VMEM((head, keys), bf16),
                pltpu.VMEM((1, tile), f32),
                pltpu.VMEM((head, tile), f32),
                pltpu.VMEM((queries, head), f32),
                pltpu.VMEM((keys, head), f32),
                pltpu.VMEM((keys, head), f32),
            ],
        ),
        compiler_params=pltpu.CompilerParams(
            vmem_limit_bytes=min(60 << 20, (16 << 20) + 7168 * keys)
        ),
        cost_estimate=pl.CostEstimate(
            flops=10 * queries * keys * head, bytes_accessed=40 * keys * head, transcendentals=queries * keys
        ),
        name="attend_back",
    )(*tables, *raw, cosine, sine, query_gain, key_gain, *saved, *out, *d_out, lse)


def project_kernel(weight_ref, gain_ref, *refs):
    count = len(refs) - 2
    normed_ref, out_ref = refs[count:]
    rows = refs[0].shape[0]
    for index in range(count):
        wide = refs[index][...].astype(f32)
        normed = (wide * inv_root(wide) * gain_ref[...]).astype(bf16)
        place = pl.ds(index * rows, rows)
        normed_ref[place, :] = normed
        out_ref[place, :] = dot_nn(normed, weight_ref[...])


def project(blocks, gain, weight):
    rows, width = blocks[0].shape
    total, columns = rows * len(blocks), weight.shape[1]
    return pl.pallas_call(
        project_kernel,
        out_shape=(
            jax.ShapeDtypeStruct((total, width), bf16),
            jax.ShapeDtypeStruct((total, columns), f32),
        ),
        grid=(1,),
        in_specs=[whole_spec(weight.shape), whole_spec((1, width))]
        + [whole_spec((rows, width))] * len(blocks),
        out_specs=(whole_spec((total, width)), whole_spec((total, columns))),
        compiler_params=pltpu.CompilerParams(
            vmem_limit_bytes=(12 << 20) + 12 * total * width
        ),
        cost_estimate=pl.CostEstimate(
            flops=2 * total * width * columns, bytes_accessed=4 * total * width, transcendentals=total
        ),
        name="project",
    )(weight, gain[None, :], *blocks)


class Ring:
    def __init__(self, size):
        self.chips = size // 2
        self.reach = self.chips // 2
        self.order = list(range(0, self.chips, 2)) + list(range(self.chips - 1, 0, -2))
        self.swap_pairs = [(i, i ^ 1) for i in range(size)]
        self.out_pairs = []
        for place, chip in enumerate(self.order):
            after_it = self.order[(place + 1) % self.chips]
            self.out_pairs.append((2 * chip, 2 * after_it))
            self.out_pairs.append((2 * after_it + 1, 2 * chip + 1))
        self.home_pairs = [(target, source) for source, target in self.out_pairs]

    def swap(self, field):
        return lax.ppermute(field, "ctx", self.swap_pairs)

    def out(self, field):
        return lax.ppermute(field, "ctx", self.out_pairs)

    def home(self, field):
        return lax.ppermute(field, "ctx", self.home_pairs)

    def members(self, rank):
        chip, core = rank // 2, rank % 2
        place = self.order.index(chip)
        blocks = [rank]
        for step in range(1, self.reach + 1):
            near = self.order[(place + (2 * core - 1) * step) % self.chips]
            blocks.append(2 * near + core)
            if step < self.reach:
                blocks.append(2 * near + 1 - core)
        return blocks

    def gather(self, block, hooks=None):
        hooks = hooks or {}
        streams = [block, self.swap(block)]
        blocks = [block]
        for hop in range(2 * self.reach - 1):
            held = streams[hop % 2]
            if hop >= 3:
                held = after(held, blocks[hop - 2])
            if hop in hooks:
                held = after(held, hooks[hop](blocks))
            streams[hop % 2] = self.out(held)
            blocks.append(streams[hop % 2])
        return blocks

    def scatter_hops(self, term, streams, hops, needs=None, first_twice=False):
        needs = needs or {}
        order = list(range(2 * self.reach - 1, 0, -1))
        if first_twice:
            for place in range(1, len(order), 2):
                order[place : place + 2] = reversed(order[place : place + 2])
        streams, marks, total = list(streams), [], None
        for hop in hops:
            index = order[hop]
            stream, held = 1 - index % 2, streams[1 - index % 2]
            if held is None:
                total = term(index)
            else:
                held = held if total is None else after(held, total)
                total = (term(index).astype(f32) + held.astype(f32)).astype(bf16)
            if hop in needs:
                total = after(total, needs[hop](marks))
            streams[stream] = self.home(total)
            marks.append(streams[stream])
        return streams, marks

    def scatter_end(self, term, streams):
        first, second = streams
        return first.astype(f32) + term(0).astype(f32) + self.swap(second).astype(f32)

    def scatter_sum(self, term, needs=None, first_twice=False):
        streams, marks = self.scatter_hops(
            term, [None, None], range(2 * self.reach - 1), needs, first_twice
        )
        return self.scatter_end(term, streams), marks


def after(value, *events):
    return lax.optimization_barrier((value, events))[0]


def spread(rows_block):
    return lax.all_to_all(rows_block, "ctx", split_axis=0, concat_axis=0, tiled=False)


def swap_rows(field):
    return lax.ppermute(field, "fsdp", [(0, 1), (1, 0)])


def to_columns(received, partner, fsdp_rank):
    first = jnp.where(fsdp_rank == 0, received, partner)
    second = jnp.where(fsdp_rank == 0, partner, received)
    both = jnp.stack([first, second], axis=1)
    return both.reshape(-1, received.shape[-1])


def halves(grads, extra, fsdp_rank, ctx_size):
    width = grads.shape[1]
    split = grads.reshape(ctx_size, 2, -1, width)
    keep = jnp.where(fsdp_rank == 0, split[:, 0], split[:, 1])
    give = jnp.where(fsdp_rank == 0, split[:, 1], split[:, 0])
    if extra is None:
        return keep, give, None
    count = extra.shape[0]
    lines = -(-count // width)
    lines = -(-lines // 16) * 16
    extra_block = jnp.pad(extra, (0, lines * width - count)).reshape(lines, width).astype(bf16)
    return keep, jnp.concatenate([give.reshape(-1, width), extra_block], axis=0), extra_block


def join(keep, given, extra_block):
    if extra_block is None:
        return (keep.astype(f32) + given.astype(f32)).astype(bf16)
    ctx_size, rows, width = keep.shape
    body = given[: ctx_size * rows].reshape(keep.shape)
    total = (keep.astype(f32) + body.astype(f32)).astype(bf16)
    extras = (extra_block.astype(f32) + given[ctx_size * rows :].astype(f32)).astype(bf16)
    return jnp.concatenate(
        [total, jnp.broadcast_to(extras[None], (ctx_size,) + extras.shape)], axis=1
    )


def apart(received, rows, width, count):
    lines = received[:, rows:, :width].astype(f32)
    return received[:, :rows], jnp.sum(lines, axis=0).reshape(-1)[:count]


def side_by_side(pieces):
    count, rows, width = pieces.shape
    return jnp.transpose(pieces, (1, 0, 2)).reshape(rows, count * width)


def shards(
    block_input,
    query_weight,
    key_weight,
    value_weight,
    output_weight,
    gate_weight,
    up_weight,
    down_weight,
    attn_gain,
    mlp_gain,
    query_gain,
    key_gain,
    block_order,
    cotangent,
):
    ctx_size = lax.axis_size("ctx")
    ctx_rank = lax.axis_index("ctx")
    fsdp_rank = lax.axis_index("fsdp")
    core = ctx_rank % 2
    tokens = block_input.shape[1]
    model = block_input.shape[2]
    head_size = query_gain.shape[0]
    kv_heads = key_weight.shape[1] // head_size
    slots = block_order.shape[0]
    length = tokens * ctx_size
    half_rows = length // slots
    per_block = tokens // half_rows
    weight_rows = query_weight.shape[0]
    hidden_slice = gate_weight.shape[1] // ctx_size
    splits = ctx_size // 2 // kv_heads
    split_rank = (ctx_rank // 2) % splits
    sorted_all = splits == 1
    score_scale = 1.0 / math.sqrt(head_size)
    ring = Ring(ctx_size)
    always = jnp.min(block_order) >= 0

    def fenced(work, *values):
        shapes = jax.eval_shape(work, *values)
        blank = lambda *_: jax.tree.map(lambda leaf: jnp.zeros(leaf.shape, leaf.dtype), shapes)
        return lax.cond(always, work, blank, *values)

    def block_rows(field, index):
        return field[index * tokens : (index + 1) * tokens]

    def by_head(weight):
        split = jnp.transpose(weight.reshape(weight_rows, kv_heads, -1, head_size), (1, 2, 0, 3))
        return jnp.broadcast_to(split[:, None], (kv_heads, splits) + split.shape[1:]).reshape(
            -1, weight_rows, head_size
        )

    key_value = jnp.stack(
        [key_weight.reshape(weight_rows, kv_heads, head_size),
         value_weight.reshape(weight_rows, kv_heads, head_size)],
        axis=2,
    ).reshape(weight_rows, -1)
    head_block = jnp.concatenate(
        [by_head(query_weight), by_head(output_weight), by_head(key_value)], axis=2
    )
    head_received = spread(after(head_block, ring.swap(block_input[0])))
    head_mine = to_columns(head_received, swap_rows(head_received), fsdp_rank)
    head_other = ring.swap(head_mine)

    def column(field, index):
        return field[:, index * head_size : (index + 1) * head_size]

    def key_first(mine, other):
        return jnp.where(core == 0, mine, other), jnp.where(core == 0, other, mine)

    key_columns, value_columns = key_first(column(head_mine, 2), column(head_other, 2))
    head_weight = jnp.concatenate(
        [column(head_mine, 0), key_columns, value_columns, column(head_other, 0)], axis=1
    )
    output_part = jnp.concatenate([column(head_mine, 1), column(head_other, 1)], axis=1)

    last_hop = 2 * ring.reach - 2
    angles = {}

    def make_angles(blocks):
        angles["tables"] = rope_tables(
            after(jnp.arange(length, dtype=jnp.int32), blocks[2]), head_size
        )
        return angles["tables"]

    input_blocks = ring.gather(block_input[0], {last_hop - 1: make_angles})
    member_table = np.array(
        [ring.members(rank) + ring.members(rank ^ 1) for rank in range(ctx_size)], np.int32
    )
    ranks = jnp.arange(ctx_size, dtype=jnp.int32)
    listed = jnp.sum(jnp.where(ranks[:, None] == ctx_rank, member_table, 0), axis=0)
    slot_index = jnp.arange(slots, dtype=jnp.int32)
    local_slot = (
        listed[:, None] * per_block + jnp.arange(per_block, dtype=jnp.int32)[None, :]
    ).reshape(-1)
    local_pos = jnp.sum(
        jnp.where(local_slot[:, None] == slot_index[None, :], block_order[None, :], 0), axis=1
    )
    cosine, sine = angles["tables"]
    if sorted_all:
        tables = (local_pos, slot_index, slot_index)
    else:
        local_of_pos = jnp.sum(
            jnp.where(local_pos[None, :] == slot_index[:, None], slot_index[None, :], 0), axis=1
        )
        compact = jnp.arange(slots // splits, dtype=jnp.int32)
        owner = (compact // per_block) * splits + split_rank
        own_pos = jnp.sort(jnp.take(block_order, owner * per_block + compact % per_block))
        tables = (local_pos, jnp.take(local_of_pos, own_pos), own_pos)
    query_row, key_row = query_gain[None, :], key_gain[None, :]

    input_blocks[4] = after(input_blocks[4], head_received)

    def by_slice(weight):
        return jnp.transpose(weight.reshape(weight_rows, ctx_size, hidden_slice), (1, 0, 2))

    gate, up, down = after((gate_weight, up_weight, down_weight), input_blocks[3])
    mlp_block = jnp.concatenate([by_slice(gate), by_slice(up), by_slice(down)], axis=2)
    normed_attn, projected = project(input_blocks, attn_gain, head_weight)
    projected_given = ring.swap(
        jnp.concatenate(
            [projected[:, 3 * head_size :], projected[:, head_size : 3 * head_size]], axis=1
        )
    )
    raw = (projected, projected_given)
    attn_a, attn_b, lse, *saved = attend(
        tables, raw, cosine, sine, query_row, key_row, half_rows, sorted_all, score_scale
    )
    mlp_received = spread(after(mlp_block, input_blocks[-1], input_blocks[-2]))
    mlp_received = after(mlp_received, attn_a)
    mlp_partner = swap_rows(mlp_received)
    attn_pair = jnp.concatenate([attn_a, ring.swap(attn_b)], axis=1)

    inputs32 = block_input[0].astype(f32)
    attn_terms = dot_nt(attn_pair, output_part).astype(bf16)
    attn_out = fenced(
        lambda terms: ring.scatter_sum(lambda i: block_rows(terms, i))[0], attn_terms
    )
    hidden_one = inputs32 + attn_out
    scale_mlp = inv_root(hidden_one)
    normed_mlp = (hidden_one * scale_mlp * mlp_gain).astype(bf16)
    mlp_mine = to_columns(mlp_received, mlp_partner, fsdp_rank)
    mlp_other = ring.swap(mlp_mine)
    pair = 2 * hidden_slice
    gate_up = jnp.concatenate([mlp_mine[:, :pair], mlp_other[:, :pair]], axis=1)
    down_part = jnp.concatenate([mlp_mine[:, pair:], mlp_other[:, pair:]], axis=1)

    normed_blocks = ring.gather(normed_mlp)
    normed_all = jnp.concatenate(normed_blocks, axis=0)
    gate_up, down_part = lax.optimization_barrier((gate_up, down_part))
    middle = ring.reach * tokens
    hidden_parts = [dot_nn(normed_all[:middle], gate_up), dot_nn(normed_all[middle:], gate_up)]
    cot_blocks = ring.gather(
        after(cotangent[0], normed_blocks[-2]),
        {
            last_hop - 4: lambda _: gate_up,
            last_hop - 3: lambda _: hidden_parts[0],
            last_hop - 1: lambda _: hidden_parts[1],
        },
    )
    hidden_all = jnp.concatenate(hidden_parts, axis=0)
    cot_all = jnp.concatenate(cot_blocks, axis=0)
    act_grad_all = dot_nn(cot_all, down_part)
    activated_list, back_list = [], []
    for member in range(2):
        gate_pre = hidden_all[:, 2 * member * hidden_slice : (2 * member + 1) * hidden_slice]
        up_pre = hidden_all[:, (2 * member + 1) * hidden_slice : (2 * member + 2) * hidden_slice]
        act_grad = act_grad_all[:, member * hidden_slice : (member + 1) * hidden_slice]
        sigma = jax.nn.sigmoid(gate_pre)
        activated_list.append((gate_pre * sigma * up_pre).astype(bf16))
        back_list.append(
            (act_grad * up_pre * sigma * (1.0 + gate_pre * (1.0 - sigma))).astype(bf16)
        )
        back_list.append((act_grad * gate_pre * sigma).astype(bf16))
    activated_all = jnp.concatenate(activated_list, axis=1)
    back_all = jnp.concatenate(back_list, axis=1)
    far = (2 * ring.reach - 3) * tokens
    far_terms = dot_nt(back_all[far:], gate_up).astype(bf16)
    near_blocks = far // tokens
    add = lambda left, right: (left.astype(f32) + right.astype(f32)).astype(bf16)

    def feed_forward_grads(far_terms, back_all, activated_all, normed_all, cot_all, gate_up):
        near_terms = dot_nt(back_all[:far], gate_up).astype(bf16)
        ready = {}

        def piece(left, right, mark):
            grad = dot_tn(left, after(right, mark)).astype(bf16)
            return with_layout_constraint(grad, Layout((0, 1)))

        def down_away(marks):
            ready["down_give"] = piece(cot_all, activated_all[:, hidden_slice:], marks[0])
            return ready["down_give"]

        def gate_up_away(marks):
            ready["gate_up_give"] = piece(normed_all, back_all[:, pair:], marks[1])
            return ready["gate_up_give"]

        def down_here(marks):
            ready["down"] = piece(cot_all, activated_all[:, :hidden_slice], marks[2])
            return ready["down"]

        def gate_up_here(marks):
            ready["gate_up"] = piece(normed_all, back_all[:, :pair], marks[3])
            return ready["gate_up"]

        summed, marks = ring.scatter_sum(
            lambda i: block_rows(near_terms, i)
            if i < near_blocks
            else block_rows(far_terms, i - near_blocks),
            {2: down_away, 3: gate_up_away, 4: down_here, 5: gate_up_here},
            first_twice=True,
        )
        ready["down"] = add(ready["down"], ring.swap(ready["down_give"]))
        ready["gate_up"] = add(ready["gate_up"], ring.swap(ready["gate_up_give"]))
        near_late, far_late = after((near_terms, far_terms), marks[4])
        gain_part = jnp.sum(
            near_late.astype(f32) * normed_all[:far].astype(f32), axis=0
        ) + jnp.sum(far_late.astype(f32) * normed_all[far:].astype(f32), axis=0)
        down_own, down_away, _ = halves(ready["down"], None, fsdp_rank, ctx_size)
        gate_up_own, gate_up_away, _ = halves(ready["gate_up"], None, fsdp_rank, ctx_size)
        return summed, gain_part / mlp_gain, down_own, down_away, gate_up_own, gate_up_away

    normed_mlp_grad, mlp_gain_part, down_own, down_away, gate_up_own, gate_up_away = fenced(
        feed_forward_grads, far_terms, back_all, activated_all, normed_all, cot_all, gate_up
    )
    grad32 = cotangent[0].astype(f32)
    hidden_grad = grad32 + norm_back(hidden_one, scale_mlp, mlp_gain, normed_mlp_grad)
    hidden_grad_bf = hidden_grad.astype(bf16)
    down_own, gate_up_own = lax.optimization_barrier((down_own, gate_up_own))
    down_other, gate_up_other = swap_rows(down_away), swap_rows(gate_up_away)


    def gather_grads(block, activated_all, down_part):
        ready = {}

        def output_terms(blocks):
            ready["out"] = dot_nt(after(activated_all, blocks[2]), down_part).astype(bf16)
            return ready["out"]

        blocks = ring.gather(block, {last_hop - 1: output_terms})
        return jnp.concatenate(blocks, axis=0), ready["out"]

    grad_all, out_terms = fenced(gather_grads, hidden_grad_bf, activated_all, down_part)
    attn_grad_pair = dot_nn(grad_all, output_part).astype(bf16)
    attn_grad = (attn_grad_pair[:, :head_size], ring.swap(attn_grad_pair[:, head_size:]))
    mlp_sent = jnp.concatenate(
        [join(down_own, down_other, None), join(gate_up_own, gate_up_other, None)], axis=2
    )
    attn_grad, mlp_sent = lax.optimization_barrier((attn_grad, mlp_sent))

    mlp_rows = spread(mlp_sent)

    def attention_back(attn_grad, attn_a, attn_b, projected, given):
        first_a, first_b, query_gain_part, key_gain_part = attend_back(
            tables, (projected, given), cosine, sine, query_row, key_row, saved, (attn_a, attn_b),
            attn_grad, lse, half_rows, sorted_all, score_scale,
        )
        given_grads = ring.swap(first_b)
        half_grads = jnp.concatenate(
            [
                first_a[:, :head_size],
                add(first_a[:, head_size:], given_grads[:, head_size:]),
                given_grads[:, :head_size],
            ],
            axis=1,
        )
        input_terms = dot_nt(half_grads, head_weight).astype(bf16)
        return half_grads, input_terms, query_gain_part[0], key_gain_part[0]

    half_grads, input_terms, query_gain_part, key_gain_part = fenced(
        attention_back, attn_grad, attn_a, attn_b, *raw
    )

    def attention_grads(input_terms, half_grads, grad_all, normed_attn, attn_pair):
        ready = {}

        def weight_grads(marks):
            late_grads, late_attn = after((half_grads, attn_pair), marks[0])
            head_grad = dot_tn(normed_attn, late_grads).astype(bf16)
            output_grad = dot_tn(grad_all, late_attn).astype(bf16)
            kv_keep, kv_give = key_first(column(head_grad, 1), column(head_grad, 2))
            keep = jnp.concatenate([column(head_grad, 0), column(output_grad, 0), kv_keep], axis=1)
            give = jnp.concatenate([column(head_grad, 3), column(output_grad, 1), kv_give], axis=1)
            ready["gain"] = (
                jnp.sum(after(input_terms, marks[1]).astype(f32) * normed_attn.astype(f32), axis=0)
                / attn_gain
            )
            ready["grads"] = add(keep, ring.swap(give))
            return ready["grads"], ready["gain"]

        summed, _ = ring.scatter_sum(
            lambda i: block_rows(input_terms, i), {last_hop: weight_grads}
        )
        return summed, ready["grads"], ready["gain"]

    normed_attn_grad, attn_grads, attn_gain_part = fenced(
        attention_grads, input_terms, half_grads, grad_all, normed_attn, attn_pair
    )
    gains = jnp.concatenate([attn_gain_part, query_gain_part, key_gain_part, mlp_gain_part])

    def out_and_home(out_terms, attn_grads, gains, mlp_rows, summed_grad, hidden_grad, inputs32):
        own, away, lines = halves(attn_grads, gains, fsdp_rank, ctx_size)
        ready = {}

        def other_rows(_):
            ready["other"] = swap_rows(away)
            return ready["other"]

        def rows_home(_):
            sent = join(own, ready["other"], lines)
            ready["rows"] = spread(sent)
            return sent

        def unpack(marks):
            rows = after(mlp_rows, marks[4])
            ready["mlp"] = tuple(
                side_by_side(rows[:, :, i * hidden_slice : (i + 1) * hidden_slice]).astype(f32)
                for i in range(3)
            )
            return ready["mlp"]

        def finish(marks):
            ready["input"] = hidden_grad + norm_back(
                inputs32, inv_root(inputs32), attn_gain, after(summed_grad, marks[3])
            )
            return ready["input"]

        summed, marks = ring.scatter_sum(
            lambda i: block_rows(out_terms, i),
            {4: other_rows, 5: rows_home},
        )
        finish(marks)
        unpack(marks)
        return summed, ready["rows"], ready["input"], ready["mlp"]

    attn_grads, mlp_rows = lax.optimization_barrier((attn_grads, mlp_rows))
    mlp_out, attn_home, input_grad, mlp_grads = fenced(
        out_and_home, out_terms, attn_grads, gains, mlp_rows, normed_attn_grad,
        hidden_grad, inputs32,
    )
    block_out = (hidden_one + mlp_out).astype(bf16)
    attn_rows, attn_extra = apart(
        attn_home,
        weight_rows,
        3 * head_size,
        2 * model + 2 * head_size,
    )

    def home(index):
        part = attn_rows[:, :, index * head_size : (index + 1) * head_size].astype(f32)
        return jnp.sum(part.reshape(kv_heads, splits, 2, weight_rows, head_size), axis=1)

    key_value_rows = home(2)
    flat = lambda part: side_by_side(part.reshape(-1, weight_rows, head_size))

    down_rows, gate_rows, up_rows = mlp_grads

    return (
        block_out[None],
        input_grad[None],
        flat(home(0)),
        flat(key_value_rows[:, 0]),
        flat(key_value_rows[:, 1]),
        flat(home(1)),
        gate_rows,
        up_rows,
        down_rows,
        attn_extra[:model],
        attn_extra[model + 2 * head_size :],
        attn_extra[model : model + head_size],
        attn_extra[model + head_size : model + 2 * head_size],
    )


def solution(mesh):
    in_specs = (
        P("fsdp", "ctx", None),
        P(("ctx", "fsdp"), None),
        P(("ctx", "fsdp"), None),
        P(("ctx", "fsdp"), None),
        P(("ctx", "fsdp"), None),
        P(("ctx", "fsdp"), None),
        P(("ctx", "fsdp"), None),
        P(("ctx", "fsdp"), None),
        P(),
        P(),
        P(),
        P(),
        P(),
        P("fsdp", "ctx", None),
    )
    out_specs = (
        P("fsdp", "ctx", None),
        P("fsdp", "ctx", None),
        P(("ctx", "fsdp"), None),
        P(("ctx", "fsdp"), None),
        P(("ctx", "fsdp"), None),
        P(("ctx", "fsdp"), None),
        P(("ctx", "fsdp"), None),
        P(("ctx", "fsdp"), None),
        P(("ctx", "fsdp"), None),
        P(),
        P(),
        P(),
        P(),
    )
    return jax.shard_map(shards, mesh=mesh, in_specs=in_specs, out_specs=out_specs, check_vma=False)
```

```python
import functools
import math

import jax
import jax.numpy as jnp
import numpy as np
from jax import lax
from jax.experimental import pallas as pl
from jax.experimental.layout import Layout, with_layout_constraint
from jax.experimental.pallas import tpu as pltpu
from jax.sharding import PartitionSpec as P

eps_model = 1e-06
rope_base = 1000000.0
f32 = jnp.float32
bf16 = jnp.bfloat16


def inv_root(field):
    return lax.rsqrt(jnp.mean(field * field, axis=-1, keepdims=True) + eps_model)


def norm_back(field, factor, gain, grad_in):
    weighted = gain * grad_in
    inner_mean = jnp.mean(weighted * field, axis=-1, keepdims=True)
    return factor * weighted - field * (factor * factor * factor) * inner_mean


def rope_tables(positions, head_size):
    half_size = head_size // 2
    exponent = jnp.arange(half_size, dtype=f32) * f32(2.0 / head_size)
    inverse = jnp.exp(-exponent * f32(math.log(rope_base)))
    angles = positions.astype(f32)[:, None] * inverse[None, :]
    cosine, sine = jnp.cos(angles), jnp.sin(angles)
    return jnp.concatenate([cosine, cosine], axis=1), jnp.concatenate([-sine, sine], axis=1)


def dot_nn(left, right):
    return lax.dot_general(left, right, (((1,), (0,)), ((), ())), preferred_element_type=f32)


def dot_nt(left, right):
    return lax.dot_general(left, right, (((1,), (1,)), ((), ())), preferred_element_type=f32)


def dot_tn(left, right):
    return lax.dot_general(left, right, (((0,), (0,)), ((), ())), preferred_element_type=f32)


def allowed_tile(key_first, query_tile, pos_table, tile_k, tile_q, rows, sorted_all):
    key_pos = key_first + lax.broadcasted_iota(jnp.int32, (tile_k, tile_q), 0)
    lane = lax.broadcasted_iota(jnp.int32, (1, tile_q), 1)
    if sorted_all:
        query_pos = query_tile * tile_q + lane
    else:
        per_tile = tile_q // rows
        query_pos = jnp.zeros((1, tile_q), jnp.int32)
        for piece in range(per_tile):
            first = pos_table[query_tile * per_tile + piece] * rows
            inside = (lane >= piece * rows) & (lane < (piece + 1) * rows)
            query_pos = jnp.where(inside, first + lane - piece * rows, query_pos)
    return key_pos <= query_pos


def tile_loop(query_tile, key_tiles, sorted_all, work):
    if sorted_all:
        for key_tile in range(query_tile):
            work(key_tile, False)
        work(query_tile, True)
    else:

        @pl.loop(0, key_tiles)
        def _(key_tile):
            work(key_tile, True)


def query_loop(query_tiles, sorted_all, work):
    if sorted_all:
        for query_tile in range(query_tiles):
            work(query_tile)
    else:

        @pl.loop(0, query_tiles)
        def _(query_tile):
            work(query_tile)


def block_loop(blocks, work):
    def step(index, carry):
        work(index)
        return carry

    lax.fori_loop(0, blocks, step, 0, unroll=4)


def rows_at(index, rows):
    return pl.ds(pl.multiple_of(index * rows, rows), rows)


def each_key(key_pos, blocks, rows, work):
    for part in range(2):
        block_loop(
            blocks // 2,
            lambda index: work(
                part, rows_at(index, rows), rows_at(key_pos[part * (blocks // 2) + index], rows)
            ),
        )


def each_query(key_pos, query_table, pos_table, blocks, count, rows, sorted_all, work):
    if sorted_all:
        each_key(key_pos, blocks, rows, lambda part, here, place: work(part, here, place, place))
        return

    @pl.loop(0, count)
    def _(index):
        local = query_table[index]
        place, at_pos = rows_at(index, rows), rows_at(pos_table[index], rows)
        for part in range(2):
            inner = local - part * (blocks // 2)

            @pl.when((inner >= 0) & (inner < blocks // 2))
            def _():
                work(part, rows_at(inner, rows), place, at_pos)


def turn(field):
    return pltpu.roll(field, field.shape[-1] // 2, 1)


def attend_kernel(
    geometry, key_pos, query_table, pos_table, raw_a, raw_b, cos_ref, sin_ref, q_gain, k_gain,
    out_a, out_b, lse_ref, q_sorted, k_sorted, v_sorted, v_turned, acc, total, out_sorted,
):
    rows, tile, sorted_all, scale = geometry
    head = q_gain.shape[1]
    keys, queries = k_sorted.shape[0], q_sorted.shape[0]
    key_tiles, query_tiles = keys // tile, queries // tile
    raw, out = (raw_a, raw_b), (out_a, out_b)
    walk = (key_pos, query_table, pos_table, keys // rows, queries // rows, rows, sorted_all)

    def rope(field, gain, place):
        normed = field * inv_root(field) * gain[...]
        return (normed * cos_ref[place, :] + turn(normed) * sin_ref[place, :]).astype(bf16)

    def take_keys(part, here, place):
        k_sorted[place, :] = rope(raw[part][here, head : 2 * head], k_gain, place)
        v_sorted[place, :] = raw[part][here, 2 * head : 3 * head].astype(bf16)

    def take_queries(part, here, place, at_pos):
        q_sorted[place, :] = rope(raw[part][here, :head], q_gain, at_pos)

    each_key(key_pos, keys // rows, rows, take_keys)
    each_query(*walk, take_queries)
    for key_tile in range(key_tiles):
        piece = v_sorted[key_tile * tile : (key_tile + 1) * tile, :]
        v_turned[:, key_tile * tile : (key_tile + 1) * tile] = piece.astype(f32).T.astype(bf16)
    if not sorted_all:
        out_a[...] = jnp.zeros_like(out_a)
        out_b[...] = jnp.zeros_like(out_b)

    def query_work(query_tile):
        q_start = pl.multiple_of(query_tile * tile, tile)
        q_tile = q_sorted[pl.ds(q_start, tile), :]
        acc[...] = jnp.zeros_like(acc)
        total[...] = jnp.zeros_like(total)

        def work(key_tile, masked):
            k_start = pl.multiple_of(key_tile * tile, tile)
            scores = dot_nt(k_sorted[pl.ds(k_start, tile), :], q_tile)
            probs = jnp.exp(scores * scale)
            if masked:
                keep = allowed_tile(k_start, query_tile, pos_table, tile, tile, rows, sorted_all)
                probs = jnp.where(keep, probs, 0.0)
            total[...] += jnp.sum(probs, axis=0, keepdims=True)
            acc[...] += dot_nn(v_turned[:, pl.ds(k_start, tile)], probs.astype(bf16))

        tile_loop(query_tile, key_tiles, sorted_all, work)
        lse_ref[:, pl.ds(q_start, tile)] = jnp.log(total[...])
        out_sorted[pl.ds(q_start, tile), :] = (acc[...] / total[...]).T.astype(bf16)

    query_loop(query_tiles, sorted_all, query_work)

    def put(part, here, place, at_pos):
        out[part][here, :] = out_sorted[place, :]

    each_query(*walk, put)


def whole_spec(shape):
    return pl.BlockSpec(memory_space=pltpu.VMEM)


def attend(tables, raw, cosine, sine, query_gain, key_gain, rows, sorted_all, scale):
    head = query_gain.shape[1]
    keys = cosine.shape[0]
    queries = tables[1].shape[0] * rows
    tile = math.gcd(math.gcd(queries, keys), 512)
    narrow, row, part = whole_spec((keys, head)), whole_spec((1, head)), whole_spec((keys // 2, head))
    return pl.pallas_call(
        functools.partial(attend_kernel, (rows, tile, sorted_all, scale)),
        out_shape=(
            jax.ShapeDtypeStruct((keys // 2, head), bf16),
            jax.ShapeDtypeStruct((keys // 2, head), bf16),
            jax.ShapeDtypeStruct((1, queries), f32),
            jax.ShapeDtypeStruct((queries, head), bf16),
            jax.ShapeDtypeStruct((keys, head), bf16),
            jax.ShapeDtypeStruct((keys, head), bf16),
        ),
        grid_spec=pltpu.PrefetchScalarGridSpec(
            num_scalar_prefetch=3,
            grid=(1,),
            in_specs=[whole_spec(raw[0].shape), whole_spec(raw[1].shape), narrow, narrow, row, row],
            out_specs=(part, part, whole_spec((1, queries)), whole_spec((queries, head)), narrow, narrow),
            scratch_shapes=[
                pltpu.VMEM((head, keys), bf16),
                pltpu.VMEM((head, tile), f32),
                pltpu.VMEM((1, tile), f32),
                pltpu.VMEM((queries, head), bf16),
            ],
        ),
        compiler_params=pltpu.CompilerParams(vmem_limit_bytes=(12 << 20) + 5120 * keys),
        cost_estimate=pl.CostEstimate(
            flops=4 * queries * keys * head, bytes_accessed=28 * keys * head, transcendentals=queries * keys
        ),
        name="attend",
    )(*tables, *raw, cosine, sine, query_gain, key_gain)


def attend_back_kernel(
    geometry, key_pos, query_table, pos_table, raw_a, raw_b, cos_ref, sin_ref, q_gain, k_gain,
    q_sorted, k_sorted, v_sorted, o_a, o_b, do_a, do_b, lse_ref,
    grads_a, grads_b, q_part, k_part,
    do_sorted, o_sorted, k_turned, delta, dq_turned, dq_sorted, dk_sorted, dv_sorted,
):
    rows, tile, sorted_all, scale = geometry
    head = q_gain.shape[1]
    keys, queries = k_sorted.shape[0], q_sorted.shape[0]
    key_tiles, query_tiles = keys // tile, queries // tile
    raw, o_ref, do_ref, grads = (raw_a, raw_b), (o_a, o_b), (do_a, do_b), (grads_a, grads_b)
    walk = (key_pos, query_table, pos_table, keys // rows, queries // rows, rows, sorted_all)

    def take(part, here, place, at_pos):
        do_sorted[place, :] = do_ref[part][here, :]
        o_sorted[place, :] = o_ref[part][here, :]

    each_query(*walk, take)
    for key_tile in range(key_tiles):
        piece = k_sorted[key_tile * tile : (key_tile + 1) * tile, :]
        k_turned[:, key_tile * tile : (key_tile + 1) * tile] = piece.astype(f32).T.astype(bf16)
    dk_sorted[...] = jnp.zeros_like(dk_sorted)
    dv_sorted[...] = jnp.zeros_like(dv_sorted)
    if not sorted_all:
        for part in range(2):
            grads[part][:, :head] = jnp.zeros((keys // 2, head), bf16)

    def query_work(query_tile):
        q_start = pl.multiple_of(query_tile * tile, tile)
        q_tile = q_sorted[pl.ds(q_start, tile), :]
        do_tile = do_sorted[pl.ds(q_start, tile), :]
        product = do_tile.astype(f32) * o_sorted[pl.ds(q_start, tile), :].astype(f32)
        delta[...] = jnp.sum(product.T, axis=0, keepdims=True)
        dq_turned[...] = jnp.zeros_like(dq_turned)

        def work(key_tile, masked):
            k_start = pl.multiple_of(key_tile * tile, tile)
            here = pl.ds(k_start, tile)
            scores = dot_nt(k_sorted[here, :], q_tile)
            probs = jnp.exp(scores * scale - lse_ref[:, pl.ds(q_start, tile)])
            if masked:
                keep = allowed_tile(k_start, query_tile, pos_table, tile, tile, rows, sorted_all)
                probs = jnp.where(keep, probs, 0.0)
            dv_sorted[here, :] += dot_nn(probs.astype(bf16), do_tile)
            d_probs = dot_nt(v_sorted[here, :], do_tile)
            d_scores = (probs * (d_probs - delta[...])).astype(bf16)
            dk_sorted[here, :] += dot_nn(d_scores, q_tile)
            dq_turned[...] += dot_nn(k_turned[:, here], d_scores)

        tile_loop(query_tile, key_tiles, sorted_all, work)
        dq_sorted[pl.ds(q_start, tile), :] = dq_turned[...].T

    query_loop(query_tiles, sorted_all, query_work)
    q_part[...] = jnp.zeros_like(q_part)
    k_part[...] = jnp.zeros_like(k_part)

    def through_norm(field, grad, gain, at_pos, gain_part):
        scaled = grad * scale
        normed_grad = scaled * cos_ref[at_pos, :] - turn(scaled) * sin_ref[at_pos, :]
        factor = inv_root(field)
        gain_part[...] += jnp.sum(normed_grad * field * factor, axis=0, keepdims=True)
        return norm_back(field, factor, gain[...], normed_grad).astype(bf16)

    def put_queries(part, here, place, at_pos):
        grads[part][here, :head] = through_norm(
            raw[part][here, :head], dq_sorted[place, :], q_gain, at_pos, q_part
        )

    def put_keys(part, here, place):
        grads[part][here, head : 2 * head] = through_norm(
            raw[part][here, head : 2 * head], dk_sorted[place, :], k_gain, place, k_part
        )
        grads[part][here, 2 * head :] = dv_sorted[place, :].astype(bf16)

    each_query(*walk, put_queries)
    each_key(key_pos, keys // rows, rows, put_keys)


def attend_back(tables, raw, cosine, sine, query_gain, key_gain, saved, out, d_out, lse, rows, sorted_all, scale):
    head = query_gain.shape[1]
    keys = cosine.shape[0]
    queries = tables[1].shape[0] * rows
    tile = math.gcd(math.gcd(queries, keys), 512)
    narrow, row, part = whole_spec((keys, head)), whole_spec((1, head)), whole_spec((keys // 2, head))
    q_spec, wide = whole_spec((queries, head)), whole_spec((keys // 2, 3 * head))
    return pl.pallas_call(
        functools.partial(attend_back_kernel, (rows, tile, sorted_all, scale)),
        out_shape=(
            jax.ShapeDtypeStruct((keys // 2, 3 * head), bf16),
            jax.ShapeDtypeStruct((keys // 2, 3 * head), bf16),
            jax.ShapeDtypeStruct((1, head), f32),
            jax.ShapeDtypeStruct((1, head), f32),
        ),
        grid_spec=pltpu.PrefetchScalarGridSpec(
            num_scalar_prefetch=3,
            grid=(1,),
            in_specs=[
                whole_spec(raw[0].shape), whole_spec(raw[1].shape), narrow, narrow, row, row,
                q_spec, narrow, narrow, part, part, part, part, whole_spec((1, queries)),
            ],
            out_specs=(wide, wide, row, row),
            scratch_shapes=[
                pltpu.VMEM((queries, head), bf16),
                pltpu.VMEM((queries, head), bf16),
                pltpu.VMEM((head, keys), bf16),
                pltpu.VMEM((1, tile), f32),
                pltpu.VMEM((head, tile), f32),
                pltpu.VMEM((queries, head), f32),
                pltpu.VMEM((keys, head), f32),
                pltpu.VMEM((keys, head), f32),
            ],
        ),
        compiler_params=pltpu.CompilerParams(
            vmem_limit_bytes=min(60 << 20, (16 << 20) + 7168 * keys)
        ),
        cost_estimate=pl.CostEstimate(
            flops=10 * queries * keys * head, bytes_accessed=40 * keys * head, transcendentals=queries * keys
        ),
        name="attend_back",
    )(*tables, *raw, cosine, sine, query_gain, key_gain, *saved, *out, *d_out, lse)


def project_kernel(weight_ref, gain_ref, *refs):
    count = len(refs) - 2
    normed_ref, out_ref = refs[count:]
    rows = refs[0].shape[0]
    for index in range(count):
        wide = refs[index][...].astype(f32)
        normed = (wide * inv_root(wide) * gain_ref[...]).astype(bf16)
        place = pl.ds(index * rows, rows)
        normed_ref[place, :] = normed
        out_ref[place, :] = dot_nn(normed, weight_ref[...])


def project(blocks, gain, weight):
    rows, width = blocks[0].shape
    total, columns = rows * len(blocks), weight.shape[1]
    return pl.pallas_call(
        project_kernel,
        out_shape=(
            jax.ShapeDtypeStruct((total, width), bf16),
            jax.ShapeDtypeStruct((total, columns), f32),
        ),
        grid=(1,),
        in_specs=[whole_spec(weight.shape), whole_spec((1, width))]
        + [whole_spec((rows, width))] * len(blocks),
        out_specs=(whole_spec((total, width)), whole_spec((total, columns))),
        compiler_params=pltpu.CompilerParams(
            vmem_limit_bytes=(12 << 20) + 12 * total * width
        ),
        cost_estimate=pl.CostEstimate(
            flops=2 * total * width * columns, bytes_accessed=4 * total * width, transcendentals=total
        ),
        name="project",
    )(weight, gain[None, :], *blocks)


class Ring:
    def __init__(self, size):
        self.chips = size // 2
        self.reach = self.chips // 2
        self.order = list(range(0, self.chips, 2)) + list(range(self.chips - 1, 0, -2))
        self.swap_pairs = [(i, i ^ 1) for i in range(size)]
        self.out_pairs = []
        for place, chip in enumerate(self.order):
            after_it = self.order[(place + 1) % self.chips]
            self.out_pairs.append((2 * chip, 2 * after_it))
            self.out_pairs.append((2 * after_it + 1, 2 * chip + 1))
        self.home_pairs = [(target, source) for source, target in self.out_pairs]

    def swap(self, field):
        return lax.ppermute(field, "ctx", self.swap_pairs)

    def out(self, field):
        return lax.ppermute(field, "ctx", self.out_pairs)

    def home(self, field):
        return lax.ppermute(field, "ctx", self.home_pairs)

    def members(self, rank):
        chip, core = rank // 2, rank % 2
        place = self.order.index(chip)
        blocks = [rank]
        for step in range(1, self.reach + 1):
            near = self.order[(place + (2 * core - 1) * step) % self.chips]
            blocks.append(2 * near + core)
            if step < self.reach:
                blocks.append(2 * near + 1 - core)
        return blocks

    def gather(self, block, hooks=None):
        hooks = hooks or {}
        streams = [block, self.swap(block)]
        blocks = [block]
        for hop in range(2 * self.reach - 1):
            held = streams[hop % 2]
            if hop >= 3:
                held = after(held, blocks[hop - 2])
            if hop in hooks:
                held = after(held, hooks[hop](blocks))
            streams[hop % 2] = self.out(held)
            blocks.append(streams[hop % 2])
        return blocks

    def scatter_hops(self, term, streams, hops, needs=None, first_twice=False):
        needs = needs or {}
        order = list(range(2 * self.reach - 1, 0, -1))
        if first_twice:
            for place in range(1, len(order), 2):
                order[place : place + 2] = reversed(order[place : place + 2])
        streams, marks, total = list(streams), [], None
        for hop in hops:
            index = order[hop]
            stream, held = 1 - index % 2, streams[1 - index % 2]
            if held is None:
                total = term(index)
            else:
                held = held if total is None else after(held, total)
                total = (term(index).astype(f32) + held.astype(f32)).astype(bf16)
            if hop in needs:
                total = after(total, needs[hop](marks))
            streams[stream] = self.home(total)
            marks.append(streams[stream])
        return streams, marks

    def scatter_end(self, term, streams):
        first, second = streams
        return first.astype(f32) + term(0).astype(f32) + self.swap(second).astype(f32)

    def scatter_sum(self, term, needs=None, first_twice=False):
        streams, marks = self.scatter_hops(
            term, [None, None], range(2 * self.reach - 1), needs, first_twice
        )
        return self.scatter_end(term, streams), marks


def after(value, *events):
    return lax.optimization_barrier((value, events))[0]


def spread(rows_block):
    return lax.all_to_all(rows_block, "ctx", split_axis=0, concat_axis=0, tiled=False)


def swap_rows(field):
    return lax.ppermute(field, "fsdp", [(0, 1), (1, 0)])


def to_columns(received, partner, fsdp_rank):
    first = jnp.where(fsdp_rank == 0, received, partner)
    second = jnp.where(fsdp_rank == 0, partner, received)
    both = jnp.stack([first, second], axis=1)
    return both.reshape(-1, received.shape[-1])


def halves(grads, extra, fsdp_rank, ctx_size):
    width = grads.shape[1]
    split = grads.reshape(ctx_size, 2, -1, width)
    keep = jnp.where(fsdp_rank == 0, split[:, 0], split[:, 1])
    give = jnp.where(fsdp_rank == 0, split[:, 1], split[:, 0])
    if extra is None:
        return keep, give, None
    count = extra.shape[0]
    lines = -(-count // width)
    lines = -(-lines // 16) * 16
    extra_block = jnp.pad(extra, (0, lines * width - count)).reshape(lines, width).astype(bf16)
    return keep, jnp.concatenate([give.reshape(-1, width), extra_block], axis=0), extra_block


def join(keep, given, extra_block):
    if extra_block is None:
        return (keep.astype(f32) + given.astype(f32)).astype(bf16)
    ctx_size, rows, width = keep.shape
    body = given[: ctx_size * rows].reshape(keep.shape)
    total = (keep.astype(f32) + body.astype(f32)).astype(bf16)
    extras = (extra_block.astype(f32) + given[ctx_size * rows :].astype(f32)).astype(bf16)
    return jnp.concatenate(
        [total, jnp.broadcast_to(extras[None], (ctx_size,) + extras.shape)], axis=1
    )


def apart(received, rows, width, count):
    lines = received[:, rows:, :width].astype(f32)
    return received[:, :rows], jnp.sum(lines, axis=0).reshape(-1)[:count]


def side_by_side(pieces):
    count, rows, width = pieces.shape
    return jnp.transpose(pieces, (1, 0, 2)).reshape(rows, count * width)


def shards(
    block_input,
    query_weight,
    key_weight,
    value_weight,
    output_weight,
    gate_weight,
    up_weight,
    down_weight,
    attn_gain,
    mlp_gain,
    query_gain,
    key_gain,
    block_order,
    cotangent,
):
    ctx_size = lax.axis_size("ctx")
    ctx_rank = lax.axis_index("ctx")
    fsdp_rank = lax.axis_index("fsdp")
    core = ctx_rank % 2
    tokens = block_input.shape[1]
    model = block_input.shape[2]
    head_size = query_gain.shape[0]
    kv_heads = key_weight.shape[1] // head_size
    slots = block_order.shape[0]
    length = tokens * ctx_size
    half_rows = length // slots
    per_block = tokens // half_rows
    weight_rows = query_weight.shape[0]
    hidden_slice = gate_weight.shape[1] // ctx_size
    splits = ctx_size // 2 // kv_heads
    split_rank = (ctx_rank // 2) % splits
    sorted_all = splits == 1
    score_scale = 1.0 / math.sqrt(head_size)
    ring = Ring(ctx_size)
    always = jnp.min(block_order) >= 0

    def fenced(work, *values):
        shapes = jax.eval_shape(work, *values)
        blank = lambda *_: jax.tree.map(lambda leaf: jnp.zeros(leaf.shape, leaf.dtype), shapes)
        return lax.cond(always, work, blank, *values)

    def block_rows(field, index):
        return field[index * tokens : (index + 1) * tokens]

    def by_head(weight):
        split = jnp.transpose(weight.reshape(weight_rows, kv_heads, -1, head_size), (1, 2, 0, 3))
        return jnp.broadcast_to(split[:, None], (kv_heads, splits) + split.shape[1:]).reshape(
            -1, weight_rows, head_size
        )

    key_value = jnp.stack(
        [key_weight.reshape(weight_rows, kv_heads, head_size),
         value_weight.reshape(weight_rows, kv_heads, head_size)],
        axis=2,
    ).reshape(weight_rows, -1)
    head_block = jnp.concatenate(
        [by_head(query_weight), by_head(output_weight), by_head(key_value)], axis=2
    )
    head_received = spread(after(head_block, ring.swap(block_input[0])))
    head_mine = to_columns(head_received, swap_rows(head_received), fsdp_rank)
    head_other = ring.swap(head_mine)

    def column(field, index):
        return field[:, index * head_size : (index + 1) * head_size]

    def key_first(mine, other):
        return jnp.where(core == 0, mine, other), jnp.where(core == 0, other, mine)

    key_columns, value_columns = key_first(column(head_mine, 2), column(head_other, 2))
    head_weight = jnp.concatenate(
        [column(head_mine, 0), key_columns, value_columns, column(head_other, 0)], axis=1
    )
    output_part = jnp.concatenate([column(head_mine, 1), column(head_other, 1)], axis=1)

    last_hop = 2 * ring.reach - 2
    angles = {}

    def make_angles(blocks):
        angles["tables"] = rope_tables(
            after(jnp.arange(length, dtype=jnp.int32), blocks[2]), head_size
        )
        return angles["tables"]

    input_blocks = ring.gather(block_input[0], {last_hop - 1: make_angles})
    member_table = np.array(
        [ring.members(rank) + ring.members(rank ^ 1) for rank in range(ctx_size)], np.int32
    )
    ranks = jnp.arange(ctx_size, dtype=jnp.int32)
    listed = jnp.sum(jnp.where(ranks[:, None] == ctx_rank, member_table, 0), axis=0)
    slot_index = jnp.arange(slots, dtype=jnp.int32)
    local_slot = (
        listed[:, None] * per_block + jnp.arange(per_block, dtype=jnp.int32)[None, :]
    ).reshape(-1)
    local_pos = jnp.sum(
        jnp.where(local_slot[:, None] == slot_index[None, :], block_order[None, :], 0), axis=1
    )
    cosine, sine = angles["tables"]
    if sorted_all:
        tables = (local_pos, slot_index, slot_index)
    else:
        local_of_pos = jnp.sum(
            jnp.where(local_pos[None, :] == slot_index[:, None], slot_index[None, :], 0), axis=1
        )
        compact = jnp.arange(slots // splits, dtype=jnp.int32)
        owner = (compact // per_block) * splits + split_rank
        own_pos = jnp.sort(jnp.take(block_order, owner * per_block + compact % per_block))
        tables = (local_pos, jnp.take(local_of_pos, own_pos), own_pos)
    query_row, key_row = query_gain[None, :], key_gain[None, :]

    input_blocks[4] = after(input_blocks[4], head_received)

    def by_slice(weight):
        return jnp.transpose(weight.reshape(weight_rows, ctx_size, hidden_slice), (1, 0, 2))

    gate, up, down = after((gate_weight, up_weight, down_weight), input_blocks[3])
    mlp_block = jnp.concatenate([by_slice(gate), by_slice(up), by_slice(down)], axis=2)
    normed_attn, projected = project(input_blocks, attn_gain, head_weight)
    projected_given = ring.swap(
        jnp.concatenate(
            [projected[:, 3 * head_size :], projected[:, head_size : 3 * head_size]], axis=1
        )
    )
    raw = (projected, projected_given)
    attn_a, attn_b, lse, *saved = attend(
        tables, raw, cosine, sine, query_row, key_row, half_rows, sorted_all, score_scale
    )
    mlp_received = spread(after(mlp_block, input_blocks[-1], input_blocks[-2]))
    mlp_received = after(mlp_received, attn_a)
    mlp_partner = swap_rows(mlp_received)
    attn_pair = jnp.concatenate([attn_a, ring.swap(attn_b)], axis=1)

    inputs32 = block_input[0].astype(f32)
    attn_terms = dot_nt(attn_pair, output_part).astype(bf16)
    attn_out = fenced(
        lambda terms: ring.scatter_sum(lambda i: block_rows(terms, i))[0], attn_terms
    )
    hidden_one = inputs32 + attn_out
    scale_mlp = inv_root(hidden_one)
    normed_mlp = (hidden_one * scale_mlp * mlp_gain).astype(bf16)
    mlp_mine = to_columns(mlp_received, mlp_partner, fsdp_rank)
    mlp_other = ring.swap(mlp_mine)
    pair = 2 * hidden_slice
    gate_up = jnp.concatenate([mlp_mine[:, :pair], mlp_other[:, :pair]], axis=1)
    down_part = jnp.concatenate([mlp_mine[:, pair:], mlp_other[:, pair:]], axis=1)

    normed_blocks = ring.gather(normed_mlp)
    normed_all = jnp.concatenate(normed_blocks, axis=0)
    gate_up, down_part = lax.optimization_barrier((gate_up, down_part))
    middle = ring.reach * tokens
    hidden_parts = [dot_nn(normed_all[:middle], gate_up), dot_nn(normed_all[middle:], gate_up)]
    cot_blocks = ring.gather(
        after(cotangent[0], normed_blocks[-2]),
        {
            last_hop - 4: lambda _: gate_up,
            last_hop - 3: lambda _: hidden_parts[0],
            last_hop - 1: lambda _: hidden_parts[1],
        },
    )
    hidden_all = jnp.concatenate(hidden_parts, axis=0)
    cot_all = jnp.concatenate(cot_blocks, axis=0)
    act_grad_all = dot_nn(cot_all, down_part)
    activated_list, back_list = [], []
    for member in range(2):
        gate_pre = hidden_all[:, 2 * member * hidden_slice : (2 * member + 1) * hidden_slice]
        up_pre = hidden_all[:, (2 * member + 1) * hidden_slice : (2 * member + 2) * hidden_slice]
        act_grad = act_grad_all[:, member * hidden_slice : (member + 1) * hidden_slice]
        sigma = jax.nn.sigmoid(gate_pre)
        activated_list.append((gate_pre * sigma * up_pre).astype(bf16))
        back_list.append(
            (act_grad * up_pre * sigma * (1.0 + gate_pre * (1.0 - sigma))).astype(bf16)
        )
        back_list.append((act_grad * gate_pre * sigma).astype(bf16))
    activated_all = jnp.concatenate(activated_list, axis=1)
    back_all = jnp.concatenate(back_list, axis=1)
    far = (2 * ring.reach - 3) * tokens
    far_terms = dot_nt(back_all[far:], gate_up).astype(bf16)
    near_blocks = far // tokens
    add = lambda left, right: (left.astype(f32) + right.astype(f32)).astype(bf16)

    def feed_forward_grads(far_terms, back_all, activated_all, normed_all, cot_all, gate_up):
        near_terms = dot_nt(back_all[:far], gate_up).astype(bf16)
        ready = {}

        def piece(left, right, mark):
            grad = dot_tn(left, after(right, mark)).astype(bf16)
            return with_layout_constraint(grad, Layout((0, 1)))

        def down_away(marks):
            ready["down_give"] = piece(cot_all, activated_all[:, hidden_slice:], marks[0])
            return ready["down_give"]

        def gate_up_away(marks):
            ready["gate_up_give"] = piece(normed_all, back_all[:, pair:], marks[1])
            return ready["gate_up_give"]

        def down_here(marks):
            ready["down"] = piece(cot_all, activated_all[:, :hidden_slice], marks[2])
            return ready["down"]

        def gate_up_here(marks):
            ready["gate_up"] = piece(normed_all, back_all[:, :pair], marks[3])
            return ready["gate_up"]

        summed, marks = ring.scatter_sum(
            lambda i: block_rows(near_terms, i)
            if i < near_blocks
            else block_rows(far_terms, i - near_blocks),
            {2: down_away, 3: gate_up_away, 4: down_here, 5: gate_up_here},
            first_twice=True,
        )
        ready["down"] = add(ready["down"], ring.swap(ready["down_give"]))
        ready["gate_up"] = add(ready["gate_up"], ring.swap(ready["gate_up_give"]))
        near_late, far_late = after((near_terms, far_terms), marks[4])
        gain_part = jnp.sum(
            near_late.astype(f32) * normed_all[:far].astype(f32), axis=0
        ) + jnp.sum(far_late.astype(f32) * normed_all[far:].astype(f32), axis=0)
        down_own, down_away, _ = halves(ready["down"], None, fsdp_rank, ctx_size)
        gate_up_own, gate_up_away, _ = halves(ready["gate_up"], None, fsdp_rank, ctx_size)
        return summed, gain_part / mlp_gain, down_own, down_away, gate_up_own, gate_up_away

    normed_mlp_grad, mlp_gain_part, down_own, down_away, gate_up_own, gate_up_away = fenced(
        feed_forward_grads, far_terms, back_all, activated_all, normed_all, cot_all, gate_up
    )
    grad32 = cotangent[0].astype(f32)
    hidden_grad = grad32 + norm_back(hidden_one, scale_mlp, mlp_gain, normed_mlp_grad)
    hidden_grad_bf = hidden_grad.astype(bf16)
    down_own, gate_up_own = lax.optimization_barrier((down_own, gate_up_own))
    down_other, gate_up_other = swap_rows(down_away), swap_rows(gate_up_away)


    def gather_grads(block, activated_all, down_part):
        ready = {}

        def output_terms(blocks):
            ready["out"] = dot_nt(after(activated_all, blocks[2]), down_part).astype(bf16)
            return ready["out"]

        blocks = ring.gather(block, {last_hop - 1: output_terms})
        return jnp.concatenate(blocks, axis=0), ready["out"]

    grad_all, out_terms = fenced(gather_grads, hidden_grad_bf, activated_all, down_part)
    attn_grad_pair = dot_nn(grad_all, output_part).astype(bf16)
    attn_grad = (attn_grad_pair[:, :head_size], ring.swap(attn_grad_pair[:, head_size:]))
    mlp_sent = jnp.concatenate(
        [join(down_own, down_other, None), join(gate_up_own, gate_up_other, None)], axis=2
    )
    attn_grad, mlp_sent = lax.optimization_barrier((attn_grad, mlp_sent))

    mlp_rows = spread(mlp_sent)

    def attention_back(attn_grad, attn_a, attn_b, projected, given):
        first_a, first_b, query_gain_part, key_gain_part = attend_back(
            tables, (projected, given), cosine, sine, query_row, key_row, saved, (attn_a, attn_b),
            attn_grad, lse, half_rows, sorted_all, score_scale,
        )
        given_grads = ring.swap(first_b)
        half_grads = jnp.concatenate(
            [
                first_a[:, :head_size],
                add(first_a[:, head_size:], given_grads[:, head_size:]),
                given_grads[:, :head_size],
            ],
            axis=1,
        )
        input_terms = dot_nt(half_grads, head_weight).astype(bf16)
        return half_grads, input_terms, query_gain_part[0], key_gain_part[0]

    half_grads, input_terms, query_gain_part, key_gain_part = fenced(
        attention_back, attn_grad, attn_a, attn_b, *raw
    )

    def attention_grads(input_terms, half_grads, grad_all, normed_attn, attn_pair, other_gains):
        ready = {}

        def weight_grads(marks):
            late_grads, late_attn = after((half_grads, attn_pair), marks[0])
            head_grad = dot_tn(normed_attn, late_grads).astype(bf16)
            output_grad = dot_tn(grad_all, late_attn).astype(bf16)
            kv_keep, kv_give = key_first(column(head_grad, 1), column(head_grad, 2))
            keep = jnp.concatenate([column(head_grad, 0), column(output_grad, 0), kv_keep], axis=1)
            give = jnp.concatenate([column(head_grad, 3), column(output_grad, 1), kv_give], axis=1)
            ready["gain"] = (
                jnp.sum(after(input_terms, marks[1]).astype(f32) * normed_attn.astype(f32), axis=0)
                / attn_gain
            )
            ready["parts"] = halves(
                add(keep, ring.swap(give)),
                jnp.concatenate([ready["gain"], other_gains]),
                fsdp_rank,
                ctx_size,
            )
            return ready["gain"]

        summed, _ = ring.scatter_sum(
            lambda i: block_rows(input_terms, i), {last_hop: weight_grads}
        )
        return summed, ready["parts"]

    normed_attn_grad, attn_parts = fenced(
        attention_grads, input_terms, half_grads, grad_all, normed_attn, attn_pair,
        jnp.concatenate([query_gain_part, key_gain_part, mlp_gain_part]),
    )

    def out_and_home(out_terms, attn_parts, mlp_rows, summed_grad, hidden_grad, inputs32):
        own, away, lines = attn_parts
        ready = {}

        def other_rows(_):
            ready["other"] = swap_rows(away)
            return ready["other"]

        def rows_home(_):
            sent = join(own, ready["other"], lines)
            ready["rows"] = spread(sent)
            return sent

        def unpack(marks):
            rows = after(mlp_rows, marks[4])
            ready["mlp"] = tuple(
                side_by_side(rows[:, :, i * hidden_slice : (i + 1) * hidden_slice]).astype(f32)
                for i in range(3)
            )
            return ready["mlp"]

        def finish(marks):
            ready["input"] = hidden_grad + norm_back(
                inputs32, inv_root(inputs32), attn_gain, after(summed_grad, marks[3])
            )
            return ready["input"]

        summed, marks = ring.scatter_sum(
            lambda i: block_rows(out_terms, i),
            {4: other_rows, 5: rows_home},
        )
        finish(marks)
        unpack(marks)
        return summed, ready["rows"], ready["input"], ready["mlp"]

    attn_parts, mlp_rows = lax.optimization_barrier((attn_parts, mlp_rows))
    mlp_out, attn_home, input_grad, mlp_grads = fenced(
        out_and_home, out_terms, attn_parts, mlp_rows, normed_attn_grad,
        hidden_grad, inputs32,
    )
    block_out = (hidden_one + mlp_out).astype(bf16)
    attn_rows, attn_extra = apart(
        attn_home,
        weight_rows,
        3 * head_size,
        2 * model + 2 * head_size,
    )

    def home(index):
        part = attn_rows[:, :, index * head_size : (index + 1) * head_size].astype(f32)
        return jnp.sum(part.reshape(kv_heads, splits, 2, weight_rows, head_size), axis=1)

    key_value_rows = home(2)
    flat = lambda part: side_by_side(part.reshape(-1, weight_rows, head_size))

    down_rows, gate_rows, up_rows = mlp_grads

    return (
        block_out[None],
        input_grad[None],
        flat(home(0)),
        flat(key_value_rows[:, 0]),
        flat(key_value_rows[:, 1]),
        flat(home(1)),
        gate_rows,
        up_rows,
        down_rows,
        attn_extra[:model],
        attn_extra[model + 2 * head_size :],
        attn_extra[model : model + head_size],
        attn_extra[model + head_size : model + 2 * head_size],
    )


def solution(mesh):
    in_specs = (
        P("fsdp", "ctx", None),
        P(("ctx", "fsdp"), None),
        P(("ctx", "fsdp"), None),
        P(("ctx", "fsdp"), None),
        P(("ctx", "fsdp"), None),
        P(("ctx", "fsdp"), None),
        P(("ctx", "fsdp"), None),
        P(("ctx", "fsdp"), None),
        P(),
        P(),
        P(),
        P(),
        P(),
        P("fsdp", "ctx", None),
    )
    out_specs = (
        P("fsdp", "ctx", None),
        P("fsdp", "ctx", None),
        P(("ctx", "fsdp"), None),
        P(("ctx", "fsdp"), None),
        P(("ctx", "fsdp"), None),
        P(("ctx", "fsdp"), None),
        P(("ctx", "fsdp"), None),
        P(("ctx", "fsdp"), None),
        P(("ctx", "fsdp"), None),
        P(),
        P(),
        P(),
        P(),
    )
    return jax.shard_map(shards, mesh=mesh, in_specs=in_specs, out_specs=out_specs, check_vma=False)
```
